512 devices in a mesh: sec: 2 (over x_hi), gx: 32 (over z, x_lo), gy: 8 (over y, core).
Axes of the slice: x: 4 (x_hi: 2, x_lo: 2; x = x_hi * 2 + x_lo), y: 4, z: 16, core: 2. Of those that a mesh axis runs over, the one named last changes fastest.
Arguments:
- velocity: float32 [2, 3, 32, 256, 1024], P('sec', None, None, 'gx', 'gy'), may hold values from -6 to 6
- turbine_cells: int32 [64, 3], replicated, may hold values from 0 to 1023, as said below
- fringe_bounds: int32 [2], replicated, may hold values from 192 to 256, as said below
Outputs:
- velocity_next: float32 [2, 3, 32, 256, 1024], P('sec', None, 'gx', None, 'gy')
- pressure: float32 [2, 32, 256, 1024], P('sec', 'gx', None, 'gy')
The draws below stay inside these ranges and needn't reach their ends.
Inputs may be any that keep to these rules, and one draw needn't show every extreme that they name: `turbine_cells`: each turbine's streamwise index is below 128 and its vertical index lies from 4 to 27. fringe_bounds[0] < fringe_bounds[1] = 256; the fringe lies in the last quarter of the streamwise columns.
All inputs are finite; a program needn't handle non-finite values.
Results may differ from the reference program's by a relative error of at most 0.00018.
Values sent between devices are 32-bit elements; how exact they have to be, the bound alone decides.
A program may use at most 64 MiB of HBM per device.

```python
import jax
import jax.numpy as jnp
from jax import lax

NZ = 32
TURB = 64
RADIUS = 4
NX = 256
NY = 1024


def draw_turbine_cells(key, part):
    subkeys = jax.random.split(jax.random.fold_in(key, 11), 3)
    streamwise = jax.random.randint(subkeys[0], (TURB,), 0, NX // 2)
    across = jax.random.randint(subkeys[1], (TURB,), 0, NY)
    height = jax.random.randint(subkeys[2], (TURB,), RADIUS, NZ - RADIUS)
    return jnp.stack([streamwise, across, height], axis=1).astype(jnp.int32)


def draw_fringe_bounds(key, part):
    subkeys = jax.random.split(jax.random.fold_in(key, 23), 1)
    first_column = jax.random.randint(subkeys[0], (), NX * 3 // 4, NX * 7 // 8 + 1)
    last_column = jnp.zeros((), jnp.int32) + NX
    return jnp.stack([first_column, last_column]).astype(jnp.int32)


def block_scale(stream_key, shape, pieces, low, largest):
    factor_of = 1.0
    for dim, shards_of in pieces:
        heights = jax.random.uniform(jax.random.fold_in(jax.random.fold_in(stream_key, 6), dim), (shards_of,), jnp.float32, low / len(pieces), largest / len(pieces))
        factor_of = factor_of * jnp.repeat(jnp.exp(heights), shape[dim] // shards_of).reshape((-1,) + (1,) * (len(shape) - 1 - dim))
    return factor_of


def scatter_about(rng, extent, deviation, reach, shards=(), held_as=jnp.bfloat16):
    gain = block_scale(rng, extent, shards, -0.22, 0.18) if shards else 1.0
    entries = jax.random.normal(rng, extent, jnp.float32) * deviation * gain
    return jnp.minimum(jnp.maximum(entries, -reach), reach).astype(held_as)


def setup_inputs(seed: int = 0) -> dict:
    splits = jax.random.split(jax.random.key(seed), 4)
    velocity = scatter_about(splits[0], (2, 3, NZ, NX, NY), 1.0, 6.0, ((0, 2), (3, 32), (4, 8)), jnp.float32)
    turbine_cells = draw_turbine_cells(jax.random.fold_in(splits[3], 71), 0)
    fringe_bounds = draw_fringe_bounds(jax.random.fold_in(splits[3], 71), 0)
    return {"velocity": velocity, "turbine_cells": turbine_cells, "fringe_bounds": fringe_bounds}


TIME_STEP = 0.05
SMAG_COEFF = 0.1
THRUST_COEFF = 4.0
DRIVING_FORCE = 0.1
FRINGE_BLEND = 0.5
HIGHEST = lax.Precision.HIGHEST

def cas_table(row_index, column_index, length):
    product = row_index[:, None] * column_index[None, :] % length
    angle = product.astype(jnp.float32) * (2.0 * jnp.pi / length)
    return jnp.cos(angle) + jnp.sin(angle)

def shift_up(values):
    zeros = jnp.zeros_like(values[..., :1, :, :])
    return jnp.concatenate([values[..., 1:, :, :], zeros], axis=-3)

def shift_down(values):
    zeros = jnp.zeros_like(values[..., :1, :, :])
    return jnp.concatenate([zeros, values[..., :-1, :, :]], axis=-3)

def thomas(right_side, eigen_value):
    length = right_side.shape[0]
    inverses = []
    reduced = []
    for level_index in range(length):
        if level_index == 0:
            diagonal = eigen_value - 1.0
        elif level_index == length - 1:
            diagonal = eigen_value - 3.0
        else:
            diagonal = eigen_value - 2.0
        if level_index == 0:
            pivot_now = diagonal
            current = right_side[0] / pivot_now
        else:
            pivot_now = diagonal - inverses[-1]
            current = (right_side[level_index] - reduced[-1]) / pivot_now
        inverses.append(1.0 / pivot_now)
        reduced.append(current)
    solution = [reduced[-1]]
    for level_index in range(length - 2, -1, -1):
        solution.append(reduced[level_index] - inverses[level_index] * solution[-1])
    return jnp.stack(solution[::-1])

def disk_weights(turbine_cells):
    along_x = jnp.arange(NX, dtype=jnp.int32)
    along_y = jnp.arange(NY, dtype=jnp.int32)
    along_z = jnp.arange(NZ, dtype=jnp.int32)
    matches = (along_x[:, None] == turbine_cells[None, :, 0]).astype(jnp.float32)
    offset_y = (along_y[None, :] - turbine_cells[:, 1:2] + NY // 2) % NY - NY // 2
    offset_z = along_z[None, :] - turbine_cells[:, 2:3]
    distance = offset_z[:, :, None] * offset_z[:, :, None] + offset_y[:, None, :] * offset_y[:, None, :]
    inside = (distance <= RADIUS * RADIUS).astype(jnp.float32)
    return jnp.einsum('xt,tzy->zxy', matches, inside, precision=HIGHEST)

def tendency(velocity_now, farm_flag, disk_weight):
    plus_x = jnp.roll(velocity_now, -1, axis=-2)
    minus_x = jnp.roll(velocity_now, 1, axis=-2)
    plus_y = jnp.roll(velocity_now, -1, axis=-1)
    minus_y = jnp.roll(velocity_now, 1, axis=-1)
    plus_z = shift_up(velocity_now)
    minus_z = shift_down(velocity_now)
    gradients = [0.5 * (plus_x - minus_x), 0.5 * (plus_y - minus_y), 0.5 * (plus_z - minus_z)]
    strain_squares = jnp.zeros_like(velocity_now[0])
    for component in range(3):
        strain_squares = strain_squares + gradients[component][component] * gradients[component][component]
        for direction in range(component + 1, 3):
            shear = 0.5 * (gradients[direction][component] + gradients[component][direction])
            strain_squares = strain_squares + 2.0 * shear * shear
    viscosity = SMAG_COEFF * jnp.sqrt(2.0 * strain_squares)
    visc_plus_x = jnp.roll(viscosity, -1, axis=-2)
    visc_minus_x = jnp.roll(viscosity, 1, axis=-2)
    visc_plus_y = jnp.roll(viscosity, -1, axis=-1)
    visc_minus_y = jnp.roll(viscosity, 1, axis=-1)
    visc_plus_z = shift_up(viscosity)
    visc_minus_z = shift_down(viscosity)
    advection = 0.5 * (plus_x[0] * plus_x - minus_x[0] * minus_x)
    advection = advection + 0.5 * (plus_y[1] * plus_y - minus_y[1] * minus_y)
    advection = advection + 0.5 * (plus_z[2] * plus_z - minus_z[2] * minus_z)
    diffusion = 0.5 * (viscosity + visc_plus_x) * (plus_x - velocity_now) - 0.5 * (viscosity + visc_minus_x) * (velocity_now - minus_x)
    diffusion = diffusion + 0.5 * (viscosity + visc_plus_y) * (plus_y - velocity_now) - 0.5 * (viscosity + visc_minus_y) * (velocity_now - minus_y)
    diffusion = diffusion + 0.5 * (viscosity + visc_plus_z) * (plus_z - velocity_now) - 0.5 * (viscosity + visc_minus_z) * (velocity_now - minus_z)
    changes = diffusion - advection
    streamwise = DRIVING_FORCE - THRUST_COEFF * farm_flag * disk_weight * velocity_now[0] * jnp.abs(velocity_now[0])
    return jnp.concatenate([changes[:1] + streamwise[None], changes[1:]], axis=0)

def project(velocity_now):
    divergence = 0.5 * (jnp.roll(velocity_now[0], -1, axis=-2) - jnp.roll(velocity_now[0], 1, axis=-2))
    divergence = divergence + 0.5 * (jnp.roll(velocity_now[1], -1, axis=-1) - jnp.roll(velocity_now[1], 1, axis=-1))
    divergence = divergence + 0.5 * (shift_up(velocity_now[2]) - shift_down(velocity_now[2]))
    index_x = jnp.arange(NX, dtype=jnp.int32)
    index_y = jnp.arange(NY, dtype=jnp.int32)
    table_x = cas_table(index_x, index_x, NX)
    table_y = cas_table(index_y, index_y, NY)
    spectrum = jnp.einsum('kx,zxy->zky', table_x, divergence, precision=HIGHEST)
    spectrum = jnp.einsum('ly,zky->zkl', table_y, spectrum, precision=HIGHEST)
    eigen_value = 2.0 * jnp.cos(index_x.astype(jnp.float32) * (2.0 * jnp.pi / NX))[:, None]
    eigen_value = eigen_value + 2.0 * jnp.cos(index_y.astype(jnp.float32) * (2.0 * jnp.pi / NY))[None, :] - 4.0
    solved = thomas(spectrum, eigen_value)
    pressure = jnp.einsum('xk,zkl->zxl', table_x, solved, precision=HIGHEST) * (1.0 / NX)
    pressure = jnp.einsum('yl,zxl->zxy', table_y, pressure, precision=HIGHEST) * (1.0 / NY)
    gradient_x = 0.5 * (jnp.roll(pressure, -1, axis=1) - jnp.roll(pressure, 1, axis=1))
    gradient_y = 0.5 * (jnp.roll(pressure, -1, axis=2) - jnp.roll(pressure, 1, axis=2))
    above_level = jnp.concatenate([pressure[1:], -pressure[-1:]], axis=0)
    below_level = jnp.concatenate([pressure[:1], pressure[:-1]], axis=0)
    gradient_z = 0.5 * (above_level - below_level)
    return (velocity_now - jnp.stack([gradient_x, gradient_y, gradient_z]), pressure)

def reference(velocity, turbine_cells, fringe_bounds):
    disk_weight = disk_weights(turbine_cells)
    advanced = []
    for section in range(2):
        farm_flag = float(section)
        initial = velocity[section]
        segment_one = initial + TIME_STEP * tendency(initial, farm_flag, disk_weight)
        segment_two = 0.75 * initial + 0.25 * (segment_one + TIME_STEP * tendency(segment_one, farm_flag, disk_weight))
        segment_three = initial / 3.0 + 2.0 / 3.0 * (segment_two + TIME_STEP * tendency(segment_two, farm_flag, disk_weight))
        advanced.append(segment_three)
    along_x = jnp.arange(NX, dtype=jnp.int32)
    inside = ((along_x >= fringe_bounds[0]) & (along_x < fringe_bounds[1])).astype(jnp.float32)
    farm_blended = advanced[1] + FRINGE_BLEND * inside[:, None] * (advanced[0] - advanced[1])
    precursor_next, precursor_pressure = project(advanced[0])
    farm_next, farm_pressure = project(farm_blended)
    return (jnp.stack([precursor_next, farm_next]), jnp.stack([precursor_pressure, farm_pressure]))
```

```python
import functools

import jax
import jax.numpy as jnp
from jax import lax
from jax.experimental import pallas as pl
from jax.experimental.pallas import tpu as pltpu
from jax.sharding import PartitionSpec as P_

TIME_STEP = 0.05
SMAG_COEFF = 0.1
THRUST_COEFF = 4.0
DRIVING_FORCE = 0.1
FRINGE_BLEND = 0.5
RADIUS = 4
MESH = pl.DeviceIdType.MESH
F32 = jnp.float32
HIGHEST = lax.Precision.HIGHEST


def turned(v, shift):
    return pltpu.roll(v, shift % 128, 1)


def viscosity(xp, xm, yp, ym, zp, zm):
    a = xp[0] - xm[0]
    b = yp[1] - ym[1]
    c = zp[2] - zm[2]
    s1 = (yp[0] - ym[0]) + (xp[1] - xm[1])
    s2 = (zp[0] - zm[0]) + (xp[2] - xm[2])
    s3 = (zp[1] - zm[1]) + (yp[2] - ym[2])
    total = 0.5 * (a * a + b * b + c * c) + 0.25 * (s1 * s1 + s2 * s2 + s3 * s3)
    return SMAG_COEFF * jnp.sqrt(total)


def lanes(rows):
    return lax.broadcasted_iota(jnp.int32, (rows, 128), 1)


def fill_pads(U, N, T3):
    zeros = jnp.zeros((8, 128), F32)

    @pl.loop(0, U.shape[0] * 3)
    def _(i):
        s, c = i // 3, i % 3
        for slot in range(12):
            U[s, c, slot, 0:8, :] = zeros
            U[s, c, slot, 40:48, :] = zeros

    for i in range(10):
        N[i, 0:8, :] = zeros
        N[i, 40:48, :] = zeros
    for c in range(3):
        T3[c, 0:8, :] = zeros
        T3[c, 40:48, :] = zeros


def load_initial(vel, U):
    @pl.loop(0, 24)
    def _(i):
        c, x = i // 8, i % 8
        for zc in range(4):
            U[0, c, x + 2, 8 + 8 * zc : 16 + 8 * zc, :] = vel[pl.ds(c * 256 + zc * 64 + x, 8, stride=8), :]


def find_disks(tur, DW, total_y):
    x_anchor = lax.axis_index("gx") * 8
    y_anchor = lax.axis_index("gy") * 128
    turb = tur.shape[0]
    lane = lanes(turb)
    match = (tur[:, 0:1] == x_anchor + lane).astype(F32)
    offset = lane + (y_anchor + total_y // 2 + total_y) - tur[:, 1:2]
    offset = jnp.where(offset >= total_y, offset - total_y, offset)
    offset = jnp.where(offset >= total_y, offset - total_y, offset) - total_y // 2
    square_y = offset * offset
    height = tur[:, 2:3] + jnp.zeros((turb, 128), jnp.int32)

    @pl.loop(0, 32)
    def _(z):
        off_z = z - height
        inside = (off_z * off_z + square_y <= RADIUS * RADIUS).astype(F32)
        count = lax.dot_general(match, inside, (((0,), (0,)), ((), ())), preferred_element_type=F32)
        DW[pl.ds(z, 8, stride=32), :] = count[0:8, :]


def remote(src, dst, send, recv, axis, index):
    return pltpu.make_async_remote_copy(
        src_ref=src, dst_ref=dst, send_sem=send, recv_sem=recv, device_id={axis: index}, device_id_type=MESH
    )


def pack_edges(U, s, comps):
    lane = lanes(32)
    packed = jnp.zeros((32, 128), F32)
    for c in comps:
        for x in range(8):
            base = c * 32 + x * 4
            packed = jnp.where(lane // 4 == base // 4, turned(U[s, c, x + 2, 8:40, :], base + 2), packed)
    return packed


def side_values(u, hh, lane):
    return (jnp.where(lane == 127, hh, turned(u, -1)), jnp.where(lane == 0, hh, turned(u, 1)))


def rk_stage(s, alpha, beta, near, U, N, P, Q, T3, NS, DW, send, recv):
    left, right, down, up = near
    lane32 = lanes(32)
    lane = lanes(8)
    to_down = remote(U.at[s, :, 2:4, 8:40, :], U.at[s, :, 10:12, 8:40, :], send.at[s, 0], recv.at[s, 0], "gx", down)
    to_up = remote(U.at[s, :, 8:10, 8:40, :], U.at[s, :, 0:2, 8:40, :], send.at[s, 1], recv.at[s, 1], "gx", up)
    to_left = remote(P.at[s, 0], P.at[s, 2], send.at[s, 2], recv.at[s, 2], "gy", left)
    to_right = remote(P.at[s, 0], P.at[s, 1], send.at[s, 3], recv.at[s, 3], "gy", right)
    q_down = remote(Q.at[s, 1], Q.at[s, 2], send.at[s, 4], recv.at[s, 4], "gx", down)
    q_up = remote(Q.at[s, 1], Q.at[s, 0], send.at[s, 5], recv.at[s, 5], "gx", up)
    P[s, 0] = pack_edges(U, s, range(3))
    to_left.start()
    to_right.start()
    to_down.start()
    to_up.start()
    to_left.wait_recv()
    to_right.wait_recv()
    own, from_left, from_right = P[s, 0], P[s, 1], P[s, 2]
    Q[s, 1] = jnp.where(lane32 % 4 == 0, turned(from_right, -2), from_left)
    q_down.start()
    q_up.start()
    strip_left = jnp.where(lane32 % 4 < 2, from_left, own)
    strip_right = jnp.where(lane32 % 4 < 2, own, from_right)
    for c in range(3):
        T3[c, 8:40, :] = jnp.where(lane32 < 32, turned(strip_left, -32 * c), turned(strip_right, 32 - 32 * c))
    to_down.wait_recv()
    to_up.wait_recv()
    q_down.wait_recv()
    q_up.wait_recv()
    q_minus, q_plus = Q[s, 0], Q[s, 2]
    parts = [[] for _ in range(6)]
    for c in range(3):
        t = T3[c, 8:40, :]
        xp = jnp.where(lane32 == 29, turned(q_plus, 28 - c * 32), turned(t, -4))
        xp = jnp.where(lane32 == 62, turned(q_plus, 62 - c * 32), xp)
        xm = jnp.where(lane32 == 1, turned(q_minus, -28 - c * 32), turned(t, 4))
        xm = jnp.where(lane32 == 34, turned(q_minus, 6 - c * 32), xm)
        values = (xp, xm, turned(t, -1), turned(t, 1), T3[c, 9:41, :], T3[c, 7:39, :])
        for part, value in zip(parts, values):
            part.append(value)
    strip = viscosity(*parts)
    NS[...] = jnp.where(lane32 % 4 == 0, turned(strip, -34), strip)

    @pl.loop(0, 10)
    def _(i):
        slot = i + 1
        which = jnp.where(i == 0, 0, jnp.where(i == 9, 2, 1))
        column = jnp.where(i == 0, 7, jnp.where(i == 9, 0, i - 1))
        for zc in range(4):
            r = 8 + 8 * zc
            hold = Q[s, which, 8 * zc : 8 * zc + 8, :]
            pieces = [[] for _ in range(6)]
            for c in range(3):
                u = U[s, c, slot, r : r + 8, :]
                hh = pltpu.roll(hold, 127 - c * 32 - column * 4, 1)
                yp, ym = side_values(u, hh, lane)
                values = (
                    U[s, c, slot + 1, r : r + 8, :],
                    U[s, c, slot - 1, r : r + 8, :],
                    yp,
                    ym,
                    U[s, c, slot, r + 1 : r + 9, :],
                    U[s, c, slot, r - 1 : r + 7, :],
                )
                for piece, value in zip(pieces, values):
                    piece.append(value)
            N[i, r : r + 8, :] = viscosity(*pieces)

    farm = lax.axis_index("sec").astype(F32)

    @pl.loop(0, 8)
    def _(x):
        slot = x + 2
        for zc in range(4):
            r = 8 + 8 * zc
            n = N[x + 1, r : r + 8, :]
            hold = Q[s, 1, 8 * zc : 8 * zc + 8, :]
            nyp, nym = side_values(n, pltpu.roll(NS[8 * zc : 8 * zc + 8, :], 127 - x * 4, 1), lane)
            around = (
                (n + N[x + 2, r : r + 8, :], n + N[x, r : r + 8, :]),
                (n + nyp, n + nym),
                (n + N[x + 1, r + 1 : r + 9, :], n + N[x + 1, r - 1 : r + 7, :]),
            )
            mids, sides = [], []
            for c in range(3):
                u = U[s, c, slot, r : r + 8, :]
                hh = pltpu.roll(hold, 127 - c * 32 - x * 4, 1)
                mids.append(u)
                sides.append(
                    (
                        (U[s, c, slot + 1, r : r + 8, :], U[s, c, slot - 1, r : r + 8, :]),
                        side_values(u, hh, lane),
                        (U[s, c, slot, r + 1 : r + 9, :], U[s, c, slot, r - 1 : r + 7, :]),
                    )
                )
            for c in range(3):
                u = mids[c]
                total = None
                for d in range(3):
                    up_c, um_c = sides[c][d]
                    up_d, um_d = sides[d][d]
                    term = around[d][0] * (up_c - u) - around[d][1] * (u - um_c) - (up_d * up_c - um_d * um_c)
                    total = term if total is None else total + term
                change = 0.5 * total
                if c == 0:
                    weight = DW[pl.ds(x * 32 + 8 * zc, 8), :]
                    change = change + (DRIVING_FORCE - (THRUST_COEFF * farm) * weight * u * jnp.abs(u))
                new = u + TIME_STEP * change
                if alpha:
                    new = alpha * U[0, c, slot, r : r + 8, :] + beta * new
                U[s + 1, c, slot, r : r + 8, :] = new

    for copy in (to_left, to_right, to_down, to_up, q_down, q_up):
        copy.wait_send()


def neighbours(gx_count, gy_count):
    gx, gy = lax.axis_index("gx"), lax.axis_index("gy")
    left = lax.rem(gy + gy_count - 1, gy_count)
    right = lax.rem(gy + 1, gy_count)
    down = lax.rem(gx + gx_count - 1, gx_count)
    up = lax.rem(gx + 1, gx_count)
    return left, right, down, up


STAGES = ((0.0, 1.0), (0.75, 0.25), (1.0 / 3.0, 2.0 / 3.0))


def rk_kernel(gx_count, gy_count, vel, tur, out, U, N, P, Q, T3, NS, DW, send, recv):
    near = neighbours(gx_count, gy_count)
    left, right, down, up = near
    barrier = pltpu.get_barrier_semaphore()
    for axis, index in (("gy", left), ("gy", right), ("gx", down), ("gx", up)):
        pl.semaphore_signal(barrier, inc=1, device_id={axis: index}, device_id_type=MESH)
    load_initial(vel, U)
    fill_pads(U, N, T3)
    find_disks(tur, DW, gy_count * 128)
    pl.semaphore_wait(barrier, 4)
    for s, (alpha, beta) in enumerate(STAGES):
        rk_stage(s, alpha, beta, near, U, N, P, Q, T3, NS, DW, send, recv)

    @pl.loop(0, 24)
    def _(i):
        c, x = i // 8, i % 8
        for zc in range(4):
            out[pl.ds(c * 256 + zc * 64 + x, 8, stride=8), :] = U[3, c, x + 2, 8 + 8 * zc : 16 + 8 * zc, :]


def rk_call(initial, turbine_cells, gx_count, gy_count):
    scratch = [
        pltpu.VMEM((4, 3, 12, 48, 128), F32),
        pltpu.VMEM((10, 48, 128), F32),
        pltpu.VMEM((3, 3, 32, 128), F32),
        pltpu.VMEM((3, 3, 32, 128), F32),
        pltpu.VMEM((3, 48, 128), F32),
        pltpu.VMEM((32, 128), F32),
        pltpu.VMEM((256, 128), F32),
        pltpu.SemaphoreType.DMA((3, 6)),
        pltpu.SemaphoreType.DMA((3, 6)),
    ]
    out = pl.pallas_call(
        functools.partial(rk_kernel, gx_count, gy_count),
        out_shape=jax.ShapeDtypeStruct((768, 128), F32),
        in_specs=[pl.BlockSpec(memory_space=pltpu.VMEM)] * 2,
        out_specs=pl.BlockSpec(memory_space=pltpu.VMEM),
        scratch_shapes=scratch,
        compiler_params=pltpu.CompilerParams(collective_id=0, has_side_effects=True, vmem_limit_bytes=48 << 20),
    )(initial.reshape(768, 128), turbine_cells)
    return out.reshape(3, 32, 8, 128)


def padded(x, sides, width):
    edges = {}
    for axis, dim in sides:
        count, length = (lax.axis_size(axis), x.shape[dim])
        up = [(i, (i + 1) % count) for i in range(count)]
        last = lax.slice_in_dim(x, length - width, length, axis=dim)
        initial = lax.slice_in_dim(x, 0, width, axis=dim)
        edges[dim] = (
            lax.ppermute(last, axis, up),
            lax.ppermute(initial, axis, [(b, a) for a, b in up]),
        )
    done = []
    for _, dim in sides:
        low, high = edges[dim]
        around = [(width, width) if d in done else (0, 0) for d in range(x.ndim)]
        x = jnp.concatenate([jnp.pad(low, around), x, jnp.pad(high, around)], axis=dim)
        done.append(dim)
    return x


def shifted(block, axis, distance):
    devices = range(lax.axis_size(axis))
    route = [(i - distance, i) for i in devices if i - distance in devices]
    return lax.ppermute(block, axis, route)


def cut_along(x, dim, count):
    dims = x.shape
    tiles = x.reshape(*dims[:dim], count, dims[dim] // count, *dims[dim + 1 :])
    return jnp.moveaxis(tiles, dim, 0)


def laid_out(tiles, dim):
    tiles = jnp.moveaxis(tiles, 0, dim)
    dims = tiles.shape
    return tiles.reshape(*dims[:dim], dims[dim] * dims[dim + 1], *dims[dim + 2 :])


def joined_exchange(x, axis, axes, splits, concats):
    sizes = [lax.axis_size(a) for a in axes]
    tiles = cut_along(x, splits[0], sizes[0])
    tiles = jnp.moveaxis(cut_along(tiles, splits[1] + 1, sizes[1]), 0, 1)
    inside = tiles.shape[2:]
    tiles = tiles.reshape(-1, *inside)
    tiles = lax.all_to_all(tiles, axis, split_axis=0, concat_axis=0, tiled=True)
    tiles = laid_out(tiles.reshape(*sizes, *inside), concats[0] + 1)
    return laid_out(tiles, concats[1])


def cas_table(row_index, column_index, length):
    product = row_index[:, None] * column_index[None, :] % length
    angle = product.astype(jnp.float32) * (2.0 * jnp.pi / length)
    return jnp.cos(angle) + jnp.sin(angle)


def shift_up(values):
    zeros = jnp.zeros_like(values[..., :1, :, :])
    return jnp.concatenate([values[..., 1:, :, :], zeros], axis=-3)


def shift_down(values):
    zeros = jnp.zeros_like(values[..., :1, :, :])
    return jnp.concatenate([zeros, values[..., :-1, :, :]], axis=-3)


def thomas(right_side, eigen_value):
    length = right_side.shape[0]
    inverses = []
    reduced = []
    for level_index in range(length):
        if level_index == 0:
            diagonal = eigen_value - 1.0
        elif level_index == length - 1:
            diagonal = eigen_value - 3.0
        else:
            diagonal = eigen_value - 2.0
        if level_index == 0:
            pivot_now = diagonal
            current = right_side[0] / pivot_now
        else:
            pivot_now = diagonal - inverses[-1]
            current = (right_side[level_index] - reduced[-1]) / pivot_now
        inverses.append(1.0 / pivot_now)
        reduced.append(current)
    solution = [reduced[-1]]
    for level_index in range(length - 2, -1, -1):
        solution.append(reduced[level_index] - inverses[level_index] * solution[-1])
    return jnp.stack(solution[::-1])


def spanwise_derivative(values, sine_y):
    return -sine_y * jnp.roll(jnp.flip(values, axis=-1), 1, axis=-1)


def widened(values):
    return padded(values, (("gx", 1), ("gy", 2)), 1)


def disk_weights(turbine_cells, along_x, along_y, along_z, total_y):
    matches = (along_x[:, None] == turbine_cells[None, :, 0]).astype(jnp.float32)
    offset_y = (along_y[None, :] - turbine_cells[:, 1:2] + total_y // 2) % total_y - total_y // 2
    offset_z = along_z[None, :] - turbine_cells[:, 2:3]
    distance = (
        offset_z[:, :, None] * offset_z[:, :, None] + offset_y[:, None, :] * offset_y[:, None, :]
    )
    inside = (distance <= RADIUS * RADIUS).astype(jnp.float32)
    return jnp.einsum("xt,tzy->zxy", matches, inside, precision=HIGHEST)


def tendency(velocity_now, farm_flag, disk_weight):
    levels, cells_x, cells_y = (velocity_now.shape[1], velocity_now.shape[2], velocity_now.shape[3])
    border = widened(velocity_now.reshape(3 * levels, cells_x, cells_y)).reshape(
        3, levels, cells_x + 2, cells_y + 2
    )
    plus_x = border[:, :, 2:, 1:-1]
    minus_x = border[:, :, :-2, 1:-1]
    plus_y = border[:, :, 1:-1, 2:]
    minus_y = border[:, :, 1:-1, :-2]
    plus_z = shift_up(velocity_now)
    minus_z = shift_down(velocity_now)
    gradients = [0.5 * (plus_x - minus_x), 0.5 * (plus_y - minus_y), 0.5 * (plus_z - minus_z)]
    strain_squares = jnp.zeros_like(velocity_now[0])
    for component in range(3):
        strain_squares = (
            strain_squares + gradients[component][component] * gradients[component][component]
        )
        for direction in range(component + 1, 3):
            shear = 0.5 * (gradients[direction][component] + gradients[component][direction])
            strain_squares = strain_squares + 2.0 * shear * shear
    viscosity = SMAG_COEFF * jnp.sqrt(2.0 * strain_squares)
    visc_border = widened(viscosity)
    visc_plus_x = visc_border[:, 2:, 1:-1]
    visc_minus_x = visc_border[:, :-2, 1:-1]
    visc_plus_y = visc_border[:, 1:-1, 2:]
    visc_minus_y = visc_border[:, 1:-1, :-2]
    visc_plus_z = shift_up(viscosity)
    visc_minus_z = shift_down(viscosity)
    advection = 0.5 * (plus_x[0] * plus_x - minus_x[0] * minus_x)
    advection = advection + 0.5 * (plus_y[1] * plus_y - minus_y[1] * minus_y)
    advection = advection + 0.5 * (plus_z[2] * plus_z - minus_z[2] * minus_z)
    diffusion = 0.5 * (viscosity + visc_plus_x) * (plus_x - velocity_now) - 0.5 * (
        viscosity + visc_minus_x
    ) * (velocity_now - minus_x)
    diffusion = (
        diffusion
        + 0.5 * (viscosity + visc_plus_y) * (plus_y - velocity_now)
        - 0.5 * (viscosity + visc_minus_y) * (velocity_now - minus_y)
    )
    diffusion = (
        diffusion
        + 0.5 * (viscosity + visc_plus_z) * (plus_z - velocity_now)
        - 0.5 * (viscosity + visc_minus_z) * (velocity_now - minus_z)
    )
    changes = diffusion - advection
    streamwise = DRIVING_FORCE - THRUST_COEFF * farm_flag * disk_weight * velocity_now[0] * jnp.abs(
        velocity_now[0]
    )
    return jnp.concatenate([changes[:1] + streamwise[None], changes[1:]], axis=0)


def on_device(velocity, turbine_cells, fringe_bounds):
    initial = velocity[0]
    levels, cells_x, cells_y = (initial.shape[1], initial.shape[2], initial.shape[3])
    total_y = cells_y * lax.axis_size("gy")
    x_anchor = lax.axis_index("gx") * cells_x
    y_anchor = lax.axis_index("gy") * cells_y
    farm_flag = lax.axis_index("sec").astype(jnp.float32)
    along_x = x_anchor + jnp.arange(cells_x, dtype=jnp.int32)
    along_y = y_anchor + jnp.arange(cells_y, dtype=jnp.int32)
    along_z = jnp.arange(levels, dtype=jnp.int32)
    segment_three = rk_call(initial, turbine_cells, lax.axis_size("gx"), lax.axis_size("gy"))
    regrouped = lax.all_to_all(segment_three, "gx", split_axis=1, concat_axis=2, tiled=True)
    count_x = regrouped.shape[2]
    quarter = count_x // 4
    cut_at = count_x - quarter
    outlet_part = regrouped[:, :, cut_at:, :]
    upstream = shifted(outlet_part, "sec", 1)
    columns = cut_at + jnp.arange(quarter, dtype=jnp.int32)
    inside = ((columns >= fringe_bounds[0]) & (columns < fringe_bounds[1])).astype(jnp.float32)
    weight = FRINGE_BLEND * farm_flag * inside
    blended_part = outlet_part + weight[:, None] * (upstream - outlet_part)
    regrouped = jnp.concatenate([regrouped[:, :, :cut_at, :], blended_part], axis=2)
    index_x = jnp.arange(count_x, dtype=jnp.int32)
    table_x = cas_table(index_x, index_x, count_x)
    gradient_u = 0.5 * (jnp.roll(regrouped[0], -1, axis=1) - jnp.roll(regrouped[0], 1, axis=1))
    fields = jnp.stack([gradient_u, regrouped[1], regrouped[2]])
    spectral_x = jnp.einsum("kx,czxy->czky", table_x, fields, precision=HIGHEST)
    columns_view = joined_exchange(spectral_x, ("gx", "gy"), ("gx", "gy"), (2, 2), (1, 3))
    slice_width = columns_view.shape[2]
    count_y = columns_view.shape[3]
    index_y = jnp.arange(count_y, dtype=jnp.int32)
    table_y = cas_table(index_y, index_y, count_y)
    spectrum = jnp.einsum("ly,czky->czkl", table_y, columns_view, precision=HIGHEST)
    sine_y = jnp.sin(index_y.astype(jnp.float32) * (2.0 * jnp.pi / count_y))
    source = (
        spectrum[0]
        + spanwise_derivative(spectrum[1], sine_y)
        + 0.5 * (shift_up(spectrum[2]) - shift_down(spectrum[2]))
    )
    wave_x = (
        lax.axis_index("gx") * cells_x
        + lax.axis_index("gy") * slice_width
        + jnp.arange(slice_width, dtype=jnp.int32)
    )
    eigen_value = 2.0 * jnp.cos(wave_x.astype(jnp.float32) * (2.0 * jnp.pi / count_x))[:, None]
    eigen_value = (
        eigen_value
        + 2.0 * jnp.cos(index_y.astype(jnp.float32) * (2.0 * jnp.pi / count_y))[None, :]
        - 4.0
    )
    solved = thomas(source, eigen_value)
    above_level = jnp.concatenate([solved[1:], -solved[-1:]], axis=0)
    below_level = jnp.concatenate([solved[:1], solved[:-1]], axis=0)
    coefficients = jnp.stack(
        [solved, spanwise_derivative(solved, sine_y), 0.5 * (above_level - below_level)]
    )
    physical_y = jnp.einsum("yl,czkl->czky", table_y, coefficients, precision=HIGHEST) * (
        1.0 / count_y
    )
    returned = joined_exchange(physical_y, ("gx", "gy"), ("gx", "gy"), (1, 3), (2, 2))
    group_size = count_x // lax.axis_size("gy")
    wave_back = (
        index_x // slice_width % lax.axis_size("gx") * cells_x
        + index_x // group_size * slice_width
        + index_x % slice_width
    )
    inverse_table = cas_table(index_x, wave_back, count_x)
    physical = jnp.einsum("xp,czpy->czxy", inverse_table, returned, precision=HIGHEST) * (
        1.0 / count_x
    )
    pressure = physical[0]
    gradient_p = 0.5 * (jnp.roll(pressure, -1, axis=1) - jnp.roll(pressure, 1, axis=1))
    velocity_next = regrouped - jnp.stack([gradient_p, physical[1], physical[2]])
    return (velocity_next[None], pressure[None])


def solution(mesh):
    return jax.shard_map(
        on_device,
        mesh=mesh,
        in_specs=(P_("sec", None, None, "gx", "gy"), P_(), P_()),
        out_specs=(P_("sec", None, "gx", None, "gy"), P_("sec", "gx", None, "gy")),
        check_vma=False,
    )
```

```python
import jax
import jax.numpy as jnp
import numpy as np
from jax import lax
from jax.experimental import pallas as pl
from jax.experimental.pallas import tpu as pltpu
from jax.sharding import PartitionSpec

TIME_STEP = 0.05
SMAG_COEFF = 0.1
THRUST_COEFF = 4.0
DRIVING_FORCE = 0.1
FRINGE_BLEND = 0.5
RADIUS = 4
MESH = pl.DeviceIdType.MESH
F32 = jnp.float32


def turned(v, shift):
    return pltpu.roll(v, shift % 128, 1)


def viscosity(xp, xm, yp, ym, zp, zm):
    a = xp[0] - xm[0]
    b = yp[1] - ym[1]
    c = zp[2] - zm[2]
    s1 = (yp[0] - ym[0]) + (xp[1] - xm[1])
    s2 = (zp[0] - zm[0]) + (xp[2] - xm[2])
    s3 = (zp[1] - zm[1]) + (yp[2] - ym[2])
    total = 0.5 * (a * a + b * b + c * c) + 0.25 * (s1 * s1 + s2 * s2 + s3 * s3)
    return SMAG_COEFF * jnp.sqrt(total)


def lanes(rows):
    return lax.broadcasted_iota(jnp.int32, (rows, 128), 1)


def fill_pads(U, N, T3):
    zeros = jnp.zeros((8, 128), F32)

    @pl.loop(0, U.shape[0] * 3)
    def _(i):
        s, c = i // 3, i % 3
        for slot in range(12):
            U[s, c, slot, 0:8, :] = zeros
            U[s, c, slot, 40:48, :] = zeros

    for i in range(10):
        N[i, 0:8, :] = zeros
        N[i, 40:48, :] = zeros
    for c in range(3):
        T3[c, 0:8, :] = zeros
        T3[c, 40:48, :] = zeros


def load_initial(vel, U):
    @pl.loop(0, 24)
    def _(i):
        c, x = i // 8, i % 8
        for zc in range(4):
            U[0, c, x + 2, 8 + 8 * zc : 16 + 8 * zc, :] = vel[pl.ds(c * 256 + zc * 64 + x, 8, stride=8), :]


def find_disks(tur, DW, total_y):
    x_anchor = lax.axis_index("gx") * 8
    y_anchor = lax.axis_index("gy") * 128
    turb = tur.shape[0]
    lane = lanes(turb)
    match = (tur[:, 0:1] == x_anchor + lane).astype(F32)
    offset = lane + (y_anchor + total_y // 2 + total_y) - tur[:, 1:2]
    offset = jnp.where(offset >= total_y, offset - total_y, offset)
    offset = jnp.where(offset >= total_y, offset - total_y, offset) - total_y // 2
    square_y = offset * offset
    height = tur[:, 2:3] + jnp.zeros((turb, 128), jnp.int32)

    @pl.loop(0, 32)
    def _(z):
        off_z = z - height
        inside = (off_z * off_z + square_y <= RADIUS * RADIUS).astype(F32)
        count = lax.dot_general(match, inside, (((0,), (0,)), ((), ())), preferred_element_type=F32)
        DW[pl.ds(z, 8, stride=32), :] = count[0:8, :]


def remote(src, dst, send, recv, axis, index):
    return pltpu.make_async_remote_copy(
        src_ref=src, dst_ref=dst, send_sem=send, recv_sem=recv, device_id={axis: index}, device_id_type=MESH
    )


def pack_edges(U, s, comps):
    lane = lanes(32)
    packed = jnp.zeros((32, 128), F32)
    for c in comps:
        for x in range(8):
            base = c * 32 + x * 4
            packed = jnp.where(lane // 4 == base // 4, turned(U[s, c, x + 2, 8:40, :], base + 2), packed)
    return packed


def side_values(u, hh, lane):
    return (jnp.where(lane == 127, hh, turned(u, -1)), jnp.where(lane == 0, hh, turned(u, 1)))


def rk_stage(s, alpha, beta, near, U, N, P, Q, T3, NS, DW, send, recv):
    left, right, down, up = near
    lane32 = lanes(32)
    lane = lanes(8)
    to_down = remote(U.at[s, :, 2:4, 8:40, :], U.at[s, :, 10:12, 8:40, :], send.at[s, 0], recv.at[s, 0], "gx", down)
    to_up = remote(U.at[s, :, 8:10, 8:40, :], U.at[s, :, 0:2, 8:40, :], send.at[s, 1], recv.at[s, 1], "gx", up)
    to_left = remote(P.at[s, 0], P.at[s, 2], send.at[s, 2], recv.at[s, 2], "gy", left)
    to_right = remote(P.at[s, 0], P.at[s, 1], send.at[s, 3], recv.at[s, 3], "gy", right)
    q_down = remote(Q.at[s, 1], Q.at[s, 2], send.at[s, 4], recv.at[s, 4], "gx", down)
    q_up = remote(Q.at[s, 1], Q.at[s, 0], send.at[s, 5], recv.at[s, 5], "gx", up)
    P[s, 0] = pack_edges(U, s, range(3))
    to_left.start()
    to_right.start()
    to_down.start()
    to_up.start()
    to_left.wait_recv()
    to_right.wait_recv()
    own, from_left, from_right = P[s, 0], P[s, 1], P[s, 2]
    Q[s, 1] = jnp.where(lane32 % 4 == 0, turned(from_right, -2), from_left)
    q_down.start()
    q_up.start()
    strip_left = jnp.where(lane32 % 4 < 2, from_left, own)
    strip_right = jnp.where(lane32 % 4 < 2, own, from_right)
    for c in range(3):
        T3[c, 8:40, :] = jnp.where(lane32 < 32, turned(strip_left, -32 * c), turned(strip_right, 32 - 32 * c))
    to_down.wait_recv()
    to_up.wait_recv()
    q_down.wait_recv()
    q_up.wait_recv()
    q_minus, q_plus = Q[s, 0], Q[s, 2]
    parts = [[] for _ in range(6)]
    for c in range(3):
        t = T3[c, 8:40, :]
        xp = jnp.where(lane32 == 29, turned(q_plus, 28 - c * 32), turned(t, -4))
        xp = jnp.where(lane32 == 62, turned(q_plus, 62 - c * 32), xp)
        xm = jnp.where(lane32 == 1, turned(q_minus, -28 - c * 32), turned(t, 4))
        xm = jnp.where(lane32 == 34, turned(q_minus, 6 - c * 32), xm)
        values = (xp, xm, turned(t, -1), turned(t, 1), T3[c, 9:41, :], T3[c, 7:39, :])
        for part, value in zip(parts, values):
            part.append(value)
    strip = viscosity(*parts)
    NS[...] = jnp.where(lane32 % 4 == 0, turned(strip, -34), strip)

    @pl.loop(0, 10)
    def _(i):
        slot = i + 1
        which = jnp.where(i == 0, 0, jnp.where(i == 9, 2, 1))
        column = jnp.where(i == 0, 7, jnp.where(i == 9, 0, i - 1))
        for zc in range(4):
            r = 8 + 8 * zc
            hold = Q[s, which, 8 * zc : 8 * zc + 8, :]
            pieces = [[] for _ in range(6)]
            for c in range(3):
                u = U[s, c, slot, r : r + 8, :]
                hh = pltpu.roll(hold, 127 - c * 32 - column * 4, 1)
                yp, ym = side_values(u, hh, lane)
                values = (
                    U[s, c, slot + 1, r : r + 8, :],
                    U[s, c, slot - 1, r : r + 8, :],
                    yp,
                    ym,
                    U[s, c, slot, r + 1 : r + 9, :],
                    U[s, c, slot, r - 1 : r + 7, :],
                )
                for piece, value in zip(pieces, values):
                    piece.append(value)
            N[i, r : r + 8, :] = viscosity(*pieces)

    farm = lax.axis_index("sec").astype(F32)

    @pl.loop(0, 8)
    def _(x):
        slot = x + 2
        for zc in range(4):
            r = 8 + 8 * zc
            n = N[x + 1, r : r + 8, :]
            hold = Q[s, 1, 8 * zc : 8 * zc + 8, :]
            nyp, nym = side_values(n, pltpu.roll(NS[8 * zc : 8 * zc + 8, :], 127 - x * 4, 1), lane)
            around = (
                (n + N[x + 2, r : r + 8, :], n + N[x, r : r + 8, :]),
                (n + nyp, n + nym),
                (n + N[x + 1, r + 1 : r + 9, :], n + N[x + 1, r - 1 : r + 7, :]),
            )
            mids, sides = [], []
            for c in range(3):
                u = U[s, c, slot, r : r + 8, :]
                hh = pltpu.roll(hold, 127 - c * 32 - x * 4, 1)
                mids.append(u)
                sides.append(
                    (
                        (U[s, c, slot + 1, r : r + 8, :], U[s, c, slot - 1, r : r + 8, :]),
                        side_values(u, hh, lane),
                        (U[s, c, slot, r + 1 : r + 9, :], U[s, c, slot, r - 1 : r + 7, :]),
                    )
                )
            for c in range(3):
                u = mids[c]
                total = None
                for d in range(3):
                    up_c, um_c = sides[c][d]
                    up_d, um_d = sides[d][d]
                    term = around[d][0] * (up_c - u) - around[d][1] * (u - um_c) - (up_d * up_c - um_d * um_c)
                    total = term if total is None else total + term
                change = 0.5 * total
                if c == 0:
                    weight = DW[pl.ds(x * 32 + 8 * zc, 8), :]
                    change = change + (DRIVING_FORCE - (THRUST_COEFF * farm) * weight * u * jnp.abs(u))
                new = u + TIME_STEP * change
                if alpha:
                    new = alpha * U[0, c, slot, r : r + 8, :] + beta * new
                U[s + 1, c, slot, r : r + 8, :] = new

    for copy in (to_left, to_right, to_down, to_up, q_down, q_up):
        copy.wait_send()


def neighbours(gx_count, gy_count):
    gx, gy = lax.axis_index("gx"), lax.axis_index("gy")
    left = lax.rem(gy + gy_count - 1, gy_count)
    right = lax.rem(gy + 1, gy_count)
    down = lax.rem(gx + gx_count - 1, gx_count)
    up = lax.rem(gx + 1, gx_count)
    return left, right, down, up


STAGES = ((0.0, 1.0), (0.75, 0.25), (1.0 / 3.0, 2.0 / 3.0))


def dht_tables():
    def cas(product, length):
        angle = (product % length).astype(np.float64) * (2.0 * np.pi / length)
        return np.cos(angle) + np.sin(angle)

    b = np.arange(128)[:, None]
    f = np.arange(128)[None, :]
    spanwise = np.zeros((4, 256, 256))
    spanwise[0, :128, :128] = cas(b * (8 * f), 1024)
    spanwise[0, 128:, 128:] = cas(b * (4 + 8 * f), 1024)
    for p in (1, 2, 3):
        low, high = p + 8 * f, 8 - p + 8 * f
        spanwise[p, :128, :128] = cas(b * low, 1024)
        spanwise[p, 128:, :128] = cas(-b * low, 1024)
        spanwise[p, :128, 128:] = cas(b * high, 1024)
        spanwise[p, 128:, 128:] = -cas(-b * high, 1024)
    x = np.arange(256)
    streamwise = cas(x[:, None] * x[None, :], 256)

    def halves(table):
        table = table.astype(np.float32)
        top = table.astype(jnp.bfloat16)
        rest = (table - top.astype(np.float32)).astype(jnp.bfloat16)
        return np.stack([top, rest])

    return halves(spanwise), halves(streamwise)


HALF_ROOT = 0.5**0.5


def halved(v):
    top = v.astype(jnp.bfloat16)
    return top, (v - top.astype(F32)).astype(jnp.bfloat16)


def dot(a, b, dims=((1,), (0,))):
    return lax.dot_general(a, b, (dims, ((), ())), preferred_element_type=F32)


def rows_by_table(v, top, rest, dims):
    rows = v.shape[0]
    v_top, v_rest = halved(v)
    both = dot(jnp.concatenate([v_top, v_rest], axis=0), top, dims)
    return both[:rows] + both[rows:] + dot(v_top, rest, dims)


def table_by_columns(top, rest, v):
    v_top, v_rest = halved(v)
    return dot(top, v_top) + dot(top, v_rest) + dot(rest, v_top)


def swap_blocks(v):
    lane = lanes(8)
    low = lane < 64
    odd = (lane // 32) % 2 == 1
    a, b, c, d = v
    a, c = jnp.where(low, a, turned(c, 64)), jnp.where(low, turned(a, 64), c)
    b, d = jnp.where(low, b, turned(d, 64)), jnp.where(low, turned(b, 64), d)
    a, b = jnp.where(odd, turned(b, 32), a), jnp.where(odd, b, turned(a, -32))
    c, d = jnp.where(odd, turned(d, 32), c), jnp.where(odd, d, turned(c, -32))
    return a, b, c, d


def far_first(i, count):
    step = (i + 1) // 2
    return count // 2 + jnp.where(i % 2 == 0, step, -step)


def find_pivots(INV):
    gx, gy = lax.axis_index("gx"), lax.axis_index("gy")
    lane = lanes(8)
    row = lax.broadcasted_iota(jnp.int32, (8, 128), 0)
    k = gy * 32 + (lane // 32) * 8 + row
    pair = gx // 8
    j = (gx % 8) * 32 + lane % 32
    second = jnp.where(pair == 0, 4, 8 - pair)
    ell = jnp.where(j < 128, pair + 8 * j, second + 8 * (j - 128))
    wave_x = jnp.sin(k.astype(F32) * (jnp.pi / 256))
    wave_y = jnp.sin(ell.astype(F32) * (jnp.pi / 1024))
    eigen = -4.0 * (wave_x * wave_x + wave_y * wave_y)
    inverse = 1.0 / (eigen - 1.0)
    INV[0] = inverse
    for z in range(1, 32):
        inverse = 1.0 / (eigen - (3.0 if z == 31 else 2.0) - inverse)
        INV[z] = inverse


def divergence(near, fringe, U, P, DM, GM, send, recv):
    left, right, down, up = near
    lane32, lane = lanes(32), lanes(8)
    s = 3
    to_down = remote(U.at[s, 0, 2, 8:40, :], U.at[s, 0, 10, 8:40, :], send.at[s, 0], recv.at[s, 0], "gx", down)
    to_up = remote(U.at[s, 0, 9, 8:40, :], U.at[s, 0, 1, 8:40, :], send.at[s, 1], recv.at[s, 1], "gx", up)
    to_left = remote(P.at[s, 0], P.at[s, 2], send.at[s, 2], recv.at[s, 2], "gy", left)
    to_right = remote(P.at[s, 0], P.at[s, 1], send.at[s, 3], recv.at[s, 3], "gy", right)
    to_down.start()
    to_up.start()
    P[s, 0] = pack_edges(U, s, [1])
    to_left.start()
    to_right.start()
    yield
    for copy in (to_left, to_right, to_down, to_up):
        copy.wait_recv()
    P[s, 0 + 3] = jnp.where(lane32 % 4 == 0, turned(P[s, 2], -2), P[s, 1])
    farm = lax.axis_index("sec").astype(F32)
    anchor = lax.axis_index("gx") * 8
    total_x = 8 * lax.axis_size("gx")

    def mask(x):
        column = jnp.full((8, 128), lax.rem(anchor + x + total_x, total_x), jnp.int32)
        return jnp.where((column >= fringe[0]) & (column < fringe[1]), FRINGE_BLEND, 0.0).astype(F32)

    @pl.loop(0, 8)
    def _(x):
        slot = x + 2
        m_here, m_plus, m_minus = mask(x), mask(x + 1), mask(x - 1)
        for zc in range(4):
            r = 8 + 8 * zc
            up_u, um_u = U[s, 0, slot + 1, r : r + 8, :], U[s, 0, slot - 1, r : r + 8, :]
            hh = pltpu.roll(P[s, 3, 8 * zc : 8 * zc + 8, :], 127 - 32 - x * 4, 1)
            yp, ym = side_values(U[s, 1, slot, r : r + 8, :], hh, lane)
            across = 0.5 * ((yp - ym) + (U[s, 2, slot, r + 1 : r + 9, :] - U[s, 2, slot, r - 1 : r + 7, :]))
            whole = 0.5 * (up_u - um_u) + across
            part = 0.5 * (m_plus * up_u - m_minus * um_u) + m_here * across
            DM[pl.ds(zc * 64 + x, 8, stride=8), :] = whole - farm * part
            GM[pl.ds(zc * 64 + x, 8, stride=8), :] = part

    for copy in (to_left, to_right, to_down, to_up):
        copy.wait_send()


def spanwise_forward(R1, WY, XS):
    x = [R1[g] for g in range(8)]
    e = [x[g] + x[g + 4] for g in range(4)]
    o = [x[g] - x[g + 4] for g in range(4)]
    plus, minus = HALF_ROOT * (o[1] + o[3]), HALF_ROOT * (o[1] - o[3])
    sides = (
        (e[0] + e[1] + e[2] + e[3], e[0] - e[1] + e[2] - e[3]),
        (o[0] + minus, plus + o[2]),
        (e[0] - e[2], e[1] - e[3]),
        (o[0] - minus, plus - o[2]),
    )
    for p in range(4):
        line = rows_by_table(jnp.concatenate(sides[p], axis=1), WY[0, p], WY[1, p], ((1,), (0,)))
        for h in range(2):
            tiles = swap_blocks([line[8 * z : 8 * z + 8, 128 * h : 128 * h + 128] for z in range(4)])
            for q in range(4):
                XS[p * 8 + h * 4 + q] = tiles[q]


def solve_levels(R3, INV, SQ):
    levels = []
    for g in range(8):
        levels.extend(swap_blocks([R3[g, 8 * i : 8 * i + 8, :] for i in range(4)]))
    scale = 1.0 / (256 * 1024)
    current = (scale * levels[0]) * INV[0]
    reduced = [current]
    for z in range(1, 32):
        current = (scale * levels[z] - current) * INV[z]
        reduced.append(current)
    solved = [None] * 32
    solved[31] = reduced[31]
    for z in range(30, -1, -1):
        solved[z] = reduced[z] - INV[z] * solved[z + 1]
    for z in range(32):
        above = solved[z + 1] if z < 31 else -solved[31]
        below = solved[z - 1] if z > 0 else solved[0]
        SQ[z, 0] = solved[z]
        SQ[z, 1] = 0.5 * (above - below)


def spanwise_back(R4, WY, F):
    lane = lanes(64)
    rows = []
    for p in range(4):
        halves = []
        for h in range(2):
            stack = []
            for f in range(2):
                stack.extend(swap_blocks([R4[p * 8 + h * 4 + q, f] for q in range(4)]))
            halves.append(jnp.concatenate(stack, axis=0))
        rows.append(rows_by_table(jnp.concatenate(halves, axis=1), WY[0, p], WY[1, p], ((1,), (1,))))
    a = [row[:, :128] for row in rows]
    b = [row[:, 128:] for row in rows]
    total, change = a[0] + b[0], a[0] - b[0]
    t = (total + a[2], change + b[2], total - a[2], change - b[2])
    minus, plus = HALF_ROOT * (a[1] - a[3]), HALF_ROOT * (b[1] + b[3])
    o = (a[1] + a[3], minus + plus, b[1] - b[3], plus - minus)
    x = [t[g] + o[g] for g in range(4)] + [t[g] - o[g] for g in range(4)]
    lane = lanes(32)
    ahead = [turned(v[:32], -1) for v in x]
    behind = [turned(v[:32], 1) for v in x]
    for g in range(8):
        F[g, 0] = x[g][:32]
        F[g, 2] = x[g][32:]
        plus_y = jnp.where(lane == 127, ahead[(g + 1) % 8], ahead[g])
        minus_y = jnp.where(lane == 0, behind[(g + 7) % 8], behind[g])
        F[g, 1] = 0.5 * (plus_y - minus_y)


def step_kernel(vel_ref, tur, fringe, wy_ref, tx_ref, out_v, out_p, U, N, P, Q, T3, NS, DW, INV, WY, TX, VEL, DM, GM, R1, RG, XS, R2, YS, R3, SQ, R4, F, R5, UZ, RA, BL, PP, send, recv, local, a_send, a_recv, x_send, x_recv, y_send, y_recv, g_send, g_recv, b_send, b_recv):
    gx_count, gy_count = lax.axis_size("gx"), lax.axis_size("gy")
    sec, gx, gy = lax.axis_index("sec"), lax.axis_index("gx"), lax.axis_index("gy")
    near = neighbours(gx_count, gy_count)
    barrier = pltpu.get_barrier_semaphore()
    loads = [
        pltpu.make_async_copy(vel_ref, VEL, local.at[0]),
        pltpu.make_async_copy(wy_ref, WY, local.at[1]),
        pltpu.make_async_copy(tx_ref, TX, local.at[2]),
    ]
    for load in loads:
        load.start()

    @pl.loop(1, gx_count)
    def _(d):
        pl.semaphore_signal(barrier, inc=1, device_id={"gx": lax.rem(gx + d, gx_count)}, device_id_type=MESH)

    @pl.loop(1, gy_count)
    def _(d):
        pl.semaphore_signal(barrier, inc=1, device_id={"gy": lax.rem(gy + d, gy_count)}, device_id_type=MESH)

    @pl.loop(0, gy_count)
    def _(d):
        pl.semaphore_signal(barrier, inc=1, device_id={"sec": 1 - sec, "gy": d}, device_id_type=MESH)

    fill_pads(U, N, T3)
    loads[0].wait()
    load_initial(VEL, U)
    find_disks(tur, DW, gy_count * 128)
    find_pivots(INV)
    pl.semaphore_wait(barrier, gx_count - 1 + gy_count - 1 + gy_count)
    for s, (alpha, beta) in enumerate(STAGES):
        rk_stage(s, alpha, beta, near, U, N, P, Q, T3, NS, DW, send, recv)

    work = divergence(near, fringe, U, P, DM, GM, send, recv)
    next(work)

    @pl.loop(0, 24)
    def _(i):
        c, x = i // 8, i % 8
        for zc in range(4):
            UZ[pl.ds(c * 256 + zc * 64 + x, 8, stride=8), :] = U[3, c, x + 2, 8 + 8 * zc : 16 + 8 * zc, :]

    def velocity_copy(c, peer, source):
        return remote(UZ.at[pl.ds(c * 256 + peer * 8, 8), :], RA.at[c, pl.ds(source * 8, 8), :], a_send.at[c, peer], a_recv.at[c, source], "gx", peer)

    def send_velocity(c):
        @pl.loop(0, gx_count - 1)
        def _(i):
            velocity_copy(c, lax.rem(gx + far_first(i, gx_count), gx_count), gx).start()

        RA[c, pl.ds(pl.multiple_of(gx * 8, 8), 8), :] = UZ[pl.ds(pl.multiple_of(c * 256 + gx * 8, 8), 8), :]

    send_velocity(0)
    send_velocity(1)
    for _ in work:
        pass

    def group_copy(peer, source):
        return remote(DM.at[pl.ds(peer * 32, 32), :], R1.at[source], y_send.at[0, peer], y_recv.at[0, source], "gy", peer)

    def fringe_copy(peer, source):
        return pltpu.make_async_remote_copy(
            src_ref=GM.at[pl.ds(peer * 32, 32), :],
            dst_ref=RG.at[source],
            send_sem=g_send.at[peer],
            recv_sem=g_recv.at[source],
            device_id={"sec": 1, "gy": peer},
            device_id_type=MESH,
        )

    touches = (gx == 0) | (gx >= 3 * gx_count // 4 - 1)

    @pl.when(touches & (sec == 0))
    def _():
        @pl.loop(0, gy_count)
        def _(peer):
            fringe_copy(peer, gy).start()

    @pl.loop(1, gy_count)
    def _(d):
        group_copy(lax.rem(gy + d, gy_count), gy).start()

    R1[gy] = DM[pl.ds(pl.multiple_of(gy * 32, 32), 32), :]

    @pl.loop(1, gy_count)
    def _(d):
        group_copy(gy, lax.rem(gy + d, gy_count)).wait_recv()

    @pl.when(touches & (sec == 1))
    def _():
        @pl.loop(0, gy_count)
        def _(source):
            fringe_copy(gy, source).wait_recv()

        for g in range(8):
            R1[g] = R1[g] + RG[g]

    loads[1].wait()
    loads[2].wait()
    spanwise_forward(R1, WY, XS)

    def chunk_copy(peer, source):
        return remote(XS.at[peer], R2.at[pl.ds(source * 8, 8), :], x_send.at[0, peer], x_recv.at[0, source], "gx", peer)

    @pl.loop(0, gx_count - 1)
    def _(i):
        chunk_copy(lax.rem(gx + far_first(i, gx_count), gx_count), gx).start()

    R2[pl.ds(pl.multiple_of(gx * 8, 8), 8), :] = XS[gx]
    send_velocity(2)

    @pl.loop(1, gx_count)
    def _(d):
        chunk_copy(gx, lax.rem(gx + d, gx_count)).wait_recv()

    YS[...] = table_by_columns(TX[0], TX[1], R2[...])

    def wave_copy(peer, source):
        return remote(YS.at[pl.ds(peer * 32, 32), :], R3.at[source], y_send.at[1, peer], y_recv.at[1, source], "gy", peer)

    @pl.loop(1, gy_count)
    def _(d):
        wave_copy(lax.rem(gy + d, gy_count), gy).start()

    R3[gy] = YS[pl.ds(pl.multiple_of(gy * 32, 32), 32), :]

    @pl.loop(1, gy_count)
    def _(d):
        wave_copy(gy, lax.rem(gy + d, gy_count)).wait_recv()

    solve_levels(R3, INV, SQ)

    def level_copy(peer, source):
        return remote(SQ.at[peer], R4.at[source], x_send.at[1, peer], x_recv.at[1, source], "gx", peer)

    @pl.loop(0, gx_count - 1)
    def _(i):
        level_copy(lax.rem(gx + far_first(i, gx_count), gx_count), gx).start()

    R4[gx] = SQ[gx]

    @pl.loop(0, 3 * (gx_count - 1))
    def _(i):
        c, d = i // (gx_count - 1), 1 + i % (gx_count - 1)
        velocity_copy(c, gx, lax.rem(gx + d, gx_count)).wait_recv()

    quarter = pltpu.make_async_remote_copy(
        src_ref=RA.at[:, 192:256, :],
        dst_ref=BL,
        send_sem=b_send.at[0],
        recv_sem=b_recv.at[0],
        device_id={"sec": 1},
        device_id_type=MESH,
    )

    @pl.when(sec == 0)
    def _():
        quarter.start()

    @pl.loop(1, gx_count)
    def _(d):
        level_copy(gx, lax.rem(gx + d, gx_count)).wait_recv()

    spanwise_back(R4, WY, F)

    def plane_copy(peer, source):
        return remote(F.at[peer], R5.at[source], y_send.at[2, peer], y_recv.at[2, source], "gy", peer)

    @pl.loop(1, gy_count)
    def _(d):
        plane_copy(lax.rem(gy + d, gy_count), gy).start()

    R5[gy] = F[gy]

    @pl.when(sec == 1)
    def _():
        quarter.wait_recv()
        row = lax.broadcasted_iota(jnp.int32, (64, 128), 0) + 192
        weight = jnp.where((row >= fringe[0]) & (row < fringe[1]), FRINGE_BLEND, 0.0).astype(F32)
        for c in range(3):
            mine = RA[c, 192:256, :]
            RA[c, 192:256, :] = mine + weight * (BL[c] - mine)

    @pl.loop(1, gy_count)
    def _(d):
        plane_copy(gy, lax.rem(gy + d, gy_count)).wait_recv()

    planes = []
    for f in range(3):
        planes.append(table_by_columns(TX[0], TX[1], jnp.concatenate([R5[g, f] for g in range(8)], axis=0)))
    pressure = planes[0]
    out_p[...] = pressure
    PP[8:264, :] = pressure
    PP[7:8, :] = pressure[255:256]
    PP[264:265, :] = pressure[0:1]
    out_v[0] = RA[0] - 0.5 * (PP[9:265, :] - PP[7:263, :])
    out_v[1] = RA[1] - planes[1]
    out_v[2] = RA[2] - planes[2]

    @pl.loop(1, gx_count)
    def _(d):
        peer = lax.rem(gx + d, gx_count)
        for c in range(3):
            velocity_copy(c, peer, gx).wait_send()
        chunk_copy(peer, gx).wait_send()
        level_copy(peer, gx).wait_send()

    @pl.loop(1, gy_count)
    def _(d):
        peer = lax.rem(gy + d, gy_count)
        group_copy(peer, gy).wait_send()
        wave_copy(peer, gy).wait_send()
        plane_copy(peer, gy).wait_send()

    @pl.when(touches & (sec == 0))
    def _():
        @pl.loop(0, gy_count)
        def _(peer):
            fringe_copy(peer, gy).wait_send()

    @pl.when(sec == 0)
    def _():
        quarter.wait_send()


def on_device(velocity, turbine_cells, fringe_bounds):
    gx_count, gy_count = lax.axis_size("gx"), lax.axis_size("gy")
    spanwise, streamwise = dht_tables()
    vmem = pltpu.VMEM
    dma = pltpu.SemaphoreType.DMA
    scratch = [
        vmem((4, 3, 12, 48, 128), F32),
        vmem((10, 48, 128), F32),
        vmem((4, 4, 32, 128), F32),
        vmem((3, 3, 32, 128), F32),
        vmem((3, 48, 128), F32),
        vmem((32, 128), F32),
        vmem((256, 128), F32),
        vmem((32, 8, 128), F32),
        vmem((2, 4, 256, 256), jnp.bfloat16),
        vmem((2, 256, 256), jnp.bfloat16),
        vmem((768, 128), F32),
        vmem((256, 128), F32),
        vmem((256, 128), F32),
        vmem((8, 32, 128), F32),
        vmem((8, 32, 128), F32),
        vmem((32, 8, 128), F32),
        vmem((256, 128), F32),
        vmem((256, 128), F32),
        vmem((8, 32, 128), F32),
        vmem((32, 2, 8, 128), F32),
        vmem((32, 2, 8, 128), F32),
        vmem((8, 3, 32, 128), F32),
        vmem((8, 3, 32, 128), F32),
        vmem((768, 128), F32),
        vmem((3, 256, 128), F32),
        vmem((3, 64, 128), F32),
        vmem((272, 128), F32),
        dma((4, 6)),
        dma((4, 6)),
        dma((3,)),
        dma((3, gx_count)),
        dma((3, gx_count)),
        dma((2, gx_count)),
        dma((2, gx_count)),
        dma((3, gy_count)),
        dma((3, gy_count)),
        dma((gy_count,)),
        dma((gy_count,)),
        dma((1,)),
        dma((1,)),
    ]
    anywhere, inside = pl.BlockSpec(memory_space=pl.ANY), pl.BlockSpec(memory_space=pltpu.VMEM)
    flat = pl.BlockSpec(memory_space=pltpu.SMEM)
    next_velocity, pressure = pl.pallas_call(
        step_kernel,
        out_shape=(jax.ShapeDtypeStruct((3, 256, 128), F32), jax.ShapeDtypeStruct((256, 128), F32)),
        in_specs=[anywhere, inside, flat, anywhere, anywhere],
        out_specs=(inside, inside),
        scratch_shapes=scratch,
        compiler_params=pltpu.CompilerParams(collective_id=0, has_side_effects=True, vmem_limit_bytes=48 << 20),
    )(velocity.reshape(768, 128), turbine_cells, fringe_bounds, jnp.asarray(spanwise), jnp.asarray(streamwise))
    return (next_velocity.reshape(1, 3, 1, 256, 128), pressure.reshape(1, 1, 256, 128))


def solution(mesh):
    return jax.shard_map(
        on_device,
        mesh=mesh,
        in_specs=(PartitionSpec("sec", None, None, "gx", "gy"), PartitionSpec(), PartitionSpec()),
        out_specs=(PartitionSpec("sec", None, "gx", None, "gy"), PartitionSpec("sec", "gx", None, "gy")),
        check_vma=False,
    )
```

```python
import jax
import jax.numpy as jnp
import numpy as np
from jax import lax
from jax.experimental import pallas as pl
from jax.experimental.pallas import tpu as pltpu
from jax.sharding import PartitionSpec

TIME_STEP = 0.05
SMAG_COEFF = 0.1
THRUST_COEFF = 4.0
DRIVING_FORCE = 0.1
FRINGE_BLEND = 0.5
RADIUS = 4
MESH = pl.DeviceIdType.MESH
F32 = jnp.float32


def turned(v, shift):
    return pltpu.roll(v, shift % 128, 1)


def viscosity(xp, xm, yp, ym, zp, zm):
    a = xp[0] - xm[0]
    b = yp[1] - ym[1]
    c = zp[2] - zm[2]
    s1 = (yp[0] - ym[0]) + (xp[1] - xm[1])
    s2 = (zp[0] - zm[0]) + (xp[2] - xm[2])
    s3 = (zp[1] - zm[1]) + (yp[2] - ym[2])
    total = 0.5 * (a * a + b * b + c * c) + 0.25 * (s1 * s1 + s2 * s2 + s3 * s3)
    return SMAG_COEFF * jnp.sqrt(total)


def lanes(rows):
    return lax.broadcasted_iota(jnp.int32, (rows, 128), 1)


def fill_pads(U, N, T3):
    zeros = jnp.zeros((8, 128), F32)

    @pl.loop(0, U.shape[0] * 3)
    def _(i):
        s, c = i // 3, i % 3
        for slot in range(12):
            U[s, c, slot, 0:8, :] = zeros
            U[s, c, slot, 40:48, :] = zeros

    for i in range(10):
        N[i, 0:8, :] = zeros
        N[i, 40:48, :] = zeros
    for c in range(3):
        T3[c, 0:8, :] = zeros
        T3[c, 40:48, :] = zeros


def load_initial(vel, U):
    @pl.loop(0, 24)
    def _(i):
        c, x = i // 8, i % 8
        for zc in range(4):
            U[0, c, x + 2, 8 + 8 * zc : 16 + 8 * zc, :] = vel[pl.ds(c * 256 + zc * 64 + x, 8, stride=8), :]


def find_disks(tur, DW, total_y):
    x_anchor = lax.axis_index("gx") * 8
    y_anchor = lax.axis_index("gy") * 128
    turb = tur.shape[1]
    rows_x = lax.broadcasted_iota(jnp.int32, (8, turb), 0)
    rows_y = lax.broadcasted_iota(jnp.int32, (128, turb), 0)
    match = (tur[0:1, :] == x_anchor + rows_x).astype(F32)
    offset = rows_y + (y_anchor + total_y // 2 + total_y) - tur[1:2, :]
    offset = jnp.where(offset >= total_y, offset - total_y, offset)
    offset = jnp.where(offset >= total_y, offset - total_y, offset) - total_y // 2
    square_y = offset * offset
    height = tur[2:3, :]

    @pl.loop(0, 32)
    def _(z):
        off_z = z - height
        inside = (square_y <= RADIUS * RADIUS - off_z * off_z).astype(F32)
        count = lax.dot_general(match, inside, (((1,), (1,)), ((), ())), preferred_element_type=F32)
        DW[pl.ds(z, 8, stride=32), :] = count


def remote(src, dst, send, recv, axis, index):
    return pltpu.make_async_remote_copy(
        src_ref=src, dst_ref=dst, send_sem=send, recv_sem=recv, device_id={axis: index}, device_id_type=MESH
    )


def pack_edges(U, s, comps):
    lane = lanes(32)
    packed = jnp.zeros((32, 128), F32)
    for c in comps:
        for x in range(8):
            base = c * 32 + x * 4
            packed = jnp.where(lane // 4 == base // 4, turned(U[s, c, x + 2, 8:40, :], base + 2), packed)
    return packed


def side_values(u, hh, lane):
    return (jnp.where(lane == 127, hh, turned(u, -1)), jnp.where(lane == 0, hh, turned(u, 1)))


def strip_viscosity(s, halo, Q, T3, NS):
    lane32 = lanes(32)
    parts = [[] for _ in range(6)]
    for c in range(3):
        t = T3[c, 8:40, :]
        xp, xm = turned(t, -4), turned(t, 4)
        if halo:
            q_minus, q_plus = Q[s, 0], Q[s, 2]
            xp = jnp.where(lane32 == 29, turned(q_plus, 28 - c * 32), xp)
            xp = jnp.where(lane32 == 62, turned(q_plus, 62 - c * 32), xp)
            xm = jnp.where(lane32 == 1, turned(q_minus, -28 - c * 32), xm)
            xm = jnp.where(lane32 == 34, turned(q_minus, 6 - c * 32), xm)
        values = (xp, xm, turned(t, -1), turned(t, 1), T3[c, 9:41, :], T3[c, 7:39, :])
        for part, value in zip(parts, values):
            part.append(value)
    strip = viscosity(*parts)
    NS[...] = jnp.where(lane32 % 4 == 0, turned(strip, -34), strip)


def row_viscosity(s, i, which, column, U, N, Q):
    lane = lanes(8)
    slot = i + 1
    for zc in range(4):
        r = 8 + 8 * zc
        hold = Q[s, which, 8 * zc : 8 * zc + 8, :]
        pieces = [[] for _ in range(6)]
        for c in range(3):
            u = U[s, c, slot, r : r + 8, :]
            hh = pltpu.roll(hold, 127 - c * 32 - column * 4, 1)
            yp, ym = side_values(u, hh, lane)
            values = (
                U[s, c, slot + 1, r : r + 8, :],
                U[s, c, slot - 1, r : r + 8, :],
                yp,
                ym,
                U[s, c, slot, r + 1 : r + 9, :],
                U[s, c, slot, r - 1 : r + 7, :],
            )
            for piece, value in zip(pieces, values):
                piece.append(value)
        N[i, r : r + 8, :] = viscosity(*pieces)


def advance_row(s, x, alpha, beta, U, N, Q, NS, DW):
    lane = lanes(8)
    farm = lax.axis_index("sec").astype(F32)
    slot = x + 2
    for zc in range(4):
        r = 8 + 8 * zc
        n = N[x + 1, r : r + 8, :]
        hold = Q[s, 1, 8 * zc : 8 * zc + 8, :]
        nyp, nym = side_values(n, pltpu.roll(NS[8 * zc : 8 * zc + 8, :], 127 - x * 4, 1), lane)
        around = (
            (n + N[x + 2, r : r + 8, :], n + N[x, r : r + 8, :]),
            (n + nyp, n + nym),
            (n + N[x + 1, r + 1 : r + 9, :], n + N[x + 1, r - 1 : r + 7, :]),
        )
        mids, sides = [], []
        for c in range(3):
            u = U[s, c, slot, r : r + 8, :]
            hh = pltpu.roll(hold, 127 - c * 32 - x * 4, 1)
            mids.append(u)
            sides.append(
                (
                    (U[s, c, slot + 1, r : r + 8, :], U[s, c, slot - 1, r : r + 8, :]),
                    side_values(u, hh, lane),
                    (U[s, c, slot, r + 1 : r + 9, :], U[s, c, slot, r - 1 : r + 7, :]),
                )
            )
        for c in range(3):
            u = mids[c]
            total = None
            for d in range(3):
                up_c, um_c = sides[c][d]
                up_d, um_d = sides[d][d]
                term = around[d][0] * (up_c - u) - around[d][1] * (u - um_c) - (up_d * up_c - um_d * um_c)
                total = term if total is None else total + term
            change = 0.5 * total
            if c == 0:
                weight = DW[pl.ds(x * 32 + 8 * zc, 8), :]
                change = change + (DRIVING_FORCE - (THRUST_COEFF * farm) * weight * u * jnp.abs(u))
            new = u + TIME_STEP * change
            if alpha:
                new = alpha * U[0, c, slot, r : r + 8, :] + beta * new
            U[s + 1, c, slot, r : r + 8, :] = new


def rk_stage(s, alpha, beta, near, U, N, P, Q, T3, NS, DW, send, recv, meanwhile, after):
    left, right, down, up = near
    lane32 = lanes(32)
    to_down = remote(U.at[s, :, 2:4, 8:40, :], U.at[s, :, 10:12, 8:40, :], send.at[s, 0], recv.at[s, 0], "gx", down)
    to_up = remote(U.at[s, :, 8:10, 8:40, :], U.at[s, :, 0:2, 8:40, :], send.at[s, 1], recv.at[s, 1], "gx", up)
    to_left = remote(P.at[s, 0], P.at[s, 2], send.at[s, 2], recv.at[s, 2], "gy", left)
    to_right = remote(P.at[s, 0], P.at[s, 1], send.at[s, 3], recv.at[s, 3], "gy", right)
    q_down = remote(Q.at[s, 1], Q.at[s, 2], send.at[s, 4], recv.at[s, 4], "gx", down)
    q_up = remote(Q.at[s, 1], Q.at[s, 0], send.at[s, 5], recv.at[s, 5], "gx", up)
    to_down.start()
    to_up.start()
    P[s, 0] = pack_edges(U, s, range(3))
    to_left.start()
    to_right.start()
    meanwhile()
    to_left.wait_recv()
    to_right.wait_recv()
    own, from_left, from_right = P[s, 0], P[s, 1], P[s, 2]
    Q[s, 1] = jnp.where(lane32 % 4 == 0, turned(from_right, -2), from_left)
    q_down.start()
    q_up.start()

    strip_left = jnp.where(lane32 % 4 < 2, from_left, own)
    strip_right = jnp.where(lane32 % 4 < 2, own, from_right)
    for c in range(3):
        T3[c, 8:40, :] = jnp.where(lane32 < 32, turned(strip_left, -32 * c), turned(strip_right, 32 - 32 * c))
    strip_viscosity(s, False, Q, T3, NS)

    @pl.loop(2, 8)
    def _(i):
        row_viscosity(s, i, 1, i - 1, U, N, Q)

    @pl.loop(2, 6)
    def _(x):
        advance_row(s, x, alpha, beta, U, N, Q, NS, DW)

    to_down.wait_recv()
    to_up.wait_recv()
    q_down.wait_recv()
    q_up.wait_recv()
    after()
    strip_viscosity(s, True, Q, T3, NS)

    @pl.loop(0, 4)
    def _(j):
        i = j + 6 * (j // 2)
        which = jnp.where(j == 0, 0, jnp.where(j == 3, 2, 1))
        column = jnp.where(j % 3 == 0, 7 * (1 - j // 3), 7 * (j // 2))
        row_viscosity(s, i, which, column, U, N, Q)

    @pl.loop(0, 4)
    def _(j):
        advance_row(s, j + 4 * (j // 2), alpha, beta, U, N, Q, NS, DW)

    for copy in (to_left, to_right, to_down, to_up, q_down, q_up):
        copy.wait_send()


def neighbours(gx_count, gy_count):
    gx, gy = lax.axis_index("gx"), lax.axis_index("gy")
    left = lax.rem(gy + gy_count - 1, gy_count)
    right = lax.rem(gy + 1, gy_count)
    down = lax.rem(gx + gx_count - 1, gx_count)
    up = lax.rem(gx + 1, gx_count)
    return left, right, down, up


STAGES = ((0.0, 1.0), (0.75, 0.25), (1.0 / 3.0, 2.0 / 3.0))


def dht_tables():
    def cas(product, length):
        angle = (product % length).astype(np.float64) * (2.0 * np.pi / length)
        return np.cos(angle) + np.sin(angle)

    b = np.arange(128)[:, None]
    f = np.arange(128)[None, :]
    spanwise = np.zeros((4, 256, 256))
    spanwise[0, :128, :128] = cas(b * (8 * f), 1024)
    spanwise[0, 128:, 128:] = cas(b * (4 + 8 * f), 1024)
    for p in (1, 2, 3):
        low, high = p + 8 * f, 8 - p + 8 * f
        spanwise[p, :128, :128] = cas(b * low, 1024)
        spanwise[p, 128:, :128] = cas(-b * low, 1024)
        spanwise[p, :128, 128:] = cas(b * high, 1024)
        spanwise[p, 128:, 128:] = -cas(-b * high, 1024)
    x = np.arange(256)
    streamwise = cas(x[:, None] * x[None, :], 256)

    def halves(table):
        table = table.astype(np.float32)
        top = table.astype(jnp.bfloat16)
        rest = (table - top.astype(np.float32)).astype(jnp.bfloat16)
        return np.stack([top, rest])

    return halves(spanwise), halves(streamwise)


HALF_ROOT = 0.5**0.5


def halved(v):
    top = v.astype(jnp.bfloat16)
    return top, (v - top.astype(F32)).astype(jnp.bfloat16)


def dot(a, b, dims=((1,), (0,))):
    return lax.dot_general(a, b, (dims, ((), ())), preferred_element_type=F32)


def rows_by_table(v, top, rest, dims):
    rows = v.shape[0]
    v_top, v_rest = halved(v)
    both = dot(jnp.concatenate([v_top, v_rest], axis=0), top, dims)
    return both[:rows] + both[rows:] + dot(v_top, rest, dims)


def table_by_columns(top, rest, v):
    v_top, v_rest = halved(v)
    return dot(top, v_top) + dot(top, v_rest) + dot(rest, v_top)


def swap_blocks(v):
    lane = lanes(8)
    low = lane < 64
    odd = (lane // 32) % 2 == 1
    a, b, c, d = v
    a, c = jnp.where(low, a, turned(c, 64)), jnp.where(low, turned(a, 64), c)
    b, d = jnp.where(low, b, turned(d, 64)), jnp.where(low, turned(b, 64), d)
    a, b = jnp.where(odd, turned(b, 32), a), jnp.where(odd, b, turned(a, -32))
    c, d = jnp.where(odd, turned(d, 32), c), jnp.where(odd, d, turned(c, -32))
    return a, b, c, d


def far_first(i, count):
    step = (i + 1) // 2
    return count // 2 + jnp.where(i % 2 == 0, step, -step)


def find_pivots(INV):
    gx, gy = lax.axis_index("gx"), lax.axis_index("gy")
    lane = lanes(8)
    row = lax.broadcasted_iota(jnp.int32, (8, 128), 0)
    k = gy * 32 + (lane // 32) * 8 + row
    pair = gx // 8
    j = (gx % 8) * 32 + lane % 32
    second = jnp.where(pair == 0, 4, 8 - pair)
    ell = jnp.where(j < 128, pair + 8 * j, second + 8 * (j - 128))
    wave_x = jnp.sin(k.astype(F32) * (jnp.pi / 256))
    wave_y = jnp.sin(ell.astype(F32) * (jnp.pi / 1024))
    eigen = -4.0 * (wave_x * wave_x + wave_y * wave_y)
    inverse = 1.0 / (eigen - 1.0)
    INV[0] = inverse
    for z in range(1, 32):
        inverse = 1.0 / (eigen - (3.0 if z == 31 else 2.0) - inverse)
        INV[z] = inverse


def divergence(near, fringe, U, P, DM, GM, send, recv):
    left, right, down, up = near
    lane32, lane = lanes(32), lanes(8)
    s = 3
    to_down = remote(U.at[s, 0, 2, 8:40, :], U.at[s, 0, 10, 8:40, :], send.at[s, 0], recv.at[s, 0], "gx", down)
    to_up = remote(U.at[s, 0, 9, 8:40, :], U.at[s, 0, 1, 8:40, :], send.at[s, 1], recv.at[s, 1], "gx", up)
    to_left = remote(P.at[s, 0], P.at[s, 2], send.at[s, 2], recv.at[s, 2], "gy", left)
    to_right = remote(P.at[s, 0], P.at[s, 1], send.at[s, 3], recv.at[s, 3], "gy", right)
    to_down.start()
    to_up.start()
    P[s, 0] = pack_edges(U, s, [1])
    to_left.start()
    to_right.start()
    yield
    for copy in (to_left, to_right, to_down, to_up):
        copy.wait_recv()
    P[s, 0 + 3] = jnp.where(lane32 % 4 == 0, turned(P[s, 2], -2), P[s, 1])
    farm = lax.axis_index("sec").astype(F32)
    anchor = lax.axis_index("gx") * 8
    total_x = 8 * lax.axis_size("gx")

    def mask(x):
        column = jnp.full((8, 128), lax.rem(anchor + x + total_x, total_x), jnp.int32)
        return jnp.where((column >= fringe[0]) & (column < fringe[1]), FRINGE_BLEND, 0.0).astype(F32)

    @pl.loop(0, 8)
    def _(x):
        slot = x + 2
        m_here, m_plus, m_minus = mask(x), mask(x + 1), mask(x - 1)
        for zc in range(4):
            r = 8 + 8 * zc
            up_u, um_u = U[s, 0, slot + 1, r : r + 8, :], U[s, 0, slot - 1, r : r + 8, :]
            hh = pltpu.roll(P[s, 3, 8 * zc : 8 * zc + 8, :], 127 - 32 - x * 4, 1)
            yp, ym = side_values(U[s, 1, slot, r : r + 8, :], hh, lane)
            across = 0.5 * ((yp - ym) + (U[s, 2, slot, r + 1 : r + 9, :] - U[s, 2, slot, r - 1 : r + 7, :]))
            whole = 0.5 * (up_u - um_u) + across
            part = 0.5 * (m_plus * up_u - m_minus * um_u) + m_here * across
            DM[pl.ds(zc * 64 + x, 8, stride=8), :] = whole - farm * part
            GM[pl.ds(zc * 64 + x, 8, stride=8), :] = part

    for copy in (to_left, to_right, to_down, to_up):
        copy.wait_send()


def spanwise_forward(R1, WY, XS):
    x = [R1[g] for g in range(8)]
    e = [x[g] + x[g + 4] for g in range(4)]
    o = [x[g] - x[g + 4] for g in range(4)]
    plus, minus = HALF_ROOT * (o[1] + o[3]), HALF_ROOT * (o[1] - o[3])
    sides = (
        (e[0] + e[1] + e[2] + e[3], e[0] - e[1] + e[2] - e[3]),
        (o[0] + minus, plus + o[2]),
        (e[0] - e[2], e[1] - e[3]),
        (o[0] - minus, plus - o[2]),
    )
    for p in range(4):
        line = rows_by_table(jnp.concatenate(sides[p], axis=1), WY[0, p], WY[1, p], ((1,), (0,)))
        for h in range(2):
            tiles = swap_blocks([line[8 * z : 8 * z + 8, 128 * h : 128 * h + 128] for z in range(4)])
            for q in range(4):
                XS[p * 8 + h * 4 + q] = tiles[q]


def solve_levels(R3, INV, SQ):
    levels = []
    for g in range(8):
        levels.extend(swap_blocks([R3[g, 8 * i : 8 * i + 8, :] for i in range(4)]))
    scale = 1.0 / (256 * 1024)
    current = (scale * levels[0]) * INV[0]
    reduced = [current]
    for z in range(1, 32):
        current = (scale * levels[z] - current) * INV[z]
        reduced.append(current)
    solved = [None] * 32
    solved[31] = reduced[31]
    for z in range(30, -1, -1):
        solved[z] = reduced[z] - INV[z] * solved[z + 1]
    for z in range(32):
        above = solved[z + 1] if z < 31 else -solved[31]
        below = solved[z - 1] if z > 0 else solved[0]
        SQ[0, z] = solved[z]
        SQ[1, z] = 0.5 * (above - below)


def spanwise_back(R4, f, WY):
    rows = []
    for p in range(4):
        halves = []
        for h in range(2):
            tiles = swap_blocks([R4[f, p * 8 + h * 4 + q] for q in range(4)])
            halves.append(jnp.concatenate(tiles, axis=0))
        rows.append(rows_by_table(jnp.concatenate(halves, axis=1), WY[0, p], WY[1, p], ((1,), (1,))))
    a = [row[:, :128] for row in rows]
    b = [row[:, 128:] for row in rows]
    total, change = a[0] + b[0], a[0] - b[0]
    t = (total + a[2], change + b[2], total - a[2], change - b[2])
    minus, plus = HALF_ROOT * (a[1] - a[3]), HALF_ROOT * (b[1] + b[3])
    o = (a[1] + a[3], minus + plus, b[1] - b[3], plus - minus)
    return [t[g] + o[g] for g in range(4)] + [t[g] - o[g] for g in range(4)]


def step_kernel(vel_ref, tur, fringe, wy_ref, tx_ref, out_v, out_p, U, N, P, Q, T3, NS, DW, INV, WY, TX, VEL, DM, GM, R1, RG, XS, R2, YS, R3, SQ, R4, F, R5, UZ, RA, BL, PP, send, recv, local, a_send, a_recv, x_send, x_recv, y_send, y_recv, g_send, g_recv, b_send, b_recv, met):
    gx_count, gy_count = lax.axis_size("gx"), lax.axis_size("gy")
    sec, gx, gy = lax.axis_index("sec"), lax.axis_index("gx"), lax.axis_index("gy")
    near = neighbours(gx_count, gy_count)
    barrier = pltpu.get_barrier_semaphore()
    loads = [
        pltpu.make_async_copy(vel_ref, VEL, local.at[0]),
        pltpu.make_async_copy(wy_ref, WY, local.at[1]),
        pltpu.make_async_copy(tx_ref, TX, local.at[2]),
    ]
    for load in loads:
        load.start()

    left, right, down, up = near

    def greet(semaphore, **device):
        pl.semaphore_signal(semaphore, inc=1, device_id=device, device_id_type=MESH)

    greet(barrier, gx=down)
    greet(barrier, gx=up)
    greet(barrier, sec=1 - sec)

    @pl.loop(1, gy_count)
    def _(d):
        greet(barrier, gy=lax.rem(gy + d, gy_count))

    loads[0].wait()
    load_initial(VEL, U)
    pl.semaphore_wait(barrier, gy_count + 2)
    greet(met.at[0], gx=down)
    greet(met.at[0], gx=up)
    greet(met.at[4], sec=1 - sec)

    def prepare():
        fill_pads(U, N, T3)
        find_disks(tur, DW, gy_count * 128)
        find_pivots(INV)

    def spread(s):
        pl.semaphore_wait(met.at[s], 2)
        distance = 2 ** (s + 1)
        greet(met.at[s + 1], gx=lax.rem(gx + distance, gx_count))
        greet(met.at[s + 1], gx=lax.rem(gx + gx_count - distance, gx_count))

    for s, (alpha, beta) in enumerate(STAGES):
        meanwhile = prepare if s == 0 else lambda: None
        rk_stage(s, alpha, beta, near, U, N, P, Q, T3, NS, DW, send, recv, meanwhile, lambda: spread(s))

    work = divergence(near, fringe, U, P, DM, GM, send, recv)
    next(work)

    @pl.loop(0, 24)
    def _(i):
        c, x = i // 8, i % 8
        for zc in range(4):
            UZ[pl.ds(c * 256 + zc * 64 + x, 8, stride=8), :] = U[3, c, x + 2, 8 + 8 * zc : 16 + 8 * zc, :]

    def velocity_copy(c, peer, source):
        return remote(UZ.at[pl.ds(c * 256 + peer * 8, 8), :], RA.at[c, pl.ds(source * 8, 8), :], a_send.at[c, peer], a_recv.at[c, source], "gx", peer)

    def send_velocity(c):
        @pl.loop(0, gx_count - 1)
        def _(i):
            velocity_copy(c, lax.rem(gx + far_first(i, gx_count), gx_count), gx).start()

        RA[c, pl.ds(pl.multiple_of(gx * 8, 8), 8), :] = UZ[pl.ds(pl.multiple_of(c * 256 + gx * 8, 8), 8), :]

    pl.semaphore_wait(met.at[3], 2)
    pl.semaphore_wait(met.at[4], 1)
    send_velocity(0)
    send_velocity(1)
    for _ in work:
        pass

    def group_copy(peer, source):
        return remote(DM.at[pl.ds(peer * 32, 32), :], R1.at[source], y_send.at[0, peer], y_recv.at[0, source], "gy", peer)

    def fringe_copy(peer, source):
        return pltpu.make_async_remote_copy(
            src_ref=GM.at[pl.ds(peer * 32, 32), :],
            dst_ref=RG.at[source],
            send_sem=g_send.at[peer],
            recv_sem=g_recv.at[source],
            device_id={"sec": 1, "gy": peer},
            device_id_type=MESH,
        )

    touches = (gx == 0) | (gx >= 3 * gx_count // 4 - 1)

    @pl.when(touches & (sec == 0))
    def _():
        @pl.loop(0, gy_count)
        def _(peer):
            fringe_copy(peer, gy).start()

    @pl.loop(1, gy_count)
    def _(d):
        group_copy(lax.rem(gy + d, gy_count), gy).start()

    R1[gy] = DM[pl.ds(pl.multiple_of(gy * 32, 32), 32), :]

    @pl.loop(1, gy_count)
    def _(d):
        group_copy(gy, lax.rem(gy + d, gy_count)).wait_recv()

    @pl.when(touches & (sec == 1))
    def _():
        @pl.loop(0, gy_count)
        def _(source):
            fringe_copy(gy, source).wait_recv()

        for g in range(8):
            R1[g] = R1[g] + RG[g]

    loads[1].wait()
    loads[2].wait()
    spanwise_forward(R1, WY, XS)

    def chunk_copy(peer, source):
        return remote(XS.at[peer], R2.at[pl.ds(source * 8, 8), :], x_send.at[0, peer], x_recv.at[0, source], "gx", peer)

    @pl.loop(0, gx_count - 1)
    def _(i):
        chunk_copy(lax.rem(gx + far_first(i, gx_count), gx_count), gx).start()

    R2[pl.ds(pl.multiple_of(gx * 8, 8), 8), :] = XS[gx]

    @pl.loop(1, gx_count)
    def _(d):
        chunk_copy(gx, lax.rem(gx + d, gx_count)).wait_recv()

    YS[...] = table_by_columns(TX[0], TX[1], R2[...])

    def wave_copy(peer, source):
        return remote(YS.at[pl.ds(peer * 32, 32), :], R3.at[source], y_send.at[1, peer], y_recv.at[1, source], "gy", peer)

    @pl.loop(1, gy_count)
    def _(d):
        wave_copy(lax.rem(gy + d, gy_count), gy).start()

    R3[gy] = YS[pl.ds(pl.multiple_of(gy * 32, 32), 32), :]
    send_velocity(2)

    @pl.loop(1, gy_count)
    def _(d):
        wave_copy(gy, lax.rem(gy + d, gy_count)).wait_recv()

    solve_levels(R3, INV, SQ)

    def level_copy(f, peer, source):
        return remote(SQ.at[f, peer], R4.at[f, source], x_send.at[1 + f, peer], x_recv.at[1 + f, source], "gx", peer)

    for f in range(2):

        @pl.loop(0, gx_count - 1)
        def _(i):
            level_copy(f, lax.rem(gx + far_first(i, gx_count), gx_count), gx).start()

        R4[f, gx] = SQ[f, gx]

    def wait_levels(f):
        @pl.loop(1, gx_count)
        def _(d):
            level_copy(f, gx, lax.rem(gx + d, gx_count)).wait_recv()

    @pl.loop(0, 3 * (gx_count - 1))
    def _(i):
        c, d = i // (gx_count - 1), 1 + i % (gx_count - 1)
        velocity_copy(c, gx, lax.rem(gx + d, gx_count)).wait_recv()

    quarter = pltpu.make_async_remote_copy(
        src_ref=RA.at[:, 192:256, :],
        dst_ref=BL,
        send_sem=b_send.at[0],
        recv_sem=b_recv.at[0],
        device_id={"sec": 1},
        device_id_type=MESH,
    )

    @pl.when(sec == 0)
    def _():
        quarter.start()

    wait_levels(0)
    x = spanwise_back(R4, 0, WY)
    lane32 = lanes(32)
    ahead = [turned(v, -1) for v in x]
    behind = [turned(v, 1) for v in x]
    for g in range(8):
        F[g, 0] = x[g]
        plus_y = jnp.where(lane32 == 127, ahead[(g + 1) % 8], ahead[g])
        minus_y = jnp.where(lane32 == 0, behind[(g + 7) % 8], behind[g])
        F[g, 1] = 0.5 * (plus_y - minus_y)

    def plane_copy(peer, source):
        return remote(F.at[peer, 0:2], R5.at[source, 0:2], y_send.at[2, peer], y_recv.at[2, source], "gy", peer)

    def slope_copy(peer, source):
        return remote(F.at[peer, 2], R5.at[source, 2], y_send.at[3, peer], y_recv.at[3, source], "gy", peer)

    @pl.loop(1, gy_count)
    def _(d):
        plane_copy(lax.rem(gy + d, gy_count), gy).start()

    wait_levels(1)
    x = spanwise_back(R4, 1, WY)
    for g in range(8):
        F[g, 2] = x[g]

    @pl.loop(1, gy_count)
    def _(d):
        slope_copy(lax.rem(gy + d, gy_count), gy).start()

    R5[gy] = F[gy]

    @pl.when(sec == 1)
    def _():
        quarter.wait_recv()
        row = lax.broadcasted_iota(jnp.int32, (64, 128), 0) + 192
        weight = jnp.where((row >= fringe[0]) & (row < fringe[1]), FRINGE_BLEND, 0.0).astype(F32)
        for c in range(3):
            mine = RA[c, 192:256, :]
            RA[c, 192:256, :] = mine + weight * (BL[c] - mine)

    @pl.loop(1, gy_count)
    def _(d):
        plane_copy(gy, lax.rem(gy + d, gy_count)).wait_recv()

    def streamwise_back(f):
        return table_by_columns(TX[0], TX[1], jnp.concatenate([R5[g, f] for g in range(8)], axis=0))

    planes = [streamwise_back(0), streamwise_back(1)]
    pressure = planes[0]
    out_p[...] = pressure
    PP[8:264, :] = pressure
    PP[7:8, :] = pressure[255:256]
    PP[264:265, :] = pressure[0:1]
    out_v[0] = RA[0] - 0.5 * (PP[9:265, :] - PP[7:263, :])
    out_v[1] = RA[1] - planes[1]

    @pl.loop(1, gy_count)
    def _(d):
        slope_copy(gy, lax.rem(gy + d, gy_count)).wait_recv()

    out_v[2] = RA[2] - streamwise_back(2)

    @pl.loop(1, gx_count)
    def _(d):
        peer = lax.rem(gx + d, gx_count)
        for c in range(3):
            velocity_copy(c, peer, gx).wait_send()
        chunk_copy(peer, gx).wait_send()
        level_copy(0, peer, gx).wait_send()
        level_copy(1, peer, gx).wait_send()

    @pl.loop(1, gy_count)
    def _(d):
        peer = lax.rem(gy + d, gy_count)
        group_copy(peer, gy).wait_send()
        wave_copy(peer, gy).wait_send()
        plane_copy(peer, gy).wait_send()
        slope_copy(peer, gy).wait_send()

    @pl.when(touches & (sec == 0))
    def _():
        @pl.loop(0, gy_count)
        def _(peer):
            fringe_copy(peer, gy).wait_send()

    @pl.when(sec == 0)
    def _():
        quarter.wait_send()


def on_device(velocity, turbine_cells, fringe_bounds):
    gx_count, gy_count = lax.axis_size("gx"), lax.axis_size("gy")
    spanwise, streamwise = dht_tables()
    vmem = pltpu.VMEM
    dma = pltpu.SemaphoreType.DMA
    scratch = [
        vmem((4, 3, 12, 48, 128), F32),
        vmem((10, 48, 128), F32),
        vmem((4, 4, 32, 128), F32),
        vmem((3, 3, 32, 128), F32),
        vmem((3, 48, 128), F32),
        vmem((32, 128), F32),
        vmem((256, 128), F32),
        vmem((32, 8, 128), F32),
        vmem((2, 4, 256, 256), jnp.bfloat16),
        vmem((2, 256, 256), jnp.bfloat16),
        vmem((768, 128), F32),
        vmem((256, 128), F32),
        vmem((256, 128), F32),
        vmem((8, 32, 128), F32),
        vmem((8, 32, 128), F32),
        vmem((32, 8, 128), F32),
        vmem((256, 128), F32),
        vmem((256, 128), F32),
        vmem((8, 32, 128), F32),
        vmem((2, 32, 8, 128), F32),
        vmem((2, 32, 8, 128), F32),
        vmem((8, 3, 32, 128), F32),
        vmem((8, 3, 32, 128), F32),
        vmem((768, 128), F32),
        vmem((3, 256, 128), F32),
        vmem((3, 64, 128), F32),
        vmem((272, 128), F32),
        dma((4, 6)),
        dma((4, 6)),
        dma((3,)),
        dma((3, gx_count)),
        dma((3, gx_count)),
        dma((3, gx_count)),
        dma((3, gx_count)),
        dma((4, gy_count)),
        dma((4, gy_count)),
        dma((gy_count,)),
        dma((gy_count,)),
        dma((1,)),
        dma((1,)),
        pltpu.SemaphoreType.REGULAR((5,)),
    ]
    anywhere, inside = pl.BlockSpec(memory_space=pltpu.HBM), pl.BlockSpec(memory_space=pltpu.VMEM)
    flat = pl.BlockSpec(memory_space=pltpu.SMEM)
    next_velocity, pressure = pl.pallas_call(
        step_kernel,
        out_shape=(jax.ShapeDtypeStruct((3, 256, 128), F32), jax.ShapeDtypeStruct((256, 128), F32)),
        in_specs=[anywhere, inside, flat, anywhere, anywhere],
        out_specs=(inside, inside),
        scratch_shapes=scratch,
        compiler_params=pltpu.CompilerParams(collective_id=0, has_side_effects=True, vmem_limit_bytes=67043328),
    )(velocity.reshape(768, 128), turbine_cells.T, fringe_bounds, jnp.asarray(spanwise), jnp.asarray(streamwise))
    return (next_velocity.reshape(1, 3, 1, 256, 128), pressure.reshape(1, 1, 256, 128))


def solution(mesh):
    return jax.shard_map(
        on_device,
        mesh=mesh,
        in_specs=(PartitionSpec("sec", None, None, "gx", "gy"), PartitionSpec(), PartitionSpec()),
        out_specs=(PartitionSpec("sec", None, "gx", None, "gy"), PartitionSpec("sec", "gx", None, "gy")),
        check_vma=False,
    )
```

```python
import jax
import jax.numpy as jnp
import numpy as np
from jax import lax
from jax.experimental import pallas as pl
from jax.experimental.pallas import tpu as pltpu
from jax.sharding import PartitionSpec

TIME_STEP = 0.05
SMAG_COEFF = 0.1
THRUST_COEFF = 4.0
DRIVING_FORCE = 0.1
FRINGE_BLEND = 0.5
RADIUS = 4
MESH = pl.DeviceIdType.MESH
F32 = jnp.float32


def turned(v, shift):
    return pltpu.roll(v, shift % 128, 1)


def viscosity(xp, xm, yp, ym, zp, zm):
    a = xp[0] - xm[0]
    b = yp[1] - ym[1]
    c = zp[2] - zm[2]
    s1 = (yp[0] - ym[0]) + (xp[1] - xm[1])
    s2 = (zp[0] - zm[0]) + (xp[2] - xm[2])
    s3 = (zp[1] - zm[1]) + (yp[2] - ym[2])
    total = 0.5 * (a * a + b * b + c * c) + 0.25 * (s1 * s1 + s2 * s2 + s3 * s3)
    return SMAG_COEFF * jnp.sqrt(total)


def lanes(rows):
    return lax.broadcasted_iota(jnp.int32, (rows, 128), 1)


def fill_pads(U, N, T3):
    zeros = jnp.zeros((8, 128), F32)

    @pl.loop(0, U.shape[0] * 3)
    def _(i):
        s, c = i // 3, i % 3
        for slot in range(12):
            U[s, c, slot, 0:8, :] = zeros
            U[s, c, slot, 40:48, :] = zeros

    for i in range(10):
        N[i, 0:8, :] = zeros
        N[i, 40:48, :] = zeros
    for c in range(3):
        T3[c, 0:8, :] = zeros
        T3[c, 40:48, :] = zeros


def load_initial(vel, U):
    @pl.loop(0, 24)
    def _(i):
        c, x = i // 8, i % 8
        for zc in range(4):
            U[0, c, x + 2, 8 + 8 * zc : 16 + 8 * zc, :] = vel[pl.ds(c * 256 + zc * 64 + x, 8, stride=8), :]


def find_disks(tur, DW, total_y):
    x_anchor = lax.axis_index("gx") * 8
    y_anchor = lax.axis_index("gy") * 128
    turb = tur.shape[1]
    twice = jnp.concatenate([tur[...], tur[...]], axis=1)
    rows_x = lax.broadcasted_iota(jnp.int32, (16, 2 * turb), 0)
    upper = lax.broadcasted_iota(jnp.int32, (16, 2 * turb), 1) // turb
    match = (twice[0:1, :] == x_anchor + rows_x % 8) & (upper == rows_x // 8)
    match = match.astype(F32).astype(jnp.bfloat16)
    rows_y = lax.broadcasted_iota(jnp.int32, (128, 2 * turb), 0)
    offset = rows_y + (y_anchor + total_y // 2 + total_y) - twice[1:2, :]
    offset = jnp.where(offset >= total_y, offset - total_y, offset)
    offset = jnp.where(offset >= total_y, offset - total_y, offset) - total_y // 2
    square_y = offset * offset
    level = upper[0:1, :] - twice[2:3, :]

    @pl.loop(0, 16)
    def _(i):
        off_z = 2 * i + level
        inside = (square_y <= RADIUS * RADIUS - off_z * off_z).astype(F32).astype(jnp.bfloat16)
        count = lax.dot_general(match, inside, (((1,), (1,)), ((), ())), preferred_element_type=F32)
        DW[pl.ds(2 * i, 8, stride=32), :] = count[0:8, :]
        DW[pl.ds(2 * i + 1, 8, stride=32), :] = count[8:16, :]


def remote(src, dst, send, recv, axis, index):
    return pltpu.make_async_remote_copy(
        src_ref=src, dst_ref=dst, send_sem=send, recv_sem=recv, device_id={axis: index}, device_id_type=MESH
    )


def pack_edges(U, s, comps):
    lane = lanes(32)
    packed = jnp.zeros((32, 128), F32)
    for c in comps:
        for x in range(8):
            base = c * 32 + x * 4
            packed = jnp.where(lane // 4 == base // 4, turned(U[s, c, x + 2, 8:40, :], base + 2), packed)
    return packed


def side_values(u, hh, lane):
    return (jnp.where(lane == 127, hh, turned(u, -1)), jnp.where(lane == 0, hh, turned(u, 1)))


def strip_viscosity(s, halo, Q, T3, NS):
    lane32 = lanes(32)
    parts = [[] for _ in range(6)]
    for c in range(3):
        t = T3[c, 8:40, :]
        xp, xm = turned(t, -4), turned(t, 4)
        if halo:
            q_minus, q_plus = Q[s, 0], Q[s, 2]
            xp = jnp.where(lane32 == 29, turned(q_plus, 28 - c * 32), xp)
            xp = jnp.where(lane32 == 62, turned(q_plus, 62 - c * 32), xp)
            xm = jnp.where(lane32 == 1, turned(q_minus, -28 - c * 32), xm)
            xm = jnp.where(lane32 == 34, turned(q_minus, 6 - c * 32), xm)
        values = (xp, xm, turned(t, -1), turned(t, 1), T3[c, 9:41, :], T3[c, 7:39, :])
        for part, value in zip(parts, values):
            part.append(value)
    strip = viscosity(*parts)
    NS[...] = jnp.where(lane32 % 4 == 0, turned(strip, -34), strip)


def row_viscosity(s, i, which, column, U, N, Q):
    lane = lanes(8)
    slot = i + 1
    for zc in range(4):
        r = 8 + 8 * zc
        hold = Q[s, which, 8 * zc : 8 * zc + 8, :]
        pieces = [[] for _ in range(6)]
        for c in range(3):
            u = U[s, c, slot, r : r + 8, :]
            hh = pltpu.roll(hold, 127 - c * 32 - column * 4, 1)
            yp, ym = side_values(u, hh, lane)
            values = (
                U[s, c, slot + 1, r : r + 8, :],
                U[s, c, slot - 1, r : r + 8, :],
                yp,
                ym,
                U[s, c, slot, r + 1 : r + 9, :],
                U[s, c, slot, r - 1 : r + 7, :],
            )
            for piece, value in zip(pieces, values):
                piece.append(value)
        N[i, r : r + 8, :] = viscosity(*pieces)


def advance_row(s, x, alpha, beta, U, N, Q, NS, DW):
    lane = lanes(8)
    farm = lax.axis_index("sec").astype(F32)
    slot = x + 2
    for zc in range(4):
        r = 8 + 8 * zc
        n = N[x + 1, r : r + 8, :]
        hold = Q[s, 1, 8 * zc : 8 * zc + 8, :]
        nyp, nym = side_values(n, pltpu.roll(NS[8 * zc : 8 * zc + 8, :], 127 - x * 4, 1), lane)
        around = (
            (n + N[x + 2, r : r + 8, :], n + N[x, r : r + 8, :]),
            (n + nyp, n + nym),
            (n + N[x + 1, r + 1 : r + 9, :], n + N[x + 1, r - 1 : r + 7, :]),
        )
        mids, sides = [], []
        for c in range(3):
            u = U[s, c, slot, r : r + 8, :]
            hh = pltpu.roll(hold, 127 - c * 32 - x * 4, 1)
            mids.append(u)
            sides.append(
                (
                    (U[s, c, slot + 1, r : r + 8, :], U[s, c, slot - 1, r : r + 8, :]),
                    side_values(u, hh, lane),
                    (U[s, c, slot, r + 1 : r + 9, :], U[s, c, slot, r - 1 : r + 7, :]),
                )
            )
        for c in range(3):
            u = mids[c]
            total = None
            for d in range(3):
                up_c, um_c = sides[c][d]
                up_d, um_d = sides[d][d]
                term = around[d][0] * (up_c - u) - around[d][1] * (u - um_c) - (up_d * up_c - um_d * um_c)
                total = term if total is None else total + term
            change = 0.5 * total
            if c == 0:
                weight = DW[pl.ds(x * 32 + 8 * zc, 8), :]
                change = change + (DRIVING_FORCE - (THRUST_COEFF * farm) * weight * u * jnp.abs(u))
            new = u + TIME_STEP * change
            if alpha:
                new = alpha * U[0, c, slot, r : r + 8, :] + beta * new
            U[s + 1, c, slot, r : r + 8, :] = new


def row_copies(s, near, U, send, recv):
    _, _, down, up = near
    if s == 3:
        parts = ((U.at[s, 0, 2, 8:40, :], U.at[s, 0, 10, 8:40, :]), (U.at[s, 0, 9, 8:40, :], U.at[s, 0, 1, 8:40, :]))
    else:
        parts = (
            (U.at[s, :, 2:4, 8:40, :], U.at[s, :, 10:12, 8:40, :]),
            (U.at[s, :, 8:10, 8:40, :], U.at[s, :, 0:2, 8:40, :]),
        )
    return tuple(
        remote(src, dst, send.at[s, i], recv.at[s, i], "gx", device)
        for i, ((src, dst), device) in enumerate(zip(parts, (down, up)))
    )


def rk_stage(s, alpha, beta, near, U, N, P, Q, T3, NS, DW, send, recv, meanwhile, after):
    left, right, down, up = near
    lane32 = lanes(32)
    to_down, to_up = row_copies(s, near, U, send, recv)
    to_left = remote(P.at[s, 0], P.at[s, 2], send.at[s, 2], recv.at[s, 2], "gy", left)
    to_right = remote(P.at[s, 0], P.at[s, 1], send.at[s, 3], recv.at[s, 3], "gy", right)
    q_down = remote(Q.at[s, 1], Q.at[s, 2], send.at[s, 4], recv.at[s, 4], "gx", down)
    q_up = remote(Q.at[s, 1], Q.at[s, 0], send.at[s, 5], recv.at[s, 5], "gx", up)
    if s == 0:
        to_down.start()
        to_up.start()
    P[s, 0] = pack_edges(U, s, range(3))
    to_left.start()
    to_right.start()
    meanwhile()
    to_left.wait_recv()
    to_right.wait_recv()
    own, from_left, from_right = P[s, 0], P[s, 1], P[s, 2]
    Q[s, 1] = jnp.where(lane32 % 4 == 0, turned(from_right, -2), from_left)
    q_down.start()
    q_up.start()

    strip_left = jnp.where(lane32 % 4 < 2, from_left, own)
    strip_right = jnp.where(lane32 % 4 < 2, own, from_right)
    for c in range(3):
        T3[c, 8:40, :] = jnp.where(lane32 < 32, turned(strip_left, -32 * c), turned(strip_right, 32 - 32 * c))
    strip_viscosity(s, False, Q, T3, NS)

    @pl.loop(2, 8)
    def _(i):
        row_viscosity(s, i, 1, i - 1, U, N, Q)

    @pl.loop(2, 6)
    def _(x):
        advance_row(s, x, alpha, beta, U, N, Q, NS, DW)

    to_down.wait_recv()
    to_up.wait_recv()
    q_down.wait_recv()
    q_up.wait_recv()
    after()
    strip_viscosity(s, True, Q, T3, NS)

    @pl.loop(0, 4)
    def _(j):
        i = j + 6 * (j // 2)
        which = jnp.where(j == 0, 0, jnp.where(j == 3, 2, 1))
        column = jnp.where(j % 3 == 0, 7 * (1 - j // 3), 7 * (j // 2))
        row_viscosity(s, i, which, column, U, N, Q)

    next_down, next_up = row_copies(s + 1, near, U, send, recv)

    @pl.loop(0, 2)
    def _(x):
        advance_row(s, x, alpha, beta, U, N, Q, NS, DW)

    next_down.start()

    @pl.loop(6, 8)
    def _(x):
        advance_row(s, x, alpha, beta, U, N, Q, NS, DW)

    next_up.start()

    for copy in (to_left, to_right, to_down, to_up, q_down, q_up):
        copy.wait_send()


def neighbours(gx_count, gy_count):
    gx, gy = lax.axis_index("gx"), lax.axis_index("gy")
    left = lax.rem(gy + gy_count - 1, gy_count)
    right = lax.rem(gy + 1, gy_count)
    down = lax.rem(gx + gx_count - 1, gx_count)
    up = lax.rem(gx + 1, gx_count)
    return left, right, down, up


STAGES = ((0.0, 1.0), (0.75, 0.25), (1.0 / 3.0, 2.0 / 3.0))


def dht_tables():
    def cas(product, length):
        angle = (product % length).astype(np.float64) * (2.0 * np.pi / length)
        return np.cos(angle) + np.sin(angle)

    b = np.arange(128)[:, None]
    f = np.arange(128)[None, :]
    spanwise = np.zeros((4, 256, 256))
    spanwise[0, :128, :128] = cas(b * (8 * f), 1024)
    spanwise[0, 128:, 128:] = cas(b * (4 + 8 * f), 1024)
    for p in (1, 2, 3):
        low, high = p + 8 * f, 8 - p + 8 * f
        spanwise[p, :128, :128] = cas(b * low, 1024)
        spanwise[p, 128:, :128] = cas(-b * low, 1024)
        spanwise[p, :128, 128:] = cas(b * high, 1024)
        spanwise[p, 128:, 128:] = -cas(-b * high, 1024)
    x = np.arange(256)
    streamwise = cas(x[:, None] * x[None, :], 256)

    def halves(table):
        table = table.astype(np.float32)
        top = table.astype(jnp.bfloat16)
        rest = (table - top.astype(np.float32)).astype(jnp.bfloat16)
        return np.stack([top, rest])

    return halves(np.concatenate([spanwise, streamwise[None]]))


HALF_ROOT = 0.5**0.5


def halved(v):
    top = v.astype(jnp.bfloat16)
    return top, (v - top.astype(F32)).astype(jnp.bfloat16)


def dot(a, b, dims=((1,), (0,))):
    return lax.dot_general(a, b, (dims, ((), ())), preferred_element_type=F32)


def rows_by_table(v, top, rest, dims):
    rows = v.shape[0]
    v_top, v_rest = halved(v)
    both = dot(jnp.concatenate([v_top, v_rest], axis=0), top, dims)
    return both[:rows] + both[rows:] + dot(v_top, rest, dims)


def table_by_columns(top, rest, v):
    v_top, v_rest = halved(v)
    return dot(top, v_top) + dot(top, v_rest) + dot(rest, v_top)


def swap_blocks(v):
    lane = lanes(8)
    low = lane < 64
    odd = (lane // 32) % 2 == 1
    a, b, c, d = v
    a, c = jnp.where(low, a, turned(c, 64)), jnp.where(low, turned(a, 64), c)
    b, d = jnp.where(low, b, turned(d, 64)), jnp.where(low, turned(b, 64), d)
    a, b = jnp.where(odd, turned(b, 32), a), jnp.where(odd, b, turned(a, -32))
    c, d = jnp.where(odd, turned(d, 32), c), jnp.where(odd, d, turned(c, -32))
    return a, b, c, d


def wrapped(index, count):
    return index - jnp.where(index >= count, count, 0)


def to_all(start, me, count):
    half = count // 2
    start(wrapped(me + half, count))

    @pl.loop(1, half)
    def _(step):
        start(wrapped(me + (half + step), count))
        start(wrapped(me + (half - step), count))


def find_pivots(INV):
    gx, gy = lax.axis_index("gx"), lax.axis_index("gy")
    lane = lanes(8)
    row = lax.broadcasted_iota(jnp.int32, (8, 128), 0)
    k = gy * 32 + (lane // 32) * 8 + row
    pair = gx // 8
    j = (gx % 8) * 32 + lane % 32
    second = jnp.where(pair == 0, 4, 8 - pair)
    ell = jnp.where(j < 128, pair + 8 * j, second + 8 * (j - 128))
    wave_x = jnp.sin(k.astype(F32) * (jnp.pi / 256))
    wave_y = jnp.sin(ell.astype(F32) * (jnp.pi / 1024))
    eigen = -4.0 * (wave_x * wave_x + wave_y * wave_y)
    inverse = 1.0 / (eigen - 1.0)
    INV[0] = inverse
    for z in range(1, 32):
        inverse = 1.0 / (eigen - (3.0 if z == 31 else 2.0) - inverse)
        INV[z] = inverse


def divergence(near, fringe, U, P, DM, GM, send, recv):
    left, right, down, up = near
    lane32, lane = lanes(32), lanes(8)
    s = 3
    to_down, to_up = row_copies(s, near, U, send, recv)
    to_left = remote(P.at[s, 0], P.at[s, 2], send.at[s, 2], recv.at[s, 2], "gy", left)
    to_right = remote(P.at[s, 0], P.at[s, 1], send.at[s, 3], recv.at[s, 3], "gy", right)
    P[s, 0] = pack_edges(U, s, [1])
    to_left.start()
    to_right.start()
    yield
    for copy in (to_left, to_right, to_down, to_up):
        copy.wait_recv()
    P[s, 0 + 3] = jnp.where(lane32 % 4 == 0, turned(P[s, 2], -2), P[s, 1])
    farm = lax.axis_index("sec").astype(F32)
    anchor = lax.axis_index("gx") * 8
    total_x = 8 * lax.axis_size("gx")

    def mask(x):
        column = jnp.full((8, 128), lax.rem(anchor + x + total_x, total_x), jnp.int32)
        return jnp.where((column >= fringe[0]) & (column < fringe[1]), FRINGE_BLEND, 0.0).astype(F32)

    @pl.loop(0, 8)
    def _(x):
        slot = x + 2
        m_here, m_plus, m_minus = mask(x), mask(x + 1), mask(x - 1)
        for zc in range(4):
            r = 8 + 8 * zc
            up_u, um_u = U[s, 0, slot + 1, r : r + 8, :], U[s, 0, slot - 1, r : r + 8, :]
            hh = pltpu.roll(P[s, 3, 8 * zc : 8 * zc + 8, :], 127 - 32 - x * 4, 1)
            yp, ym = side_values(U[s, 1, slot, r : r + 8, :], hh, lane)
            across = 0.5 * ((yp - ym) + (U[s, 2, slot, r + 1 : r + 9, :] - U[s, 2, slot, r - 1 : r + 7, :]))
            whole = 0.5 * (up_u - um_u) + across
            part = 0.5 * (m_plus * up_u - m_minus * um_u) + m_here * across
            DM[pl.ds(zc * 64 + x, 8, stride=8), :] = whole - farm * part
            GM[pl.ds(zc * 64 + x, 8, stride=8), :] = part

    for copy in (to_left, to_right, to_down, to_up):
        copy.wait_send()


def spanwise_forward(R1, WY, XS):
    x = [R1[g] for g in range(8)]
    e = [x[g] + x[g + 4] for g in range(4)]
    o = [x[g] - x[g + 4] for g in range(4)]
    plus, minus = HALF_ROOT * (o[1] + o[3]), HALF_ROOT * (o[1] - o[3])
    sides = (
        (e[0] + e[1] + e[2] + e[3], e[0] - e[1] + e[2] - e[3]),
        (o[0] + minus, plus + o[2]),
        (e[0] - e[2], e[1] - e[3]),
        (o[0] - minus, plus - o[2]),
    )
    for p in range(4):
        line = rows_by_table(jnp.concatenate(sides[p], axis=1), WY[0, p], WY[1, p], ((1,), (0,)))
        for h in range(2):
            tiles = swap_blocks([line[8 * z : 8 * z + 8, 128 * h : 128 * h + 128] for z in range(4)])
            for q in range(4):
                XS[p * 8 + h * 4 + q] = tiles[q]


def solve_levels(R3, INV, SQ):
    levels = []
    for g in range(8):
        levels.extend(swap_blocks([R3[g, 8 * i : 8 * i + 8, :] for i in range(4)]))
    scale = 1.0 / (256 * 1024)
    current = (scale * levels[0]) * INV[0]
    reduced = [current]
    for z in range(1, 32):
        current = (scale * levels[z] - current) * INV[z]
        reduced.append(current)
    solved = [None] * 32
    solved[31] = reduced[31]
    for z in range(30, -1, -1):
        solved[z] = reduced[z] - INV[z] * solved[z + 1]
    for z in range(32):
        above = solved[z + 1] if z < 31 else -solved[31]
        below = solved[z - 1] if z > 0 else solved[0]
        SQ[0, z] = solved[z]
        SQ[1, z] = 0.5 * (above - below)


def spanwise_back(R4, f, WY):
    rows = []
    for p in range(4):
        halves = []
        for h in range(2):
            tiles = swap_blocks([R4[f, p * 8 + h * 4 + q] for q in range(4)])
            halves.append(jnp.concatenate(tiles, axis=0))
        rows.append(rows_by_table(jnp.concatenate(halves, axis=1), WY[0, p], WY[1, p], ((1,), (1,))))
    a = [row[:, :128] for row in rows]
    b = [row[:, 128:] for row in rows]
    total, change = a[0] + b[0], a[0] - b[0]
    t = (total + a[2], change + b[2], total - a[2], change - b[2])
    minus, plus = HALF_ROOT * (a[1] - a[3]), HALF_ROOT * (b[1] + b[3])
    o = (a[1] + a[3], minus + plus, b[1] - b[3], plus - minus)
    return [t[g] + o[g] for g in range(4)] + [t[g] - o[g] for g in range(4)]


def step_kernel(vel_ref, tur, fringe, wy_ref, out_v, out_p, U, N, P, Q, T3, NS, DW, INV, WY, DM, GM, R1, RG, XS, R2, YS, R3, SQ, R4, F, R5, UZ, RA, BL, PP, send, recv, local, a_send, a_recv, x_send, x_recv, y_send, y_recv, g_send, g_recv, b_send, b_recv, met):
    gx_count, gy_count = lax.axis_size("gx"), lax.axis_size("gy")
    sec, gx, gy = lax.axis_index("sec"), lax.axis_index("gx"), lax.axis_index("gy")
    near = neighbours(gx_count, gy_count)
    barrier = pltpu.get_barrier_semaphore()
    loads = [
        pltpu.make_async_copy(wy_ref, WY, local.at[0]),
    ]
    for load in loads:
        load.start()

    left, right, down, up = near

    def greet(semaphore, **device):
        pl.semaphore_signal(semaphore, inc=1, device_id=device, device_id_type=MESH)

    greet(barrier, gx=down)
    greet(barrier, gx=up)
    greet(barrier, sec=1 - sec)

    @pl.loop(1, gy_count)
    def _(d):
        greet(barrier, gy=wrapped(gy + d, gy_count))

    load_initial(vel_ref, U)
    pl.semaphore_wait(barrier, gy_count + 2)
    greet(met.at[0], gx=down)
    greet(met.at[0], gx=up)
    greet(met.at[4], sec=1 - sec)

    def prepare():
        fill_pads(U, N, T3)
        find_disks(tur, DW, gy_count * 128)

    def spread(s):
        pl.semaphore_wait(met.at[s], 2)
        distance = 2 ** (s + 1)
        greet(met.at[s + 1], gx=lax.rem(gx + distance, gx_count))
        greet(met.at[s + 1], gx=lax.rem(gx + gx_count - distance, gx_count))

    for s, (alpha, beta) in enumerate(STAGES):
        meanwhile = (prepare, lambda: find_pivots(INV), lambda: None)[s]
        rk_stage(s, alpha, beta, near, U, N, P, Q, T3, NS, DW, send, recv, meanwhile, lambda: spread(s))

    work = divergence(near, fringe, U, P, DM, GM, send, recv)
    next(work)
    flat_uz = UZ.reshape(768, 128)

    @pl.loop(0, 24)
    def _(i):
        c, x = i // 8, i % 8
        for zc in range(4):
            flat_uz[pl.ds(c * 256 + zc * 64 + x, 8, stride=8), :] = U[3, c, x + 2, 8 + 8 * zc : 16 + 8 * zc, :]

    groups = ((0, 1), (1, 2), (2, 3))

    def velocity_copy(c, peer, source):
        low, high = groups[c]
        return remote(UZ.at[low:high, peer], RA.at[low:high, source], a_send.at[c, peer], a_recv.at[c, source], "gx", peer)

    def send_velocity(c):
        to_all(lambda peer: velocity_copy(c, peer, gx).start(), gx, gx_count)

        for i in range(*groups[c]):
            RA[i, gx] = UZ[i, gx]

    pl.semaphore_wait(met.at[3], 2)
    pl.semaphore_wait(met.at[4], 1)
    send_velocity(0)
    for _ in work:
        pass

    def group_copy(peer, source):
        return remote(DM.at[pl.ds(peer * 32, 32), :], R1.at[source], y_send.at[0, peer], y_recv.at[0, source], "gy", peer)

    def fringe_copy(peer, source):
        return pltpu.make_async_remote_copy(
            src_ref=GM.at[pl.ds(peer * 32, 32), :],
            dst_ref=RG.at[source],
            send_sem=g_send.at[peer],
            recv_sem=g_recv.at[source],
            device_id={"sec": 1, "gy": peer},
            device_id_type=MESH,
        )

    touches = (gx == 0) | (gx >= 3 * gx_count // 4 - 1)

    @pl.when(touches & (sec == 0))
    def _():
        @pl.loop(0, gy_count)
        def _(peer):
            fringe_copy(peer, gy).start()

    @pl.loop(1, gy_count)
    def _(d):
        group_copy(wrapped(gy + d, gy_count), gy).start()

    R1[gy] = DM[pl.ds(pl.multiple_of(gy * 32, 32), 32), :]

    @pl.loop(1, gy_count)
    def _(d):
        group_copy(gy, wrapped(gy + d, gy_count)).wait_recv()

    @pl.when(touches & (sec == 1))
    def _():
        @pl.loop(0, gy_count)
        def _(source):
            fringe_copy(gy, source).wait_recv()

        for g in range(8):
            R1[g] = R1[g] + RG[g]

    loads[0].wait()
    spanwise_forward(R1, WY, XS)

    def chunk_copy(peer, source):
        return remote(XS.at[peer], R2.at[pl.ds(source * 8, 8), :], x_send.at[0, peer], x_recv.at[0, source], "gx", peer)

    to_all(lambda peer: chunk_copy(peer, gx).start(), gx, gx_count)

    R2[pl.ds(pl.multiple_of(gx * 8, 8), 8), :] = XS[gx]
    send_velocity(1)

    @pl.loop(1, gx_count)
    def _(d):
        chunk_copy(gx, wrapped(gx + d, gx_count)).wait_recv()

    YS[...] = table_by_columns(WY[0, 4], WY[1, 4], R2[...])

    def wave_copy(peer, source):
        return remote(YS.at[pl.ds(peer * 32, 32), :], R3.at[source], y_send.at[1, peer], y_recv.at[1, source], "gy", peer)

    @pl.loop(1, gy_count)
    def _(d):
        wave_copy(wrapped(gy + d, gy_count), gy).start()

    R3[gy] = YS[pl.ds(pl.multiple_of(gy * 32, 32), 32), :]
    send_velocity(2)

    @pl.loop(1, gy_count)
    def _(d):
        wave_copy(gy, wrapped(gy + d, gy_count)).wait_recv()

    solve_levels(R3, INV, SQ)

    def level_copy(f, peer, source):
        return remote(SQ.at[f, peer], R4.at[f, source], x_send.at[1 + f, peer], x_recv.at[1 + f, source], "gx", peer)

    for f in range(2):
        to_all(lambda peer: level_copy(f, peer, gx).start(), gx, gx_count)
        R4[f, gx] = SQ[f, gx]

    def wait_levels(f):
        @pl.loop(1, gx_count)
        def _(d):
            level_copy(f, gx, wrapped(gx + d, gx_count)).wait_recv()


    def wait_velocity(c):
        @pl.loop(1, gx_count)
        def _(d):
            velocity_copy(c, gx, wrapped(gx + d, gx_count)).wait_recv()

    def quarter_copy(c):
        return pltpu.make_async_remote_copy(
            src_ref=RA.at[c, 24:32],
            dst_ref=BL.at[c],
            send_sem=b_send.at[c],
            recv_sem=b_recv.at[c],
            device_id={"sec": 1},
            device_id_type=MESH,
        )

    def offer(c):
        wait_velocity(c)

        @pl.when(sec == 0)
        def _():
            quarter_copy(c).start()

    def blend(c):
        @pl.when(sec == 1)
        def _():
            quarter_copy(c).wait_recv()
            row = lax.broadcasted_iota(jnp.int32, (64, 128), 0) + 192
            weight = jnp.where((row >= fringe[0]) & (row < fringe[1]), FRINGE_BLEND, 0.0).astype(F32)
            mine = RA[c, 24:32].reshape(64, 128)
            theirs = BL[c].reshape(64, 128)
            RA[c, 24:32] = (mine + weight * (theirs - mine)).reshape(8, 8, 128)

    offer(0)
    offer(1)
    wait_levels(0)
    x = spanwise_back(R4, 0, WY)
    lane32 = lanes(32)
    ahead = [turned(v, -1) for v in x]
    behind = [turned(v, 1) for v in x]
    for g in range(8):
        F[g, 0] = x[g]
        plus_y = jnp.where(lane32 == 127, ahead[(g + 1) % 8], ahead[g])
        minus_y = jnp.where(lane32 == 0, behind[(g + 7) % 8], behind[g])
        F[g, 1] = 0.5 * (plus_y - minus_y)

    def plane_copy(peer, source):
        return remote(F.at[peer, 0:2], R5.at[source, 0:2], y_send.at[2, peer], y_recv.at[2, source], "gy", peer)

    def slope_copy(peer, source):
        return remote(F.at[peer, 2], R5.at[source, 2], y_send.at[3, peer], y_recv.at[3, source], "gy", peer)

    @pl.loop(1, gy_count)
    def _(d):
        plane_copy(wrapped(gy + d, gy_count), gy).start()

    wait_levels(1)
    x = spanwise_back(R4, 1, WY)
    for g in range(8):
        F[g, 2] = x[g]

    @pl.loop(1, gy_count)
    def _(d):
        slope_copy(wrapped(gy + d, gy_count), gy).start()

    R5[gy] = F[gy]

    offer(2)
    blend(0)
    blend(1)

    @pl.loop(1, gy_count)
    def _(d):
        plane_copy(gy, wrapped(gy + d, gy_count)).wait_recv()

    def streamwise_back(f):
        return table_by_columns(WY[0, 4], WY[1, 4], jnp.concatenate([R5[g, f] for g in range(8)], axis=0))

    planes = [streamwise_back(0), streamwise_back(1)]
    pressure = planes[0]
    out_p[...] = pressure
    PP[8:264, :] = pressure
    PP[7:8, :] = pressure[255:256]
    PP[264:265, :] = pressure[0:1]
    out_v[0] = RA[0].reshape(256, 128) - 0.5 * (PP[9:265, :] - PP[7:263, :])
    out_v[1] = RA[1].reshape(256, 128) - planes[1]
    blend(2)

    @pl.loop(1, gy_count)
    def _(d):
        slope_copy(gy, wrapped(gy + d, gy_count)).wait_recv()

    out_v[2] = RA[2].reshape(256, 128) - streamwise_back(2)

    @pl.loop(1, gx_count)
    def _(d):
        peer = wrapped(gx + d, gx_count)
        for c in range(3):
            velocity_copy(c, peer, gx).wait_send()
        chunk_copy(peer, gx).wait_send()
        level_copy(0, peer, gx).wait_send()
        level_copy(1, peer, gx).wait_send()

    @pl.loop(1, gy_count)
    def _(d):
        peer = wrapped(gy + d, gy_count)
        group_copy(peer, gy).wait_send()
        wave_copy(peer, gy).wait_send()
        plane_copy(peer, gy).wait_send()
        slope_copy(peer, gy).wait_send()

    @pl.when(touches & (sec == 0))
    def _():
        @pl.loop(0, gy_count)
        def _(peer):
            fringe_copy(peer, gy).wait_send()

    @pl.when(sec == 0)
    def _():
        for c in range(3):
            quarter_copy(c).wait_send()


def on_device(velocity, turbine_cells, fringe_bounds):
    gx_count, gy_count = lax.axis_size("gx"), lax.axis_size("gy")
    vmem = pltpu.VMEM
    dma = pltpu.SemaphoreType.DMA
    scratch = [
        vmem((4, 3, 12, 48, 128), F32),
        vmem((10, 48, 128), F32),
        vmem((4, 4, 32, 128), F32),
        vmem((3, 3, 32, 128), F32),
        vmem((3, 48, 128), F32),
        vmem((32, 128), F32),
        vmem((256, 128), F32),
        vmem((32, 8, 128), F32),
        vmem((2, 5, 256, 256), jnp.bfloat16),
        vmem((256, 128), F32),
        vmem((256, 128), F32),
        vmem((8, 32, 128), F32),
        vmem((8, 32, 128), F32),
        vmem((32, 8, 128), F32),
        vmem((256, 128), F32),
        vmem((256, 128), F32),
        vmem((8, 32, 128), F32),
        vmem((2, 32, 8, 128), F32),
        vmem((2, 32, 8, 128), F32),
        vmem((8, 3, 32, 128), F32),
        vmem((8, 3, 32, 128), F32),
        vmem((3, 32, 8, 128), F32),
        vmem((3, 32, 8, 128), F32),
        vmem((3, 8, 8, 128), F32),
        vmem((272, 128), F32),
        dma((4, 6)),
        dma((4, 6)),
        dma((1,)),
        dma((3, gx_count)),
        dma((3, gx_count)),
        dma((3, gx_count)),
        dma((3, gx_count)),
        dma((4, gy_count)),
        dma((4, gy_count)),
        dma((gy_count,)),
        dma((gy_count,)),
        dma((3,)),
        dma((3,)),
        pltpu.SemaphoreType.REGULAR((5,)),
    ]
    anywhere, inside = pl.BlockSpec(memory_space=pltpu.HBM), pl.BlockSpec(memory_space=pltpu.VMEM)
    flat = pl.BlockSpec(memory_space=pltpu.SMEM)
    next_velocity, pressure = pl.pallas_call(
        step_kernel,
        out_shape=(jax.ShapeDtypeStruct((3, 256, 128), F32), jax.ShapeDtypeStruct((256, 128), F32)),
        in_specs=[inside, inside, flat, anywhere],
        out_specs=(inside, inside),
        scratch_shapes=scratch,
        compiler_params=pltpu.CompilerParams(collective_id=0, has_side_effects=True, vmem_limit_bytes=55000000),
    )(velocity.reshape(768, 128), turbine_cells.T, fringe_bounds, jnp.asarray(dht_tables()))
    return (next_velocity.reshape(1, 3, 1, 256, 128), pressure.reshape(1, 1, 256, 128))


def solution(mesh):
    return jax.shard_map(
        on_device,
        mesh=mesh,
        in_specs=(PartitionSpec("sec", None, None, "gx", "gy"), PartitionSpec(), PartitionSpec()),
        out_specs=(PartitionSpec("sec", None, "gx", None, "gy"), PartitionSpec("sec", "gx", None, "gy")),
        check_vma=False,
    )
```

```python
import jax
import jax.numpy as jnp
import numpy as np
from jax import lax
from jax.experimental import pallas as pl
from jax.experimental.pallas import tpu as pltpu
from jax.sharding import PartitionSpec

TIME_STEP = 0.05
SMAG_COEFF = 0.1
THRUST_COEFF = 4.0
DRIVING_FORCE = 0.1
FRINGE_BLEND = 0.5
RADIUS = 4
MESH = pl.DeviceIdType.MESH
F32 = jnp.float32


def turned(v, shift):
    return pltpu.roll(v, shift % 128, 1)


def viscosity(xp, xm, yp, ym, zp, zm):
    a = xp[0] - xm[0]
    b = yp[1] - ym[1]
    c = zp[2] - zm[2]
    s1 = (yp[0] - ym[0]) + (xp[1] - xm[1])
    s2 = (zp[0] - zm[0]) + (xp[2] - xm[2])
    s3 = (zp[1] - zm[1]) + (yp[2] - ym[2])
    total = 0.5 * (a * a + b * b + c * c) + 0.25 * (s1 * s1 + s2 * s2 + s3 * s3)
    return SMAG_COEFF * jnp.sqrt(total)


def lanes(rows):
    return lax.broadcasted_iota(jnp.int32, (rows, 128), 1)


def fill_pads(U, N, T3):
    zeros = jnp.zeros((8, 128), F32)

    @pl.loop(0, U.shape[0] * 3)
    def _(i):
        s, c = i // 3, i % 3
        for slot in range(12):
            U[s, c, slot, 0:8, :] = zeros
            U[s, c, slot, 40:48, :] = zeros

    for i in range(10):
        N[i, 0:8, :] = zeros
        N[i, 40:48, :] = zeros
    for c in range(3):
        T3[c, 0:8, :] = zeros
        T3[c, 40:48, :] = zeros


def load_rows(vel, U, first, last):
    @pl.loop(first, last)
    def _(x):
        for c in range(3):
            for zc in range(4):
                U[0, c, x + 2, 8 + 8 * zc : 16 + 8 * zc, :] = vel[pl.ds(c * 256 + zc * 64 + x, 8, stride=8), :]


def find_disks(tur, DW, total_y):
    x_anchor = lax.axis_index("gx") * 8
    y_anchor = lax.axis_index("gy") * 128
    turb = tur.shape[1]
    twice = jnp.concatenate([tur[...], tur[...]], axis=1)
    rows_x = lax.broadcasted_iota(jnp.int32, (16, 2 * turb), 0)
    upper = lax.broadcasted_iota(jnp.int32, (16, 2 * turb), 1) // turb
    match = (twice[0:1, :] == x_anchor + rows_x % 8) & (upper == rows_x // 8)
    match = match.astype(F32).astype(jnp.bfloat16)
    rows_y = lax.broadcasted_iota(jnp.int32, (128, 2 * turb), 0)
    offset = rows_y + (y_anchor + total_y // 2 + total_y) - twice[1:2, :]
    offset = jnp.where(offset >= total_y, offset - total_y, offset)
    offset = jnp.where(offset >= total_y, offset - total_y, offset) - total_y // 2
    square_y = offset * offset
    level = upper[0:1, :] - twice[2:3, :]

    @pl.loop(0, 16)
    def _(i):
        off_z = 2 * i + level
        inside = (square_y <= RADIUS * RADIUS - off_z * off_z).astype(F32).astype(jnp.bfloat16)
        count = lax.dot_general(match, inside, (((1,), (1,)), ((), ())), preferred_element_type=F32)
        DW[pl.ds(2 * i, 8, stride=32), :] = count[0:8, :]
        DW[pl.ds(2 * i + 1, 8, stride=32), :] = count[8:16, :]


def remote(src, dst, send, recv, axis, index):
    return pltpu.make_async_remote_copy(
        src_ref=src, dst_ref=dst, send_sem=send, recv_sem=recv, device_id={axis: index}, device_id_type=MESH
    )


def pack_edges(U, s, comps):
    lane = lanes(32)
    packed = jnp.zeros((32, 128), F32)
    for c in comps:
        for x in range(8):
            base = c * 32 + x * 4
            packed = jnp.where(lane // 4 == base // 4, turned(U[s, c, x + 2, 8:40, :], base + 2), packed)
    return packed


def side_values(u, hh, lane):
    return (jnp.where(lane == 127, hh, turned(u, -1)), jnp.where(lane == 0, hh, turned(u, 1)))


def strip_viscosity(s, halo, Q, T3, NS):
    lane32 = lanes(32)
    parts = [[] for _ in range(6)]
    for c in range(3):
        t = T3[c, 8:40, :]
        xp, xm = turned(t, -4), turned(t, 4)
        if halo:
            q_minus, q_plus = Q[s, 0], Q[s, 2]
            xp = jnp.where(lane32 == 29, turned(q_plus, 28 - c * 32), xp)
            xp = jnp.where(lane32 == 62, turned(q_plus, 62 - c * 32), xp)
            xm = jnp.where(lane32 == 1, turned(q_minus, -28 - c * 32), xm)
            xm = jnp.where(lane32 == 34, turned(q_minus, 6 - c * 32), xm)
        values = (xp, xm, turned(t, -1), turned(t, 1), T3[c, 9:41, :], T3[c, 7:39, :])
        for part, value in zip(parts, values):
            part.append(value)
    strip = viscosity(*parts)
    NS[...] = jnp.where(lane32 % 4 == 0, turned(strip, -34), strip)


def row_viscosity(s, i, which, column, U, N, Q):
    lane = lanes(8)
    slot = i + 1
    for zc in range(4):
        r = 8 + 8 * zc
        hold = Q[s, which, 8 * zc : 8 * zc + 8, :]
        pieces = [[] for _ in range(6)]
        for c in range(3):
            u = U[s, c, slot, r : r + 8, :]
            hh = pltpu.roll(hold, 127 - c * 32 - column * 4, 1)
            yp, ym = side_values(u, hh, lane)
            values = (
                U[s, c, slot + 1, r : r + 8, :],
                U[s, c, slot - 1, r : r + 8, :],
                yp,
                ym,
                U[s, c, slot, r + 1 : r + 9, :],
                U[s, c, slot, r - 1 : r + 7, :],
            )
            for piece, value in zip(pieces, values):
                piece.append(value)
        N[i, r : r + 8, :] = viscosity(*pieces)


def advance_row(s, x, alpha, beta, U, N, Q, NS, DW):
    lane = lanes(8)
    farm = lax.axis_index("sec").astype(F32)
    slot = x + 2
    for zc in range(4):
        r = 8 + 8 * zc
        n = N[x + 1, r : r + 8, :]
        hold = Q[s, 1, 8 * zc : 8 * zc + 8, :]
        nyp, nym = side_values(n, pltpu.roll(NS[8 * zc : 8 * zc + 8, :], 127 - x * 4, 1), lane)
        around = (
            (n + N[x + 2, r : r + 8, :], n + N[x, r : r + 8, :]),
            (n + nyp, n + nym),
            (n + N[x + 1, r + 1 : r + 9, :], n + N[x + 1, r - 1 : r + 7, :]),
        )
        mids, sides = [], []
        for c in range(3):
            u = U[s, c, slot, r : r + 8, :]
            hh = pltpu.roll(hold, 127 - c * 32 - x * 4, 1)
            mids.append(u)
            sides.append(
                (
                    (U[s, c, slot + 1, r : r + 8, :], U[s, c, slot - 1, r : r + 8, :]),
                    side_values(u, hh, lane),
                    (U[s, c, slot, r + 1 : r + 9, :], U[s, c, slot, r - 1 : r + 7, :]),
                )
            )
        for c in range(3):
            u = mids[c]
            total = None
            for d in range(3):
                up_c, um_c = sides[c][d]
                up_d, um_d = sides[d][d]
                term = around[d][0] * (up_c - u) - around[d][1] * (u - um_c) - (up_d * up_c - um_d * um_c)
                total = term if total is None else total + term
            change = 0.5 * total
            if c == 0:
                weight = DW[pl.ds(x * 32 + 8 * zc, 8), :]
                change = change + (DRIVING_FORCE - (THRUST_COEFF * farm) * weight * u * jnp.abs(u))
            new = u + TIME_STEP * change
            if alpha:
                new = alpha * U[0, c, slot, r : r + 8, :] + beta * new
            U[s + 1, c, slot, r : r + 8, :] = new


def row_copies(s, near, U, send, recv):
    _, _, down, up = near
    if s == 3:
        parts = ((U.at[s, 0, 2, 8:40, :], U.at[s, 0, 10, 8:40, :]), (U.at[s, 0, 9, 8:40, :], U.at[s, 0, 1, 8:40, :]))
    else:
        parts = (
            (U.at[s, :, 2:4, 8:40, :], U.at[s, :, 10:12, 8:40, :]),
            (U.at[s, :, 8:10, 8:40, :], U.at[s, :, 0:2, 8:40, :]),
        )
    return tuple(
        remote(src, dst, send.at[s, i], recv.at[s, i], "gx", device)
        for i, ((src, dst), device) in enumerate(zip(parts, (down, up)))
    )


def rk_stage(s, alpha, beta, near, U, N, P, Q, T3, NS, DW, send, recv, early, meanwhile, after):
    left, right, down, up = near
    lane32 = lanes(32)
    to_down, to_up = row_copies(s, near, U, send, recv)
    to_left = remote(P.at[s, 0], P.at[s, 2], send.at[s, 2], recv.at[s, 2], "gy", left)
    to_right = remote(P.at[s, 0], P.at[s, 1], send.at[s, 3], recv.at[s, 3], "gy", right)
    q_down = remote(Q.at[s, 1], Q.at[s, 2], send.at[s, 4], recv.at[s, 4], "gx", down)
    q_up = remote(Q.at[s, 1], Q.at[s, 0], send.at[s, 5], recv.at[s, 5], "gx", up)
    P[s, 0] = pack_edges(U, s, range(3))
    to_left.start()
    to_right.start()
    early()
    to_left.wait_recv()
    to_right.wait_recv()
    own, from_left, from_right = P[s, 0], P[s, 1], P[s, 2]
    Q[s, 1] = jnp.where(lane32 % 4 == 0, turned(from_right, -2), from_left)
    q_down.start()
    q_up.start()
    meanwhile()

    strip_left = jnp.where(lane32 % 4 < 2, from_left, own)
    strip_right = jnp.where(lane32 % 4 < 2, own, from_right)
    for c in range(3):
        T3[c, 8:40, :] = jnp.where(lane32 < 32, turned(strip_left, -32 * c), turned(strip_right, 32 - 32 * c))
    strip_viscosity(s, False, Q, T3, NS)

    @pl.loop(2, 8)
    def _(i):
        row_viscosity(s, i, 1, i - 1, U, N, Q)

    @pl.loop(2, 6)
    def _(x):
        advance_row(s, x, alpha, beta, U, N, Q, NS, DW)

    to_down.wait_recv()
    to_up.wait_recv()
    q_down.wait_recv()
    q_up.wait_recv()
    after()
    strip_viscosity(s, True, Q, T3, NS)

    @pl.loop(0, 4)
    def _(j):
        i = j + 6 * (j // 2)
        which = jnp.where(j == 0, 0, jnp.where(j == 3, 2, 1))
        column = jnp.where(j % 3 == 0, 7 * (1 - j // 3), 7 * (j // 2))
        row_viscosity(s, i, which, column, U, N, Q)

    next_down, next_up = row_copies(s + 1, near, U, send, recv)

    @pl.loop(0, 2)
    def _(x):
        advance_row(s, x, alpha, beta, U, N, Q, NS, DW)

    next_down.start()

    @pl.loop(6, 8)
    def _(x):
        advance_row(s, x, alpha, beta, U, N, Q, NS, DW)

    next_up.start()

    for copy in (to_left, to_right, to_down, to_up, q_down, q_up):
        copy.wait_send()


def neighbours(gx_count, gy_count):
    gx, gy = lax.axis_index("gx"), lax.axis_index("gy")
    left = lax.rem(gy + gy_count - 1, gy_count)
    right = lax.rem(gy + 1, gy_count)
    down = lax.rem(gx + gx_count - 1, gx_count)
    up = lax.rem(gx + 1, gx_count)
    return left, right, down, up


STAGES = ((0.0, 1.0), (0.75, 0.25), (1.0 / 3.0, 2.0 / 3.0))


def dht_tables():
    def cas(product, length):
        angle = (product % length).astype(np.float64) * (2.0 * np.pi / length)
        return np.cos(angle) + np.sin(angle)

    b = np.arange(128)[:, None]
    f = np.arange(128)[None, :]
    spanwise = np.zeros((4, 256, 256))
    spanwise[0, :128, :128] = cas(b * (8 * f), 1024)
    spanwise[0, 128:, 128:] = cas(b * (4 + 8 * f), 1024)
    for p in (1, 2, 3):
        low, high = p + 8 * f, 8 - p + 8 * f
        spanwise[p, :128, :128] = cas(b * low, 1024)
        spanwise[p, 128:, :128] = cas(-b * low, 1024)
        spanwise[p, :128, 128:] = cas(b * high, 1024)
        spanwise[p, 128:, 128:] = -cas(-b * high, 1024)
    x = np.arange(256)
    streamwise = cas(x[:, None] * x[None, :], 256)

    def halves(table):
        table = table.astype(np.float32)
        top = table.astype(jnp.bfloat16)
        rest = (table - top.astype(np.float32)).astype(jnp.bfloat16)
        return np.stack([top, rest])

    return halves(np.concatenate([spanwise, streamwise[None]]))


HALF_ROOT = 0.5**0.5


def halved(v):
    top = v.astype(jnp.bfloat16)
    return top, (v - top.astype(F32)).astype(jnp.bfloat16)


def dot(a, b, dims=((1,), (0,))):
    return lax.dot_general(a, b, (dims, ((), ())), preferred_element_type=F32)


def rows_by_table(v, top, rest, dims):
    rows = v.shape[0]
    v_top, v_rest = halved(v)
    both = dot(jnp.concatenate([v_top, v_rest], axis=0), top, dims)
    return both[:rows] + both[rows:] + dot(v_top, rest, dims)


def table_by_columns(top, rest, v):
    v_top, v_rest = halved(v)
    return dot(top, v_top) + dot(top, v_rest) + dot(rest, v_top)


def swap_blocks(v):
    lane = lanes(8)
    low = lane < 64
    odd = (lane // 32) % 2 == 1
    a, b, c, d = v
    a, c = jnp.where(low, a, turned(c, 64)), jnp.where(low, turned(a, 64), c)
    b, d = jnp.where(low, b, turned(d, 64)), jnp.where(low, turned(b, 64), d)
    a, b = jnp.where(odd, turned(b, 32), a), jnp.where(odd, b, turned(a, -32))
    c, d = jnp.where(odd, turned(d, 32), c), jnp.where(odd, d, turned(c, -32))
    return a, b, c, d


def wrapped(index, count):
    return index - jnp.where(index >= count, count, 0)


def all_of(ref, semaphore):
    pltpu.make_async_copy(ref, ref, semaphore).wait()


def to_all(start, me, count):
    half = count // 2
    start(wrapped(me + half, count))

    @pl.loop(1, half)
    def _(step):
        start(wrapped(me + (half + step), count))
        start(wrapped(me + (half - step), count))


def find_pivots(INV):
    gx, gy = lax.axis_index("gx"), lax.axis_index("gy")
    lane = lanes(8)
    row = lax.broadcasted_iota(jnp.int32, (8, 128), 0)
    k = gy * 32 + (lane // 32) * 8 + row
    pair = gx // 8
    j = (gx % 8) * 32 + lane % 32
    second = jnp.where(pair == 0, 4, 8 - pair)
    ell = jnp.where(j < 128, pair + 8 * j, second + 8 * (j - 128))
    wave_x = jnp.sin(k.astype(F32) * (jnp.pi / 256))
    wave_y = jnp.sin(ell.astype(F32) * (jnp.pi / 1024))
    eigen = -4.0 * (wave_x * wave_x + wave_y * wave_y)
    inverse = 1.0 / (eigen - 1.0)
    INV[0] = inverse
    for z in range(1, 32):
        inverse = 1.0 / (eigen - (3.0 if z == 31 else 2.0) - inverse)
        INV[z] = inverse


def divergence(near, fringe, U, P, DM, GM, send, recv):
    left, right, down, up = near
    lane32, lane = lanes(32), lanes(8)
    s = 3
    to_down, to_up = row_copies(s, near, U, send, recv)
    to_left = remote(P.at[s, 0], P.at[s, 2], send.at[s, 2], recv.at[s, 2], "gy", left)
    to_right = remote(P.at[s, 0], P.at[s, 1], send.at[s, 3], recv.at[s, 3], "gy", right)
    P[s, 0] = pack_edges(U, s, [1])
    to_left.start()
    to_right.start()
    yield
    for copy in (to_left, to_right, to_down, to_up):
        copy.wait_recv()
    P[s, 0 + 3] = jnp.where(lane32 % 4 == 0, turned(P[s, 2], -2), P[s, 1])
    farm = lax.axis_index("sec").astype(F32)
    anchor = lax.axis_index("gx") * 8
    total_x = 8 * lax.axis_size("gx")

    def mask(x):
        column = jnp.full((8, 128), lax.rem(anchor + x + total_x, total_x), jnp.int32)
        return jnp.where((column >= fringe[0]) & (column < fringe[1]), FRINGE_BLEND, 0.0).astype(F32)

    @pl.loop(0, 8)
    def _(x):
        slot = x + 2
        m_here, m_plus, m_minus = mask(x), mask(x + 1), mask(x - 1)
        for zc in range(4):
            r = 8 + 8 * zc
            up_u, um_u = U[s, 0, slot + 1, r : r + 8, :], U[s, 0, slot - 1, r : r + 8, :]
            hh = pltpu.roll(P[s, 3, 8 * zc : 8 * zc + 8, :], 127 - 32 - x * 4, 1)
            yp, ym = side_values(U[s, 1, slot, r : r + 8, :], hh, lane)
            across = 0.5 * ((yp - ym) + (U[s, 2, slot, r + 1 : r + 9, :] - U[s, 2, slot, r - 1 : r + 7, :]))
            whole = 0.5 * (up_u - um_u) + across
            part = 0.5 * (m_plus * up_u - m_minus * um_u) + m_here * across
            DM[pl.ds(zc * 64 + x, 8, stride=8), :] = whole - farm * part
            GM[pl.ds(zc * 64 + x, 8, stride=8), :] = part

    for copy in (to_left, to_right, to_down, to_up):
        copy.wait_send()


def spanwise_forward(R1, WY, XS):
    x = [R1[g] for g in range(8)]
    e = [x[g] + x[g + 4] for g in range(4)]
    o = [x[g] - x[g + 4] for g in range(4)]
    plus, minus = HALF_ROOT * (o[1] + o[3]), HALF_ROOT * (o[1] - o[3])
    sides = (
        (e[0] + e[1] + e[2] + e[3], e[0] - e[1] + e[2] - e[3]),
        (o[0] + minus, plus + o[2]),
        (e[0] - e[2], e[1] - e[3]),
        (o[0] - minus, plus - o[2]),
    )
    for p in range(4):
        line = rows_by_table(jnp.concatenate(sides[p], axis=1), WY[0, p], WY[1, p], ((1,), (0,)))
        for h in range(2):
            tiles = swap_blocks([line[8 * z : 8 * z + 8, 128 * h : 128 * h + 128] for z in range(4)])
            for q in range(4):
                XS[p * 8 + h * 4 + q] = tiles[q]


def solve_levels(R3, INV, SQ):
    levels = []
    for g in range(8):
        levels.extend(swap_blocks([R3[g, 8 * i : 8 * i + 8, :] for i in range(4)]))
    scale = 1.0 / (256 * 1024)
    current = (scale * levels[0]) * INV[0]
    reduced = [current]
    for z in range(1, 32):
        current = (scale * levels[z] - current) * INV[z]
        reduced.append(current)
    solved = [None] * 32
    solved[31] = reduced[31]
    for z in range(30, -1, -1):
        solved[z] = reduced[z] - INV[z] * solved[z + 1]
    for z in range(32):
        above = solved[z + 1] if z < 31 else -solved[31]
        below = solved[z - 1] if z > 0 else solved[0]
        SQ[0, z] = solved[z]
        SQ[1, z] = 0.5 * (above - below)


def spanwise_back(R4, f, WY):
    rows = []
    for p in range(4):
        halves = []
        for h in range(2):
            tiles = swap_blocks([R4[f, p * 8 + h * 4 + q] for q in range(4)])
            halves.append(jnp.concatenate(tiles, axis=0))
        rows.append(rows_by_table(jnp.concatenate(halves, axis=1), WY[0, p], WY[1, p], ((1,), (1,))))
    a = [row[:, :128] for row in rows]
    b = [row[:, 128:] for row in rows]
    total, change = a[0] + b[0], a[0] - b[0]
    t = (total + a[2], change + b[2], total - a[2], change - b[2])
    minus, plus = HALF_ROOT * (a[1] - a[3]), HALF_ROOT * (b[1] + b[3])
    o = (a[1] + a[3], minus + plus, b[1] - b[3], plus - minus)
    return [t[g] + o[g] for g in range(4)] + [t[g] - o[g] for g in range(4)]


def step_kernel(vel_ref, tur, fringe, wy_ref, out_v, out_p, U, N, P, Q, T3, NS, DW, INV, WY, DM, GM, R1, RG, XS, R2, YS, R3, SQ, R4, F, R5, UZ, RA, BL, PP, send, recv, local, a_send, a_recv, x_send, x_recv, y_send, y_recv, g_send, g_recv, b_send, b_recv, met):
    gx_count, gy_count = lax.axis_size("gx"), lax.axis_size("gy")
    sec, gx, gy = lax.axis_index("sec"), lax.axis_index("gx"), lax.axis_index("gy")
    near = neighbours(gx_count, gy_count)
    barrier = pltpu.get_barrier_semaphore()
    loads = [
        pltpu.make_async_copy(wy_ref, WY, local.at[0]),
    ]
    for load in loads:
        load.start()

    left, right, down, up = near

    def greet(semaphore, **device):
        pl.semaphore_signal(semaphore, inc=1, device_id=device, device_id_type=MESH)

    greet(barrier, gx=down)
    greet(barrier, gx=up)
    greet(barrier, sec=1 - sec)

    @pl.loop(1, gy_count)
    def _(d):
        greet(barrier, gy=wrapped(gy + d, gy_count))

    load_rows(vel_ref, U, 0, 2)
    load_rows(vel_ref, U, 6, 8)
    pl.semaphore_wait(barrier, gy_count + 2)
    for copy in row_copies(0, near, U, send, recv):
        copy.start()
    load_rows(vel_ref, U, 2, 6)
    early = lambda: fill_pads(U, N, T3)
    greet(met.at[0], gx=down)
    greet(met.at[0], gx=up)
    greet(met.at[4], sec=1 - sec)

    def prepare():
        find_disks(tur, DW, gy_count * 128)

    def spread(s):
        pl.semaphore_wait(met.at[s], 2)
        distance = 2 ** (s + 1)
        greet(met.at[s + 1], gx=lax.rem(gx + distance, gx_count))
        greet(met.at[s + 1], gx=lax.rem(gx + gx_count - distance, gx_count))

    for s, (alpha, beta) in enumerate(STAGES):
        meanwhile = (prepare, lambda: find_pivots(INV), lambda: None)[s]
        rk_stage(s, alpha, beta, near, U, N, P, Q, T3, NS, DW, send, recv, early, meanwhile, lambda: spread(s))
        early = lambda: None

    work = divergence(near, fringe, U, P, DM, GM, send, recv)
    next(work)
    flat_uz = UZ.reshape(768, 128)

    @pl.loop(0, 8)
    def _(x):
        for c in range(3):
            for zc in range(4):
                flat_uz[pl.ds(c * 256 + zc * 64 + x, 8, stride=8), :] = U[3, c, x + 2, 8 + 8 * zc : 16 + 8 * zc, :]

    groups = ((0, 1), (1, 2), (2, 3))

    def velocity_copy(c, peer, source):
        low, high = groups[c]
        return remote(UZ.at[low:high, peer], RA.at[low:high, source], a_send.at[c], a_recv.at[c], "gx", peer)

    def send_velocity(c):
        to_all(lambda peer: velocity_copy(c, peer, gx).start(), gx, gx_count)

        for i in range(*groups[c]):
            RA[i, gx] = UZ[i, gx]

    pl.semaphore_wait(met.at[3], 2)
    pl.semaphore_wait(met.at[4], 1)
    send_velocity(0)
    for _ in work:
        pass

    def group_copy(peer, source):
        return remote(DM.at[pl.ds(peer * 32, 32), :], R1.at[source], y_send.at[0], y_recv.at[0], "gy", peer)

    def fringe_copy(peer, source):
        return pltpu.make_async_remote_copy(
            src_ref=GM.at[pl.ds(peer * 32, 32), :],
            dst_ref=RG.at[source],
            send_sem=g_send.at[peer],
            recv_sem=g_recv.at[source],
            device_id={"sec": 1, "gy": peer},
            device_id_type=MESH,
        )

    touches = (gx == 0) | (gx >= 3 * gx_count // 4 - 1)

    @pl.when(touches & (sec == 0))
    def _():
        @pl.loop(0, gy_count)
        def _(peer):
            fringe_copy(peer, gy).start()

    @pl.loop(1, gy_count)
    def _(d):
        group_copy(wrapped(gy + d, gy_count), gy).start()

    R1[gy] = DM[pl.ds(pl.multiple_of(gy * 32, 32), 32), :]

    all_of(R1.at[0 : gy_count - 1], y_recv.at[0])

    @pl.when(touches & (sec == 1))
    def _():
        @pl.loop(0, gy_count)
        def _(source):
            fringe_copy(gy, source).wait_recv()

        for g in range(8):
            R1[g] = R1[g] + RG[g]

    loads[0].wait()
    spanwise_forward(R1, WY, XS)

    def chunk_copy(peer, source):
        return remote(XS.at[peer], R2.at[pl.ds(source * 8, 8), :], x_send.at[0], x_recv.at[0], "gx", peer)

    to_all(lambda peer: chunk_copy(peer, gx).start(), gx, gx_count)

    R2[pl.ds(pl.multiple_of(gx * 8, 8), 8), :] = XS[gx]
    send_velocity(1)

    all_of(XS.at[0 : gx_count - 1], x_recv.at[0])

    YS[...] = table_by_columns(WY[0, 4], WY[1, 4], R2[...])

    def wave_copy(peer, source):
        return remote(YS.at[pl.ds(peer * 32, 32), :], R3.at[source], y_send.at[1], y_recv.at[1], "gy", peer)

    @pl.loop(1, gy_count)
    def _(d):
        wave_copy(wrapped(gy + d, gy_count), gy).start()

    R3[gy] = YS[pl.ds(pl.multiple_of(gy * 32, 32), 32), :]
    send_velocity(2)

    all_of(R3.at[0 : gy_count - 1], y_recv.at[1])

    solve_levels(R3, INV, SQ)

    def level_copy(f, peer, source):
        return remote(SQ.at[f, peer], R4.at[f, source], x_send.at[1 + f], x_recv.at[1 + f], "gx", peer)

    for f in range(2):
        to_all(lambda peer: level_copy(f, peer, gx).start(), gx, gx_count)
        R4[f, gx] = SQ[f, gx]

    def wait_levels(f):
        all_of(R4.at[f, 0 : gx_count - 1], x_recv.at[1 + f])


    def wait_velocity(c):
        all_of(RA.at[c, 0 : gx_count - 1], a_recv.at[c])

    def quarter_copy(c):
        return pltpu.make_async_remote_copy(
            src_ref=RA.at[c, 24:32],
            dst_ref=BL.at[c],
            send_sem=b_send.at[c],
            recv_sem=b_recv.at[c],
            device_id={"sec": 1},
            device_id_type=MESH,
        )

    def offer(c):
        wait_velocity(c)

        @pl.when(sec == 0)
        def _():
            quarter_copy(c).start()

    def blend(c):
        @pl.when(sec == 1)
        def _():
            quarter_copy(c).wait_recv()
            row = lax.broadcasted_iota(jnp.int32, (64, 128), 0) + 192
            weight = jnp.where((row >= fringe[0]) & (row < fringe[1]), FRINGE_BLEND, 0.0).astype(F32)
            mine = RA[c, 24:32].reshape(64, 128)
            theirs = BL[c].reshape(64, 128)
            RA[c, 24:32] = (mine + weight * (theirs - mine)).reshape(8, 8, 128)

    offer(0)
    offer(1)
    offer(2)
    wait_levels(0)
    x = spanwise_back(R4, 0, WY)
    lane32 = lanes(32)
    ahead = [turned(v, -1) for v in x]
    behind = [turned(v, 1) for v in x]
    for g in range(8):
        F[g, 0] = x[g]
        plus_y = jnp.where(lane32 == 127, ahead[(g + 1) % 8], ahead[g])
        minus_y = jnp.where(lane32 == 0, behind[(g + 7) % 8], behind[g])
        F[g, 1] = 0.5 * (plus_y - minus_y)

    def plane_copy(peer, source):
        return remote(F.at[peer, 0:2], R5.at[source, 0:2], y_send.at[2], y_recv.at[2], "gy", peer)

    def slope_copy(peer, source):
        return remote(F.at[peer, 2], R5.at[source, 2], y_send.at[3], y_recv.at[3], "gy", peer)

    @pl.loop(1, gy_count)
    def _(d):
        plane_copy(wrapped(gy + d, gy_count), gy).start()

    wait_levels(1)
    x = spanwise_back(R4, 1, WY)
    for g in range(8):
        F[g, 2] = x[g]

    @pl.loop(1, gy_count)
    def _(d):
        slope_copy(wrapped(gy + d, gy_count), gy).start()

    R5[gy] = F[gy]

    blend(0)
    blend(1)

    for c in range(3):
        all_of(RA.at[c, 0 : gx_count - 1], a_send.at[c])
    for k in range(3):
        all_of(XS.at[0 : gx_count - 1], x_send.at[k])
    for k in range(2):
        all_of(R1.at[0 : gy_count - 1], y_send.at[k])

    @pl.when(touches & (sec == 0))
    def _():
        @pl.loop(0, gy_count)
        def _(peer):
            fringe_copy(peer, gy).wait_send()


    all_of(R5.at[0 : gy_count - 1, 0:2], y_recv.at[2])

    def streamwise_back(f):
        return table_by_columns(WY[0, 4], WY[1, 4], jnp.concatenate([R5[g, f] for g in range(8)], axis=0))

    planes = [streamwise_back(0), streamwise_back(1)]
    pressure = planes[0]
    out_p[...] = pressure
    PP[8:264, :] = pressure
    PP[7:8, :] = pressure[255:256]
    PP[264:265, :] = pressure[0:1]
    out_v[0] = RA[0].reshape(256, 128) - 0.5 * (PP[9:265, :] - PP[7:263, :])
    out_v[1] = RA[1].reshape(256, 128) - planes[1]
    blend(2)

    all_of(R5.at[0 : gy_count - 1, 2], y_recv.at[3])

    out_v[2] = RA[2].reshape(256, 128) - streamwise_back(2)

    all_of(R5.at[0 : gy_count - 1, 0:2], y_send.at[2])
    all_of(R1.at[0 : gy_count - 1], y_send.at[3])

    @pl.when(sec == 0)
    def _():
        for c in range(3):
            quarter_copy(c).wait_send()


def on_device(velocity, turbine_cells, fringe_bounds):
    gx_count, gy_count = lax.axis_size("gx"), lax.axis_size("gy")
    vmem = pltpu.VMEM
    dma = pltpu.SemaphoreType.DMA
    scratch = [
        vmem((4, 3, 12, 48, 128), F32),
        vmem((10, 48, 128), F32),
        vmem((4, 4, 32, 128), F32),
        vmem((3, 3, 32, 128), F32),
        vmem((3, 48, 128), F32),
        vmem((32, 128), F32),
        vmem((256, 128), F32),
        vmem((32, 8, 128), F32),
        vmem((2, 5, 256, 256), jnp.bfloat16),
        vmem((256, 128), F32),
        vmem((256, 128), F32),
        vmem((8, 32, 128), F32),
        vmem((8, 32, 128), F32),
        vmem((32, 8, 128), F32),
        vmem((256, 128), F32),
        vmem((256, 128), F32),
        vmem((8, 32, 128), F32),
        vmem((2, 32, 8, 128), F32),
        vmem((2, 32, 8, 128), F32),
        vmem((8, 3, 32, 128), F32),
        vmem((8, 3, 32, 128), F32),
        vmem((3, 32, 8, 128), F32),
        vmem((3, 32, 8, 128), F32),
        vmem((3, 8, 8, 128), F32),
        vmem((272, 128), F32),
        dma((4, 6)),
        dma((4, 6)),
        dma((1,)),
        dma((3,)),
        dma((3,)),
        dma((3,)),
        dma((3,)),
        dma((4,)),
        dma((4,)),
        dma((gy_count,)),
        dma((gy_count,)),
        dma((3,)),
        dma((3,)),
        pltpu.SemaphoreType.REGULAR((5,)),
    ]
    anywhere, inside = pl.BlockSpec(memory_space=pltpu.HBM), pl.BlockSpec(memory_space=pltpu.VMEM)
    flat = pl.BlockSpec(memory_space=pltpu.SMEM)
    next_velocity, pressure = pl.pallas_call(
        step_kernel,
        out_shape=(jax.ShapeDtypeStruct((3, 256, 128), F32), jax.ShapeDtypeStruct((256, 128), F32)),
        in_specs=[inside, inside, flat, anywhere],
        out_specs=(inside, inside),
        scratch_shapes=scratch,
        compiler_params=pltpu.CompilerParams(collective_id=0, has_side_effects=True, vmem_limit_bytes=55000000),
    )(velocity.reshape(768, 128), turbine_cells.T, fringe_bounds, jnp.asarray(dht_tables()))
    return (next_velocity.reshape(1, 3, 1, 256, 128), pressure.reshape(1, 1, 256, 128))


def solution(mesh):
    return jax.shard_map(
        on_device,
        mesh=mesh,
        in_specs=(PartitionSpec("sec", None, None, "gx", "gy"), PartitionSpec(), PartitionSpec()),
        out_specs=(PartitionSpec("sec", None, "gx", None, "gy"), PartitionSpec("sec", "gx", None, "gy")),
        check_vma=False,
    )
```

```python
import jax
import jax.numpy as jnp
import numpy as np
from jax import lax
from jax.experimental import pallas as pl
from jax.experimental.pallas import tpu as pltpu
from jax.sharding import PartitionSpec

TIME_STEP = 0.05
SMAG_COEFF = 0.1
THRUST_COEFF = 4.0
DRIVING_FORCE = 0.1
FRINGE_BLEND = 0.5
RADIUS = 4
MESH = pl.DeviceIdType.MESH
F32 = jnp.float32


def turned(v, shift):
    return pltpu.roll(v, shift % 128, 1)


def viscosity(xp, xm, yp, ym, zp, zm):
    a = xp[0] - xm[0]
    b = yp[1] - ym[1]
    c = zp[2] - zm[2]
    s1 = (yp[0] - ym[0]) + (xp[1] - xm[1])
    s2 = (zp[0] - zm[0]) + (xp[2] - xm[2])
    s3 = (zp[1] - zm[1]) + (yp[2] - ym[2])
    total = 0.5 * (a * a + b * b + c * c) + 0.25 * (s1 * s1 + s2 * s2 + s3 * s3)
    return SMAG_COEFF * jnp.sqrt(total)


def lanes(rows):
    return lax.broadcasted_iota(jnp.int32, (rows, 128), 1)


def fill_pads(U, N, T3):
    zeros = jnp.zeros((8, 128), F32)

    @pl.loop(0, U.shape[0] * 3)
    def _(i):
        s, c = i // 3, i % 3
        for slot in range(12):
            U[s, c, slot, 0:8, :] = zeros
            U[s, c, slot, 40:48, :] = zeros

    for i in range(10):
        N[i, 0:8, :] = zeros
        N[i, 40:48, :] = zeros
    for c in range(3):
        T3[c, 0:8, :] = zeros
        T3[c, 40:48, :] = zeros


def load_rows(vel, U, first, last):
    @pl.loop(first, last)
    def _(x):
        for c in range(3):
            for zc in range(4):
                U[0, c, x + 2, 8 + 8 * zc : 16 + 8 * zc, :] = vel[pl.ds(c * 256 + zc * 64 + x, 8, stride=8), :]


def find_disks(tur, DW, total_y):
    x_anchor = lax.axis_index("gx") * 8
    y_anchor = lax.axis_index("gy") * 128
    turb = tur.shape[1]
    twice = jnp.concatenate([tur[...], tur[...]], axis=1)
    rows_x = lax.broadcasted_iota(jnp.int32, (16, 2 * turb), 0)
    upper = lax.broadcasted_iota(jnp.int32, (16, 2 * turb), 1) // turb
    match = (twice[0:1, :] == x_anchor + rows_x % 8) & (upper == rows_x // 8)
    match = match.astype(F32).astype(jnp.bfloat16)
    rows_y = lax.broadcasted_iota(jnp.int32, (128, 2 * turb), 0)
    offset = rows_y + (y_anchor + total_y // 2 + total_y) - twice[1:2, :]
    offset = jnp.where(offset >= total_y, offset - total_y, offset)
    offset = jnp.where(offset >= total_y, offset - total_y, offset) - total_y // 2
    square_y = offset * offset
    level = upper[0:1, :] - twice[2:3, :]

    @pl.loop(0, 16)
    def _(i):
        off_z = 2 * i + level
        inside = (square_y <= RADIUS * RADIUS - off_z * off_z).astype(F32).astype(jnp.bfloat16)
        count = lax.dot_general(match, inside, (((1,), (1,)), ((), ())), preferred_element_type=F32)
        DW[pl.ds(2 * i, 8, stride=32), :] = count[0:8, :]
        DW[pl.ds(2 * i + 1, 8, stride=32), :] = count[8:16, :]


def remote(src, dst, send, recv, axis, index):
    return pltpu.make_async_remote_copy(
        src_ref=src, dst_ref=dst, send_sem=send, recv_sem=recv, device_id={axis: index}, device_id_type=MESH
    )


def pack_edges(U, s, comps):
    lane = lanes(32)
    packed = jnp.zeros((32, 128), F32)
    for c in comps:
        for x in range(8):
            base = c * 32 + x * 4
            packed = jnp.where(lane // 4 == base // 4, turned(U[s, c, x + 2, 8:40, :], base + 2), packed)
    return packed


def side_values(u, hh, lane):
    return (jnp.where(lane == 127, hh, turned(u, -1)), jnp.where(lane == 0, hh, turned(u, 1)))


def strip_viscosity(s, halo, Q, T3, NS):
    lane32 = lanes(32)
    parts = [[] for _ in range(6)]
    for c in range(3):
        t = T3[c, 8:40, :]
        xp, xm = turned(t, -4), turned(t, 4)
        if halo:
            q_minus, q_plus = Q[s, 0], Q[s, 2]
            xp = jnp.where(lane32 == 29, turned(q_plus, 28 - c * 32), xp)
            xp = jnp.where(lane32 == 62, turned(q_plus, 62 - c * 32), xp)
            xm = jnp.where(lane32 == 1, turned(q_minus, -28 - c * 32), xm)
            xm = jnp.where(lane32 == 34, turned(q_minus, 6 - c * 32), xm)
        values = (xp, xm, turned(t, -1), turned(t, 1), T3[c, 9:41, :], T3[c, 7:39, :])
        for part, value in zip(parts, values):
            part.append(value)
    strip = viscosity(*parts)
    NS[...] = jnp.where(lane32 % 4 == 0, turned(strip, -34), strip)


def row_viscosity(s, i, which, column, U, N, Q):
    lane = lanes(8)
    slot = i + 1
    for zc in range(4):
        r = 8 + 8 * zc
        hold = Q[s, which, 8 * zc : 8 * zc + 8, :]
        pieces = [[] for _ in range(6)]
        for c in range(3):
            u = U[s, c, slot, r : r + 8, :]
            hh = pltpu.roll(hold, 127 - c * 32 - column * 4, 1)
            yp, ym = side_values(u, hh, lane)
            values = (
                U[s, c, slot + 1, r : r + 8, :],
                U[s, c, slot - 1, r : r + 8, :],
                yp,
                ym,
                U[s, c, slot, r + 1 : r + 9, :],
                U[s, c, slot, r - 1 : r + 7, :],
            )
            for piece, value in zip(pieces, values):
                piece.append(value)
        N[i, r : r + 8, :] = viscosity(*pieces)


def advance_row(s, x, alpha, beta, U, N, Q, NS, DW):
    lane = lanes(8)
    farm = lax.axis_index("sec").astype(F32)
    slot = x + 2
    for zc in range(4):
        r = 8 + 8 * zc
        n = N[x + 1, r : r + 8, :]
        hold = Q[s, 1, 8 * zc : 8 * zc + 8, :]
        nyp, nym = side_values(n, pltpu.roll(NS[8 * zc : 8 * zc + 8, :], 127 - x * 4, 1), lane)
        around = (
            (n + N[x + 2, r : r + 8, :], n + N[x, r : r + 8, :]),
            (n + nyp, n + nym),
            (n + N[x + 1, r + 1 : r + 9, :], n + N[x + 1, r - 1 : r + 7, :]),
        )
        mids, sides = [], []
        for c in range(3):
            u = U[s, c, slot, r : r + 8, :]
            hh = pltpu.roll(hold, 127 - c * 32 - x * 4, 1)
            mids.append(u)
            sides.append(
                (
                    (U[s, c, slot + 1, r : r + 8, :], U[s, c, slot - 1, r : r + 8, :]),
                    side_values(u, hh, lane),
                    (U[s, c, slot, r + 1 : r + 9, :], U[s, c, slot, r - 1 : r + 7, :]),
                )
            )
        for c in range(3):
            u = mids[c]
            total = None
            for d in range(3):
                up_c, um_c = sides[c][d]
                up_d, um_d = sides[d][d]
                term = around[d][0] * (up_c - u) - around[d][1] * (u - um_c) - (up_d * up_c - um_d * um_c)
                total = term if total is None else total + term
            change = 0.5 * total
            if c == 0:
                weight = DW[pl.ds(x * 32 + 8 * zc, 8), :]
                change = change + (DRIVING_FORCE - (THRUST_COEFF * farm) * weight * u * jnp.abs(u))
            new = u + TIME_STEP * change
            if alpha:
                new = alpha * U[0, c, slot, r : r + 8, :] + beta * new
            U[s + 1, c, slot, r : r + 8, :] = new


def row_copies(s, near, U, send, recv):
    _, _, down, up = near
    if s == 3:
        parts = ((U.at[s, 0, 2, 8:40, :], U.at[s, 0, 10, 8:40, :]), (U.at[s, 0, 9, 8:40, :], U.at[s, 0, 1, 8:40, :]))
    else:
        parts = (
            (U.at[s, :, 2:4, 8:40, :], U.at[s, :, 10:12, 8:40, :]),
            (U.at[s, :, 8:10, 8:40, :], U.at[s, :, 0:2, 8:40, :]),
        )
    return tuple(
        remote(src, dst, send.at[s, i], recv.at[s, i], "gx", device)
        for i, ((src, dst), device) in enumerate(zip(parts, (down, up)))
    )


def rk_stage(s, alpha, beta, near, U, N, P, Q, T3, NS, DW, send, recv, early, meanwhile, after):
    left, right, down, up = near
    lane32 = lanes(32)
    to_down, to_up = row_copies(s, near, U, send, recv)
    to_left = remote(P.at[s, 0], P.at[s, 2], send.at[s, 2], recv.at[s, 2], "gy", left)
    to_right = remote(P.at[s, 0], P.at[s, 1], send.at[s, 3], recv.at[s, 3], "gy", right)
    q_down = remote(Q.at[s, 1], Q.at[s, 2], send.at[s, 4], recv.at[s, 4], "gx", down)
    q_up = remote(Q.at[s, 1], Q.at[s, 0], send.at[s, 5], recv.at[s, 5], "gx", up)
    P[s, 0] = pack_edges(U, s, range(3))
    to_left.start()
    to_right.start()
    early()
    to_left.wait_recv()
    to_right.wait_recv()
    own, from_left, from_right = P[s, 0], P[s, 1], P[s, 2]
    Q[s, 1] = jnp.where(lane32 % 4 == 0, turned(from_right, -2), from_left)
    q_down.start()
    q_up.start()
    meanwhile()

    strip_left = jnp.where(lane32 % 4 < 2, from_left, own)
    strip_right = jnp.where(lane32 % 4 < 2, own, from_right)
    for c in range(3):
        T3[c, 8:40, :] = jnp.where(lane32 < 32, turned(strip_left, -32 * c), turned(strip_right, 32 - 32 * c))
    strip_viscosity(s, False, Q, T3, NS)

    @pl.loop(2, 8)
    def _(i):
        row_viscosity(s, i, 1, i - 1, U, N, Q)

    @pl.loop(2, 6)
    def _(x):
        advance_row(s, x, alpha, beta, U, N, Q, NS, DW)

    to_down.wait_recv()
    to_up.wait_recv()
    q_down.wait_recv()
    q_up.wait_recv()
    after()
    strip_viscosity(s, True, Q, T3, NS)

    @pl.loop(0, 4)
    def _(j):
        i = j + 6 * (j // 2)
        which = jnp.where(j == 0, 0, jnp.where(j == 3, 2, 1))
        column = jnp.where(j % 3 == 0, 7 * (1 - j // 3), 7 * (j // 2))
        row_viscosity(s, i, which, column, U, N, Q)

    next_down, next_up = row_copies(s + 1, near, U, send, recv)

    @pl.loop(0, 2)
    def _(x):
        advance_row(s, x, alpha, beta, U, N, Q, NS, DW)

    next_down.start()

    @pl.loop(6, 8)
    def _(x):
        advance_row(s, x, alpha, beta, U, N, Q, NS, DW)

    next_up.start()

    for copy in (to_left, to_right, to_down, to_up, q_down, q_up):
        copy.wait_send()


def neighbours(gx_count, gy_count):
    gx, gy = lax.axis_index("gx"), lax.axis_index("gy")
    left = lax.rem(gy + gy_count - 1, gy_count)
    right = lax.rem(gy + 1, gy_count)
    down = lax.rem(gx + gx_count - 1, gx_count)
    up = lax.rem(gx + 1, gx_count)
    return left, right, down, up


STAGES = ((0.0, 1.0), (0.75, 0.25), (1.0 / 3.0, 2.0 / 3.0))


def dht_tables():
    def cas(product, length):
        angle = (product % length).astype(np.float64) * (2.0 * np.pi / length)
        return np.cos(angle) + np.sin(angle)

    b = np.arange(128)[:, None]
    f = np.arange(128)[None, :]
    spanwise = np.zeros((4, 256, 256))
    spanwise[0, :128, :128] = cas(b * (8 * f), 1024)
    spanwise[0, 128:, 128:] = cas(b * (4 + 8 * f), 1024)
    for p in (1, 2, 3):
        low, high = p + 8 * f, 8 - p + 8 * f
        spanwise[p, :128, :128] = cas(b * low, 1024)
        spanwise[p, 128:, :128] = cas(-b * low, 1024)
        spanwise[p, :128, 128:] = cas(b * high, 1024)
        spanwise[p, 128:, 128:] = -cas(-b * high, 1024)
    x = np.arange(256)
    streamwise = cas(x[:, None] * x[None, :], 256)

    def halves(table):
        table = table.astype(np.float32)
        top = table.astype(jnp.bfloat16)
        rest = (table - top.astype(np.float32)).astype(jnp.bfloat16)
        return np.stack([top, rest])

    return halves(np.concatenate([spanwise, streamwise[None]]))


HALF_ROOT = 0.5**0.5


def halved(v):
    top = v.astype(jnp.bfloat16)
    return top, (v - top.astype(F32)).astype(jnp.bfloat16)


def dot(a, b, dims=((1,), (0,))):
    return lax.dot_general(a, b, (dims, ((), ())), preferred_element_type=F32)


def rows_by_table(v, top, rest, dims):
    rows = v.shape[0]
    v_top, v_rest = halved(v)
    both = dot(jnp.concatenate([v_top, v_rest], axis=0), top, dims)
    return both[:rows] + both[rows:] + dot(v_top, rest, dims)


def table_by_columns(top, rest, v):
    v_top, v_rest = halved(v)
    return dot(top, v_top) + dot(top, v_rest) + dot(rest, v_top)


def swap_blocks(v):
    lane = lanes(8)
    low = lane < 64
    odd = (lane // 32) % 2 == 1
    a, b, c, d = v
    a, c = jnp.where(low, a, turned(c, 64)), jnp.where(low, turned(a, 64), c)
    b, d = jnp.where(low, b, turned(d, 64)), jnp.where(low, turned(b, 64), d)
    a, b = jnp.where(odd, turned(b, 32), a), jnp.where(odd, b, turned(a, -32))
    c, d = jnp.where(odd, turned(d, 32), c), jnp.where(odd, d, turned(c, -32))
    return a, b, c, d


def wrapped(index, count):
    return index - jnp.where(index >= count, count, 0)


def all_of(ref, semaphore):
    pltpu.make_async_copy(ref, ref, semaphore).wait()


def to_all(start, me, count):
    half = count // 2
    start(wrapped(me + half, count))

    @pl.loop(1, half)
    def _(step):
        start(wrapped(me + (half + step), count))
        start(wrapped(me + (half - step), count))


def find_pivots(INV):
    gx, gy = lax.axis_index("gx"), lax.axis_index("gy")
    lane = lanes(8)
    row = lax.broadcasted_iota(jnp.int32, (8, 128), 0)
    k = gy * 32 + (lane // 32) * 8 + row
    pair = gx // 8
    j = (gx % 8) * 32 + lane % 32
    second = jnp.where(pair == 0, 4, 8 - pair)
    ell = jnp.where(j < 128, pair + 8 * j, second + 8 * (j - 128))
    wave_x = jnp.sin(k.astype(F32) * (jnp.pi / 256))
    wave_y = jnp.sin(ell.astype(F32) * (jnp.pi / 1024))
    eigen = -4.0 * (wave_x * wave_x + wave_y * wave_y)
    inverse = 1.0 / (eigen - 1.0)
    INV[0] = inverse
    for z in range(1, 32):
        inverse = 1.0 / (eigen - (3.0 if z == 31 else 2.0) - inverse)
        INV[z] = inverse


def divergence(near, fringe, U, P, DM, GM, send, recv):
    left, right, down, up = near
    lane32, lane = lanes(32), lanes(8)
    s = 3
    to_down, to_up = row_copies(s, near, U, send, recv)
    to_left = remote(P.at[s, 0], P.at[s, 2], send.at[s, 2], recv.at[s, 2], "gy", left)
    to_right = remote(P.at[s, 0], P.at[s, 1], send.at[s, 3], recv.at[s, 3], "gy", right)
    P[s, 0] = pack_edges(U, s, [1])
    to_left.start()
    to_right.start()
    yield
    for copy in (to_left, to_right, to_down, to_up):
        copy.wait_recv()
    P[s, 0 + 3] = jnp.where(lane32 % 4 == 0, turned(P[s, 2], -2), P[s, 1])
    farm = lax.axis_index("sec").astype(F32)
    anchor = lax.axis_index("gx") * 8
    total_x = 8 * lax.axis_size("gx")

    def mask(x):
        column = jnp.full((8, 128), lax.rem(anchor + x + total_x, total_x), jnp.int32)
        return jnp.where((column >= fringe[0]) & (column < fringe[1]), FRINGE_BLEND, 0.0).astype(F32)

    @pl.loop(0, 8)
    def _(x):
        slot = x + 2
        m_here, m_plus, m_minus = mask(x), mask(x + 1), mask(x - 1)
        for zc in range(4):
            r = 8 + 8 * zc
            up_u, um_u = U[s, 0, slot + 1, r : r + 8, :], U[s, 0, slot - 1, r : r + 8, :]
            hh = pltpu.roll(P[s, 3, 8 * zc : 8 * zc + 8, :], 127 - 32 - x * 4, 1)
            yp, ym = side_values(U[s, 1, slot, r : r + 8, :], hh, lane)
            across = 0.5 * ((yp - ym) + (U[s, 2, slot, r + 1 : r + 9, :] - U[s, 2, slot, r - 1 : r + 7, :]))
            whole = 0.5 * (up_u - um_u) + across
            part = 0.5 * (m_plus * up_u - m_minus * um_u) + m_here * across
            DM[pl.ds(zc * 64 + x, 8, stride=8), :] = whole - farm * part
            GM[pl.ds(zc * 64 + x, 8, stride=8), :] = part

    for copy in (to_left, to_right, to_down, to_up):
        copy.wait_send()


def spanwise_forward(R1, WY, XS):
    x = [R1[g] for g in range(8)]
    e = [x[g] + x[g + 4] for g in range(4)]
    o = [x[g] - x[g + 4] for g in range(4)]
    plus, minus = HALF_ROOT * (o[1] + o[3]), HALF_ROOT * (o[1] - o[3])
    sides = (
        (e[0] + e[1] + e[2] + e[3], e[0] - e[1] + e[2] - e[3]),
        (o[0] + minus, plus + o[2]),
        (e[0] - e[2], e[1] - e[3]),
        (o[0] - minus, plus - o[2]),
    )
    for p in range(4):
        line = rows_by_table(jnp.concatenate(sides[p], axis=1), WY[0, p], WY[1, p], ((1,), (0,)))
        for h in range(2):
            tiles = swap_blocks([line[8 * z : 8 * z + 8, 128 * h : 128 * h + 128] for z in range(4)])
            for q in range(4):
                XS[p * 8 + h * 4 + q] = tiles[q]


def solve_levels(R3, INV, SQ):
    levels = []
    for g in range(8):
        levels.extend(swap_blocks([R3[g, 8 * i : 8 * i + 8, :] for i in range(4)]))
    scale = 1.0 / (256 * 1024)
    current = (scale * levels[0]) * INV[0]
    reduced = [current]
    for z in range(1, 32):
        current = (scale * levels[z] - current) * INV[z]
        reduced.append(current)
    solved = [None] * 32
    solved[31] = reduced[31]
    for z in range(30, -1, -1):
        solved[z] = reduced[z] - INV[z] * solved[z + 1]
    for z in range(32):
        above = solved[z + 1] if z < 31 else -solved[31]
        below = solved[z - 1] if z > 0 else solved[0]
        SQ[0, z] = solved[z]
        SQ[1, z] = 0.5 * (above - below)


def spanwise_back(R4, f, WY):
    rows = []
    for p in range(4):
        halves = []
        for h in range(2):
            tiles = swap_blocks([R4[f, p * 8 + h * 4 + q] for q in range(4)])
            halves.append(jnp.concatenate(tiles, axis=0))
        rows.append(rows_by_table(jnp.concatenate(halves, axis=1), WY[0, p], WY[1, p], ((1,), (1,))))
    a = [row[:, :128] for row in rows]
    b = [row[:, 128:] for row in rows]
    total, change = a[0] + b[0], a[0] - b[0]
    t = (total + a[2], change + b[2], total - a[2], change - b[2])
    minus, plus = HALF_ROOT * (a[1] - a[3]), HALF_ROOT * (b[1] + b[3])
    o = (a[1] + a[3], minus + plus, b[1] - b[3], plus - minus)
    return [t[g] + o[g] for g in range(4)] + [t[g] - o[g] for g in range(4)]


def step_kernel(vel_hbm, tur_hbm, fringe_hbm, wy_ref, out_v, out_p, U, N, P, Q, T3, NS, DW, INV, WY, DM, GM, R1, RG, XS, R2, YS, R3, SQ, R4, F, R5, UZ, RA, BL, PP, send, recv, local, a_send, a_recv, x_send, x_recv, y_send, y_recv, g_send, g_recv, b_send, b_recv, met, vel_ref, tur, fringe):
    gx_count, gy_count = lax.axis_size("gx"), lax.axis_size("gy")
    sec, gx, gy = lax.axis_index("sec"), lax.axis_index("gx"), lax.axis_index("gy")
    near = neighbours(gx_count, gy_count)
    barrier = pltpu.get_barrier_semaphore()
    loads = [
        pltpu.make_async_copy(wy_ref, WY, local.at[0]),
        pltpu.make_async_copy(tur_hbm, tur, local.at[1]),
        pltpu.make_async_copy(fringe_hbm, fringe, local.at[2]),
        pltpu.make_async_copy(vel_hbm, vel_ref, local.at[3]),
    ]
    loads[3].start()

    left, right, down, up = near

    def greet(semaphore, **device):
        pl.semaphore_signal(semaphore, inc=1, device_id=device, device_id_type=MESH)

    greet(barrier, gx=down)
    greet(barrier, gx=up)
    greet(barrier, sec=1 - sec)

    @pl.loop(1, gy_count)
    def _(d):
        greet(barrier, gy=wrapped(gy + d, gy_count))

    loads[3].wait()
    load_rows(vel_ref, U, 0, 2)
    load_rows(vel_ref, U, 6, 8)
    pl.semaphore_wait(barrier, gy_count + 2)
    for copy in row_copies(0, near, U, send, recv):
        copy.start()
    for load in loads[:3]:
        load.start()
    load_rows(vel_ref, U, 2, 6)
    early = lambda: fill_pads(U, N, T3)
    greet(met.at[0], gx=down)
    greet(met.at[0], gx=up)
    greet(met.at[4], sec=1 - sec)

    def prepare():
        loads[1].wait()
        loads[2].wait()
        find_disks(tur, DW, gy_count * 128)

    def spread(s):
        pl.semaphore_wait(met.at[s], 2)
        distance = 2 ** (s + 1)
        greet(met.at[s + 1], gx=lax.rem(gx + distance, gx_count))
        greet(met.at[s + 1], gx=lax.rem(gx + gx_count - distance, gx_count))

    for s, (alpha, beta) in enumerate(STAGES):
        meanwhile = (prepare, lambda: find_pivots(INV), lambda: None)[s]
        rk_stage(s, alpha, beta, near, U, N, P, Q, T3, NS, DW, send, recv, early, meanwhile, lambda: spread(s))
        early = lambda: None

    work = divergence(near, fringe, U, P, DM, GM, send, recv)
    next(work)
    flat_uz = UZ.reshape(768, 128)

    @pl.loop(0, 8)
    def _(x):
        for c in range(3):
            for zc in range(4):
                flat_uz[pl.ds(c * 256 + zc * 64 + x, 8, stride=8), :] = U[3, c, x + 2, 8 + 8 * zc : 16 + 8 * zc, :]

    groups = ((0, 1), (1, 2), (2, 3))

    def velocity_copy(c, peer, source):
        low, high = groups[c]
        return remote(UZ.at[low:high, peer], RA.at[low:high, source], a_send.at[c], a_recv.at[c], "gx", peer)

    def send_velocity(c):
        to_all(lambda peer: velocity_copy(c, peer, gx).start(), gx, gx_count)

        for i in range(*groups[c]):
            RA[i, gx] = UZ[i, gx]

    pl.semaphore_wait(met.at[3], 2)
    pl.semaphore_wait(met.at[4], 1)
    send_velocity(0)
    for _ in work:
        pass

    def group_copy(peer, source):
        return remote(DM.at[pl.ds(peer * 32, 32), :], R1.at[source], y_send.at[0], y_recv.at[0], "gy", peer)

    def fringe_copy(peer, source):
        return pltpu.make_async_remote_copy(
            src_ref=GM.at[pl.ds(peer * 32, 32), :],
            dst_ref=RG.at[source],
            send_sem=g_send.at[peer],
            recv_sem=g_recv.at[source],
            device_id={"sec": 1, "gy": peer},
            device_id_type=MESH,
        )

    touches = (gx == 0) | (gx >= 3 * gx_count // 4 - 1)

    @pl.when(touches & (sec == 0))
    def _():
        @pl.loop(0, gy_count)
        def _(peer):
            fringe_copy(peer, gy).start()

    to_all(lambda peer: group_copy(peer, gy).start(), gy, gy_count)

    R1[gy] = DM[pl.ds(pl.multiple_of(gy * 32, 32), 32), :]

    all_of(R1.at[0 : gy_count - 1], y_recv.at[0])

    @pl.when(touches & (sec == 1))
    def _():
        @pl.loop(0, gy_count)
        def _(source):
            fringe_copy(gy, source).wait_recv()

        for g in range(8):
            R1[g] = R1[g] + RG[g]

    loads[0].wait()
    spanwise_forward(R1, WY, XS)

    def chunk_copy(peer, source):
        return remote(XS.at[peer], R2.at[pl.ds(source * 8, 8), :], x_send.at[0], x_recv.at[0], "gx", peer)

    to_all(lambda peer: chunk_copy(peer, gx).start(), gx, gx_count)

    R2[pl.ds(pl.multiple_of(gx * 8, 8), 8), :] = XS[gx]
    send_velocity(1)

    all_of(XS.at[0 : gx_count - 1], x_recv.at[0])

    YS[...] = table_by_columns(WY[0, 4], WY[1, 4], R2[...])

    def wave_copy(peer, source):
        return remote(YS.at[pl.ds(peer * 32, 32), :], R3.at[source], y_send.at[1], y_recv.at[1], "gy", peer)

    to_all(lambda peer: wave_copy(peer, gy).start(), gy, gy_count)

    R3[gy] = YS[pl.ds(pl.multiple_of(gy * 32, 32), 32), :]
    send_velocity(2)

    all_of(R3.at[0 : gy_count - 1], y_recv.at[1])

    solve_levels(R3, INV, SQ)

    def level_copy(f, peer, source):
        return remote(SQ.at[f, peer], R4.at[f, source], x_send.at[1 + f], x_recv.at[1 + f], "gx", peer)

    for f in range(2):
        to_all(lambda peer: level_copy(f, peer, gx).start(), gx, gx_count)
        R4[f, gx] = SQ[f, gx]

    def wait_levels(f):
        all_of(R4.at[f, 0 : gx_count - 1], x_recv.at[1 + f])


    def wait_velocity(c):
        all_of(RA.at[c, 0 : gx_count - 1], a_recv.at[c])

    def quarter_copy(c):
        return pltpu.make_async_remote_copy(
            src_ref=RA.at[c, 24:32],
            dst_ref=BL.at[c],
            send_sem=b_send.at[c],
            recv_sem=b_recv.at[c],
            device_id={"sec": 1},
            device_id_type=MESH,
        )

    def offer(c):
        wait_velocity(c)

        @pl.when(sec == 0)
        def _():
            quarter_copy(c).start()

    def blend(c):
        @pl.when(sec == 1)
        def _():
            quarter_copy(c).wait_recv()
            row = lax.broadcasted_iota(jnp.int32, (64, 128), 0) + 192
            weight = jnp.where((row >= fringe[0]) & (row < fringe[1]), FRINGE_BLEND, 0.0).astype(F32)
            mine = RA[c, 24:32].reshape(64, 128)
            theirs = BL[c].reshape(64, 128)
            RA[c, 24:32] = (mine + weight * (theirs - mine)).reshape(8, 8, 128)

    offer(0)
    offer(1)
    offer(2)
    wait_levels(0)
    x = spanwise_back(R4, 0, WY)
    lane32 = lanes(32)
    ahead = [turned(v, -1) for v in x]
    behind = [turned(v, 1) for v in x]
    for g in range(8):
        F[g, 0] = x[g]
        plus_y = jnp.where(lane32 == 127, ahead[(g + 1) % 8], ahead[g])
        minus_y = jnp.where(lane32 == 0, behind[(g + 7) % 8], behind[g])
        F[g, 1] = 0.5 * (plus_y - minus_y)

    def plane_copy(peer, source):
        return remote(F.at[peer, 0:2], R5.at[source, 0:2], y_send.at[2], y_recv.at[2], "gy", peer)

    def slope_copy(peer, source):
        return remote(F.at[peer, 2], R5.at[source, 2], y_send.at[3], y_recv.at[3], "gy", peer)

    to_all(lambda peer: plane_copy(peer, gy).start(), gy, gy_count)

    wait_levels(1)
    x = spanwise_back(R4, 1, WY)
    for g in range(8):
        F[g, 2] = x[g]

    to_all(lambda peer: slope_copy(peer, gy).start(), gy, gy_count)

    R5[gy] = F[gy]

    blend(0)
    blend(1)

    for c in range(3):
        all_of(RA.at[c, 0 : gx_count - 1], a_send.at[c])
    for k in range(3):
        all_of(XS.at[0 : gx_count - 1], x_send.at[k])
    for k in range(2):
        all_of(R1.at[0 : gy_count - 1], y_send.at[k])

    @pl.when(touches & (sec == 0))
    def _():
        @pl.loop(0, gy_count)
        def _(peer):
            fringe_copy(peer, gy).wait_send()


    all_of(R5.at[0 : gy_count - 1, 0:2], y_recv.at[2])

    def streamwise_back(f):
        return table_by_columns(WY[0, 4], WY[1, 4], jnp.concatenate([R5[g, f] for g in range(8)], axis=0))

    planes = [streamwise_back(0), streamwise_back(1)]
    pressure = planes[0]
    out_p[...] = pressure
    PP[8:264, :] = pressure
    PP[7:8, :] = pressure[255:256]
    PP[264:265, :] = pressure[0:1]
    out_v[0] = RA[0].reshape(256, 128) - 0.5 * (PP[9:265, :] - PP[7:263, :])
    out_v[1] = RA[1].reshape(256, 128) - planes[1]
    blend(2)

    all_of(R5.at[0 : gy_count - 1, 2], y_recv.at[3])

    out_v[2] = RA[2].reshape(256, 128) - streamwise_back(2)

    all_of(R5.at[0 : gy_count - 1, 0:2], y_send.at[2])
    all_of(R1.at[0 : gy_count - 1], y_send.at[3])

    @pl.when(sec == 0)
    def _():
        for c in range(3):
            quarter_copy(c).wait_send()


def hand_over(velocity_in, pressure_in, velocity_out, pressure_out, done):
    copies = [
        pltpu.make_async_copy(velocity_in, velocity_out, done.at[0]),
        pltpu.make_async_copy(pressure_in, pressure_out, done.at[1]),
    ]
    for copy in copies:
        copy.start()
    for copy in copies:
        copy.wait()


def on_device(velocity, turbine_cells, fringe_bounds):
    gx_count, gy_count = lax.axis_size("gx"), lax.axis_size("gy")
    vmem = pltpu.VMEM
    dma = pltpu.SemaphoreType.DMA
    scratch = [
        vmem((4, 3, 12, 48, 128), F32),
        vmem((10, 48, 128), F32),
        vmem((4, 4, 32, 128), F32),
        vmem((3, 3, 32, 128), F32),
        vmem((3, 48, 128), F32),
        vmem((32, 128), F32),
        vmem((256, 128), F32),
        vmem((32, 8, 128), F32),
        vmem((2, 5, 256, 256), jnp.bfloat16),
        vmem((256, 128), F32),
        vmem((256, 128), F32),
        vmem((8, 32, 128), F32),
        vmem((8, 32, 128), F32),
        vmem((32, 8, 128), F32),
        vmem((256, 128), F32),
        vmem((256, 128), F32),
        vmem((8, 32, 128), F32),
        vmem((2, 32, 8, 128), F32),
        vmem((2, 32, 8, 128), F32),
        vmem((8, 3, 32, 128), F32),
        vmem((8, 3, 32, 128), F32),
        vmem((3, 32, 8, 128), F32),
        vmem((3, 32, 8, 128), F32),
        vmem((3, 8, 8, 128), F32),
        vmem((272, 128), F32),
        dma((4, 6)),
        dma((4, 6)),
        dma((4,)),
        dma((3,)),
        dma((3,)),
        dma((3,)),
        dma((3,)),
        dma((4,)),
        dma((4,)),
        dma((gy_count,)),
        dma((gy_count,)),
        dma((3,)),
        dma((3,)),
        pltpu.SemaphoreType.REGULAR((5,)),
        vmem((768, 128), F32),
        vmem((3, 64), jnp.int32),
        pltpu.SMEM((2,), jnp.int32),
    ]
    anywhere, inside = pl.BlockSpec(memory_space=pltpu.HBM), pl.BlockSpec(memory_space=pltpu.VMEM)
    next_velocity, pressure = pl.pallas_call(
        step_kernel,
        out_shape=(jax.ShapeDtypeStruct((3, 256, 128), F32), jax.ShapeDtypeStruct((256, 128), F32)),
        in_specs=[anywhere, anywhere, anywhere, anywhere],
        out_specs=(inside, inside),
        scratch_shapes=scratch,
        compiler_params=pltpu.CompilerParams(collective_id=0, has_side_effects=True, vmem_limit_bytes=67043328),
    )(velocity.reshape(768, 128), turbine_cells.T, fringe_bounds, jnp.asarray(dht_tables()))
    next_velocity, pressure = pl.pallas_call(
        hand_over,
        out_shape=(jax.ShapeDtypeStruct((3, 256, 128), F32), jax.ShapeDtypeStruct((256, 128), F32)),
        in_specs=[inside, inside],
        out_specs=(pl.BlockSpec(memory_space=pltpu.HBM), pl.BlockSpec(memory_space=pltpu.HBM)),
        scratch_shapes=[dma((2,))],
    )(next_velocity, pressure)
    return (next_velocity.reshape(1, 3, 1, 256, 128), pressure.reshape(1, 1, 256, 128))


def solution(mesh):
    return jax.shard_map(
        on_device,
        mesh=mesh,
        in_specs=(PartitionSpec("sec", None, None, "gx", "gy"), PartitionSpec(), PartitionSpec()),
        out_specs=(PartitionSpec("sec", None, "gx", None, "gy"), PartitionSpec("sec", "gx", None, "gy")),
        check_vma=False,
    )
```

```python
import jax
import jax.numpy as jnp
import numpy as np
from jax import lax
from jax.experimental import pallas as pl
from jax.experimental.pallas import tpu as pltpu
from jax.sharding import PartitionSpec

TIME_STEP = 0.05
SMAG_COEFF = 0.1
THRUST_COEFF = 4.0
DRIVING_FORCE = 0.1
FRINGE_BLEND = 0.5
RADIUS = 4
MESH = pl.DeviceIdType.MESH
F32 = jnp.float32


def turned(v, shift):
    return pltpu.roll(v, shift % 128, 1)


def viscosity(xp, xm, yp, ym, zp, zm):
    a = xp[0] - xm[0]
    b = yp[1] - ym[1]
    c = zp[2] - zm[2]
    s1 = (yp[0] - ym[0]) + (xp[1] - xm[1])
    s2 = (zp[0] - zm[0]) + (xp[2] - xm[2])
    s3 = (zp[1] - zm[1]) + (yp[2] - ym[2])
    total = 0.5 * (a * a + b * b + c * c) + 0.25 * (s1 * s1 + s2 * s2 + s3 * s3)
    return SMAG_COEFF * jnp.sqrt(total)


def lanes(rows):
    return lax.broadcasted_iota(jnp.int32, (rows, 128), 1)


def fill_pads(U, N, T3):
    zeros = jnp.zeros((8, 128), F32)

    @pl.loop(0, U.shape[0] * 3)
    def _(i):
        s, c = i // 3, i % 3
        for slot in range(12):
            U[s, c, slot, 0:8, :] = zeros
            U[s, c, slot, 40:48, :] = zeros

    for i in range(10):
        N[i, 0:8, :] = zeros
        N[i, 40:48, :] = zeros
    for c in range(3):
        T3[c, 0:8, :] = zeros
        T3[c, 40:48, :] = zeros


def load_rows(vel, U, first, last):
    @pl.loop(first, last)
    def _(x):
        for c in range(3):
            for zc in range(4):
                U[0, c, x + 2, 8 + 8 * zc : 16 + 8 * zc, :] = vel[pl.ds(c * 256 + zc * 64 + x, 8, stride=8), :]


def find_disks(tur, DW, total_y):
    x_anchor = lax.axis_index("gx") * 8
    y_anchor = lax.axis_index("gy") * 128
    turb = tur.shape[1]
    twice = jnp.concatenate([tur[...], tur[...]], axis=1)
    rows_x = lax.broadcasted_iota(jnp.int32, (16, 2 * turb), 0)
    upper = lax.broadcasted_iota(jnp.int32, (16, 2 * turb), 1) // turb
    match = (twice[0:1, :] == x_anchor + rows_x % 8) & (upper == rows_x // 8)
    match = match.astype(F32).astype(jnp.bfloat16)
    rows_y = lax.broadcasted_iota(jnp.int32, (128, 2 * turb), 0)
    offset = rows_y + (y_anchor + total_y // 2 + total_y) - twice[1:2, :]
    offset = jnp.where(offset >= total_y, offset - total_y, offset)
    offset = jnp.where(offset >= total_y, offset - total_y, offset) - total_y // 2
    square_y = offset * offset
    level = upper[0:1, :] - twice[2:3, :]

    @pl.loop(0, 16)
    def _(i):
        off_z = 2 * i + level
        inside = (square_y <= RADIUS * RADIUS - off_z * off_z).astype(F32).astype(jnp.bfloat16)
        count = lax.dot_general(match, inside, (((1,), (1,)), ((), ())), preferred_element_type=F32)
        DW[pl.ds(2 * i, 8, stride=32), :] = count[0:8, :]
        DW[pl.ds(2 * i + 1, 8, stride=32), :] = count[8:16, :]


def remote(src, dst, send, recv, axis, index):
    return pltpu.make_async_remote_copy(
        src_ref=src, dst_ref=dst, send_sem=send, recv_sem=recv, device_id={axis: index}, device_id_type=MESH
    )


def pack_edges(U, s, comps):
    lane = lanes(32)
    packed = jnp.zeros((32, 128), F32)
    for c in comps:
        for x in range(8):
            base = c * 32 + x * 4
            packed = jnp.where(lane // 4 == base // 4, turned(U[s, c, x + 2, 8:40, :], base + 2), packed)
    return packed


def side_values(u, hh, lane):
    return (jnp.where(lane == 127, hh, turned(u, -1)), jnp.where(lane == 0, hh, turned(u, 1)))


def strip_viscosity(s, halo, Q, T3, NS):
    lane32 = lanes(32)
    parts = [[] for _ in range(6)]
    for c in range(3):
        t = T3[c, 8:40, :]
        xp, xm = turned(t, -4), turned(t, 4)
        if halo:
            q_minus, q_plus = Q[s, 0], Q[s, 2]
            xp = jnp.where(lane32 == 29, turned(q_plus, 28 - c * 32), xp)
            xp = jnp.where(lane32 == 62, turned(q_plus, 62 - c * 32), xp)
            xm = jnp.where(lane32 == 1, turned(q_minus, -28 - c * 32), xm)
            xm = jnp.where(lane32 == 34, turned(q_minus, 6 - c * 32), xm)
        values = (xp, xm, turned(t, -1), turned(t, 1), T3[c, 9:41, :], T3[c, 7:39, :])
        for part, value in zip(parts, values):
            part.append(value)
    strip = viscosity(*parts)
    NS[...] = jnp.where(lane32 % 4 == 0, turned(strip, -34), strip)


def row_viscosity(s, i, which, column, U, N, Q):
    lane = lanes(8)
    slot = i + 1
    for zc in range(4):
        r = 8 + 8 * zc
        hold = Q[s, which, 8 * zc : 8 * zc + 8, :]
        pieces = [[] for _ in range(6)]
        for c in range(3):
            u = U[s, c, slot, r : r + 8, :]
            hh = pltpu.roll(hold, 127 - c * 32 - column * 4, 1)
            yp, ym = side_values(u, hh, lane)
            values = (
                U[s, c, slot + 1, r : r + 8, :],
                U[s, c, slot - 1, r : r + 8, :],
                yp,
                ym,
                U[s, c, slot, r + 1 : r + 9, :],
                U[s, c, slot, r - 1 : r + 7, :],
            )
            for piece, value in zip(pieces, values):
                piece.append(value)
        N[i, r : r + 8, :] = viscosity(*pieces)


def advance_row(s, x, alpha, beta, U, N, Q, NS, DW):
    lane = lanes(8)
    farm = lax.axis_index("sec").astype(F32)
    slot = x + 2
    for zc in range(4):
        r = 8 + 8 * zc
        n = N[x + 1, r : r + 8, :]
        hold = Q[s, 1, 8 * zc : 8 * zc + 8, :]
        nyp, nym = side_values(n, pltpu.roll(NS[8 * zc : 8 * zc + 8, :], 127 - x * 4, 1), lane)
        around = (
            (n + N[x + 2, r : r + 8, :], n + N[x, r : r + 8, :]),
            (n + nyp, n + nym),
            (n + N[x + 1, r + 1 : r + 9, :], n + N[x + 1, r - 1 : r + 7, :]),
        )
        mids, sides = [], []
        for c in range(3):
            u = U[s, c, slot, r : r + 8, :]
            hh = pltpu.roll(hold, 127 - c * 32 - x * 4, 1)
            mids.append(u)
            sides.append(
                (
                    (U[s, c, slot + 1, r : r + 8, :], U[s, c, slot - 1, r : r + 8, :]),
                    side_values(u, hh, lane),
                    (U[s, c, slot, r + 1 : r + 9, :], U[s, c, slot, r - 1 : r + 7, :]),
                )
            )
        for c in range(3):
            u = mids[c]
            total = None
            for d in range(3):
                up_c, um_c = sides[c][d]
                up_d, um_d = sides[d][d]
                term = around[d][0] * (up_c - u) - around[d][1] * (u - um_c) - (up_d * up_c - um_d * um_c)
                total = term if total is None else total + term
            change = 0.5 * total
            if c == 0:
                weight = DW[pl.ds(x * 32 + 8 * zc, 8), :]
                change = change + (DRIVING_FORCE - (THRUST_COEFF * farm) * weight * u * jnp.abs(u))
            new = u + TIME_STEP * change
            if alpha:
                new = alpha * U[0, c, slot, r : r + 8, :] + beta * new
            U[s + 1, c, slot, r : r + 8, :] = new


def row_copies(s, near, U, send, recv):
    _, _, down, up = near
    if s == 3:
        parts = ((U.at[s, 0, 2, 8:40, :], U.at[s, 0, 10, 8:40, :]), (U.at[s, 0, 9, 8:40, :], U.at[s, 0, 1, 8:40, :]))
    else:
        parts = (
            (U.at[s, :, 2:4, 8:40, :], U.at[s, :, 10:12, 8:40, :]),
            (U.at[s, :, 8:10, 8:40, :], U.at[s, :, 0:2, 8:40, :]),
        )
    return tuple(
        remote(src, dst, send.at[s, i], recv.at[s, i], "gx", device)
        for i, ((src, dst), device) in enumerate(zip(parts, (down, up)))
    )


def rk_stage(s, alpha, beta, near, U, N, P, Q, T3, NS, DW, send, recv, early, meanwhile, after):
    left, right, down, up = near
    lane32 = lanes(32)
    to_down, to_up = row_copies(s, near, U, send, recv)
    to_left = remote(P.at[s, 0], P.at[s, 2], send.at[s, 2], recv.at[s, 2], "gy", left)
    to_right = remote(P.at[s, 0], P.at[s, 1], send.at[s, 3], recv.at[s, 3], "gy", right)
    q_down = remote(Q.at[s, 1], Q.at[s, 2], send.at[s, 4], recv.at[s, 4], "gx", down)
    q_up = remote(Q.at[s, 1], Q.at[s, 0], send.at[s, 5], recv.at[s, 5], "gx", up)
    P[s, 0] = pack_edges(U, s, range(3))
    to_left.start()
    to_right.start()
    early()
    to_left.wait_recv()
    to_right.wait_recv()
    own, from_left, from_right = P[s, 0], P[s, 1], P[s, 2]
    Q[s, 1] = jnp.where(lane32 % 4 == 0, turned(from_right, -2), from_left)
    q_down.start()
    q_up.start()
    meanwhile()

    strip_left = jnp.where(lane32 % 4 < 2, from_left, own)
    strip_right = jnp.where(lane32 % 4 < 2, own, from_right)
    for c in range(3):
        T3[c, 8:40, :] = jnp.where(lane32 < 32, turned(strip_left, -32 * c), turned(strip_right, 32 - 32 * c))
    strip_viscosity(s, False, Q, T3, NS)

    @pl.loop(2, 8)
    def _(i):
        row_viscosity(s, i, 1, i - 1, U, N, Q)

    @pl.loop(2, 6)
    def _(x):
        advance_row(s, x, alpha, beta, U, N, Q, NS, DW)

    to_down.wait_recv()
    to_up.wait_recv()
    q_down.wait_recv()
    q_up.wait_recv()
    after()
    strip_viscosity(s, True, Q, T3, NS)

    @pl.loop(0, 4)
    def _(j):
        i = j + 6 * (j // 2)
        which = jnp.where(j == 0, 0, jnp.where(j == 3, 2, 1))
        column = jnp.where(j % 3 == 0, 7 * (1 - j // 3), 7 * (j // 2))
        row_viscosity(s, i, which, column, U, N, Q)

    next_down, next_up = row_copies(s + 1, near, U, send, recv)

    @pl.loop(0, 2)
    def _(x):
        advance_row(s, x, alpha, beta, U, N, Q, NS, DW)

    next_down.start()

    @pl.loop(6, 8)
    def _(x):
        advance_row(s, x, alpha, beta, U, N, Q, NS, DW)

    next_up.start()

    for copy in (to_left, to_right, to_down, to_up, q_down, q_up):
        copy.wait_send()


def neighbours(gx_count, gy_count):
    gx, gy = lax.axis_index("gx"), lax.axis_index("gy")
    left = lax.rem(gy + gy_count - 1, gy_count)
    right = lax.rem(gy + 1, gy_count)
    down = lax.rem(gx + gx_count - 1, gx_count)
    up = lax.rem(gx + 1, gx_count)
    return left, right, down, up


STAGES = ((0.0, 1.0), (0.75, 0.25), (1.0 / 3.0, 2.0 / 3.0))


def dht_tables():
    def cas(product, length):
        angle = (product % length).astype(np.float64) * (2.0 * np.pi / length)
        return np.cos(angle) + np.sin(angle)

    b = np.arange(128)[:, None]
    f = np.arange(128)[None, :]
    spanwise = np.zeros((4, 256, 256))
    spanwise[0, :128, :128] = cas(b * (8 * f), 1024)
    spanwise[0, 128:, 128:] = cas(b * (4 + 8 * f), 1024)
    for p in (1, 2, 3):
        low, high = p + 8 * f, 8 - p + 8 * f
        spanwise[p, :128, :128] = cas(b * low, 1024)
        spanwise[p, 128:, :128] = cas(-b * low, 1024)
        spanwise[p, :128, 128:] = cas(b * high, 1024)
        spanwise[p, 128:, 128:] = -cas(-b * high, 1024)
    x = np.arange(256)
    streamwise = cas(x[:, None] * x[None, :], 256)

    def halves(table):
        table = table.astype(np.float32)
        top = table.astype(jnp.bfloat16)
        rest = (table - top.astype(np.float32)).astype(jnp.bfloat16)
        return np.stack([top, rest])

    return halves(np.concatenate([spanwise, streamwise[None]]))


HALF_ROOT = 0.5**0.5


def halved(v):
    top = v.astype(jnp.bfloat16)
    return top, (v - top.astype(F32)).astype(jnp.bfloat16)


def dot(a, b, dims=((1,), (0,))):
    return lax.dot_general(a, b, (dims, ((), ())), preferred_element_type=F32)


def rows_by_table(v, top, rest, dims):
    rows = v.shape[0]
    v_top, v_rest = halved(v)
    both = dot(jnp.concatenate([v_top, v_rest], axis=0), top, dims)
    return both[:rows] + both[rows:] + dot(v_top, rest, dims)


def table_by_columns(top, rest, v):
    v_top, v_rest = halved(v)
    return dot(top, v_top) + dot(top, v_rest) + dot(rest, v_top)


def swap_blocks(v):
    lane = lanes(8)
    low = lane < 64
    odd = (lane // 32) % 2 == 1
    a, b, c, d = v
    a, c = jnp.where(low, a, turned(c, 64)), jnp.where(low, turned(a, 64), c)
    b, d = jnp.where(low, b, turned(d, 64)), jnp.where(low, turned(b, 64), d)
    a, b = jnp.where(odd, turned(b, 32), a), jnp.where(odd, b, turned(a, -32))
    c, d = jnp.where(odd, turned(d, 32), c), jnp.where(odd, d, turned(c, -32))
    return a, b, c, d


def wrapped(index, count):
    return index - jnp.where(index >= count, count, 0)


def all_of(ref, semaphore):
    pltpu.make_async_copy(ref, ref, semaphore).wait()


def to_all(start, me, count):
    half = count // 2
    start(wrapped(me + half, count))

    @pl.loop(1, half)
    def _(step):
        start(wrapped(me + (half + step), count))
        start(wrapped(me + (half - step), count))


def find_pivots(INV):
    gx, gy = lax.axis_index("gx"), lax.axis_index("gy")
    lane = lanes(8)
    row = lax.broadcasted_iota(jnp.int32, (8, 128), 0)
    k = gy * 32 + (lane // 32) * 8 + row
    pair = gx // 8
    j = (gx % 8) * 32 + lane % 32
    second = jnp.where(pair == 0, 4, 8 - pair)
    ell = jnp.where(j < 128, pair + 8 * j, second + 8 * (j - 128))
    wave_x = jnp.sin(k.astype(F32) * (jnp.pi / 256))
    wave_y = jnp.sin(ell.astype(F32) * (jnp.pi / 1024))
    eigen = -4.0 * (wave_x * wave_x + wave_y * wave_y)
    inverse = 1.0 / (eigen - 1.0)
    INV[0] = inverse
    for z in range(1, 32):
        inverse = 1.0 / (eigen - (3.0 if z == 31 else 2.0) - inverse)
        INV[z] = inverse


def divergence(near, fringe, U, P, DM, GM, send, recv):
    left, right, down, up = near
    lane32, lane = lanes(32), lanes(8)
    s = 3
    to_down, to_up = row_copies(s, near, U, send, recv)
    to_left = remote(P.at[s, 0], P.at[s, 2], send.at[s, 2], recv.at[s, 2], "gy", left)
    to_right = remote(P.at[s, 0], P.at[s, 1], send.at[s, 3], recv.at[s, 3], "gy", right)
    P[s, 0] = pack_edges(U, s, [1])
    to_left.start()
    to_right.start()
    yield
    for copy in (to_left, to_right, to_down, to_up):
        copy.wait_recv()
    P[s, 0 + 3] = jnp.where(lane32 % 4 == 0, turned(P[s, 2], -2), P[s, 1])
    farm = lax.axis_index("sec").astype(F32)
    anchor = lax.axis_index("gx") * 8
    total_x = 8 * lax.axis_size("gx")

    def mask(x):
        column = jnp.full((8, 128), lax.rem(anchor + x + total_x, total_x), jnp.int32)
        return jnp.where((column >= fringe[0]) & (column < fringe[1]), FRINGE_BLEND, 0.0).astype(F32)

    @pl.loop(0, 8)
    def _(x):
        slot = x + 2
        m_here, m_plus, m_minus = mask(x), mask(x + 1), mask(x - 1)
        for zc in range(4):
            r = 8 + 8 * zc
            up_u, um_u = U[s, 0, slot + 1, r : r + 8, :], U[s, 0, slot - 1, r : r + 8, :]
            hh = pltpu.roll(P[s, 3, 8 * zc : 8 * zc + 8, :], 127 - 32 - x * 4, 1)
            yp, ym = side_values(U[s, 1, slot, r : r + 8, :], hh, lane)
            across = 0.5 * ((yp - ym) + (U[s, 2, slot, r + 1 : r + 9, :] - U[s, 2, slot, r - 1 : r + 7, :]))
            whole = 0.5 * (up_u - um_u) + across
            part = 0.5 * (m_plus * up_u - m_minus * um_u) + m_here * across
            DM[pl.ds(zc * 64 + x, 8, stride=8), :] = whole - farm * part
            GM[pl.ds(zc * 64 + x, 8, stride=8), :] = part

    for copy in (to_left, to_right, to_down, to_up):
        copy.wait_send()


def spanwise_forward(R1, WY, XS):
    x = [R1[g] for g in range(8)]
    e = [x[g] + x[g + 4] for g in range(4)]
    o = [x[g] - x[g + 4] for g in range(4)]
    plus, minus = HALF_ROOT * (o[1] + o[3]), HALF_ROOT * (o[1] - o[3])
    sides = (
        (e[0] + e[1] + e[2] + e[3], e[0] - e[1] + e[2] - e[3]),
        (o[0] + minus, plus + o[2]),
        (e[0] - e[2], e[1] - e[3]),
        (o[0] - minus, plus - o[2]),
    )
    for p in range(4):
        line = rows_by_table(jnp.concatenate(sides[p], axis=1), WY[0, p], WY[1, p], ((1,), (0,)))
        for h in range(2):
            tiles = swap_blocks([line[8 * z : 8 * z + 8, 128 * h : 128 * h + 128] for z in range(4)])
            for q in range(4):
                XS[p * 8 + h * 4 + q] = tiles[q]


def solve_levels(R3, INV, SQ):
    levels = []
    for g in range(8):
        levels.extend(swap_blocks([R3[g, 8 * i : 8 * i + 8, :] for i in range(4)]))
    scale = 1.0 / (256 * 1024)
    current = (scale * levels[0]) * INV[0]
    reduced = [current]
    for z in range(1, 32):
        current = (scale * levels[z] - current) * INV[z]
        reduced.append(current)
    solved = [None] * 32
    solved[31] = reduced[31]
    for z in range(30, -1, -1):
        solved[z] = reduced[z] - INV[z] * solved[z + 1]
    for z in range(32):
        above = solved[z + 1] if z < 31 else -solved[31]
        below = solved[z - 1] if z > 0 else solved[0]
        SQ[0, z] = solved[z]
        SQ[1, z] = 0.5 * (above - below)


def spanwise_back(R4, f, WY):
    rows = []
    for p in range(4):
        halves = []
        for h in range(2):
            tiles = swap_blocks([R4[f, p * 8 + h * 4 + q] for q in range(4)])
            halves.append(jnp.concatenate(tiles, axis=0))
        rows.append(rows_by_table(jnp.concatenate(halves, axis=1), WY[0, p], WY[1, p], ((1,), (1,))))
    a = [row[:, :128] for row in rows]
    b = [row[:, 128:] for row in rows]
    total, change = a[0] + b[0], a[0] - b[0]
    t = (total + a[2], change + b[2], total - a[2], change - b[2])
    minus, plus = HALF_ROOT * (a[1] - a[3]), HALF_ROOT * (b[1] + b[3])
    o = (a[1] + a[3], minus + plus, b[1] - b[3], plus - minus)
    return [t[g] + o[g] for g in range(4)] + [t[g] - o[g] for g in range(4)]


def step_kernel(vel_hbm, tur_hbm, fringe_hbm, wy_ref, velocity_hbm, pressure_hbm, U, N, P, Q, T3, NS, DW, INV, WY, DM, GM, R1, RG, XS, R2, YS, R3, SQ, R4, F, R5, UZ, RA, BL, PP, send, recv, local, a_send, a_recv, x_send, x_recv, y_send, y_recv, g_send, g_recv, b_send, b_recv, met, vel_ref, tur, fringe, out_v, out_p, written):
    gx_count, gy_count = lax.axis_size("gx"), lax.axis_size("gy")
    sec, gx, gy = lax.axis_index("sec"), lax.axis_index("gx"), lax.axis_index("gy")
    near = neighbours(gx_count, gy_count)
    barrier = pltpu.get_barrier_semaphore()
    loads = [
        pltpu.make_async_copy(wy_ref, WY, local.at[0]),
        pltpu.make_async_copy(tur_hbm, tur, local.at[1]),
        pltpu.make_async_copy(fringe_hbm, fringe, local.at[2]),
        pltpu.make_async_copy(vel_hbm, vel_ref, local.at[3]),
    ]
    loads[3].start()

    left, right, down, up = near

    def greet(semaphore, **device):
        pl.semaphore_signal(semaphore, inc=1, device_id=device, device_id_type=MESH)

    greet(barrier, gx=down)
    greet(barrier, gx=up)
    greet(barrier, sec=1 - sec)

    @pl.loop(1, gy_count)
    def _(d):
        greet(barrier, gy=wrapped(gy + d, gy_count))

    loads[3].wait()
    load_rows(vel_ref, U, 0, 2)
    load_rows(vel_ref, U, 6, 8)
    pl.semaphore_wait(barrier, gy_count + 2)
    for copy in row_copies(0, near, U, send, recv):
        copy.start()
    for load in loads[:3]:
        load.start()
    load_rows(vel_ref, U, 2, 6)
    early = lambda: fill_pads(U, N, T3)
    greet(met.at[0], gx=down)
    greet(met.at[0], gx=up)
    greet(met.at[4], sec=1 - sec)

    def prepare():
        loads[1].wait()
        loads[2].wait()
        find_disks(tur, DW, gy_count * 128)

    def spread(s):
        pl.semaphore_wait(met.at[s], 2)
        distance = 2 ** (s + 1)
        greet(met.at[s + 1], gx=lax.rem(gx + distance, gx_count))
        greet(met.at[s + 1], gx=lax.rem(gx + gx_count - distance, gx_count))

    for s, (alpha, beta) in enumerate(STAGES):
        meanwhile = (prepare, lambda: find_pivots(INV), lambda: None)[s]
        rk_stage(s, alpha, beta, near, U, N, P, Q, T3, NS, DW, send, recv, early, meanwhile, lambda: spread(s))
        early = lambda: None

    work = divergence(near, fringe, U, P, DM, GM, send, recv)
    next(work)
    flat_uz = UZ.reshape(768, 128)

    @pl.loop(0, 8)
    def _(x):
        for c in range(3):
            for zc in range(4):
                flat_uz[pl.ds(c * 256 + zc * 64 + x, 8, stride=8), :] = U[3, c, x + 2, 8 + 8 * zc : 16 + 8 * zc, :]

    groups = ((0, 1), (1, 2), (2, 3))

    def velocity_copy(c, peer, source):
        low, high = groups[c]
        return remote(UZ.at[low:high, peer], RA.at[low:high, source], a_send.at[c], a_recv.at[c], "gx", peer)

    def send_velocity(c):
        to_all(lambda peer: velocity_copy(c, peer, gx).start(), gx, gx_count)

        for i in range(*groups[c]):
            RA[i, gx] = UZ[i, gx]

    pl.semaphore_wait(met.at[3], 2)
    pl.semaphore_wait(met.at[4], 1)
    send_velocity(0)
    for _ in work:
        pass

    def group_copy(peer, source):
        return remote(DM.at[pl.ds(peer * 32, 32), :], R1.at[source], y_send.at[0], y_recv.at[0], "gy", peer)

    def fringe_copy(peer, source):
        return pltpu.make_async_remote_copy(
            src_ref=GM.at[pl.ds(peer * 32, 32), :],
            dst_ref=RG.at[source],
            send_sem=g_send.at[peer],
            recv_sem=g_recv.at[source],
            device_id={"sec": 1, "gy": peer},
            device_id_type=MESH,
        )

    touches = (gx == 0) | (gx >= 3 * gx_count // 4 - 1)

    @pl.when(touches & (sec == 0))
    def _():
        @pl.loop(0, gy_count)
        def _(peer):
            fringe_copy(peer, gy).start()

    to_all(lambda peer: group_copy(peer, gy).start(), gy, gy_count)

    R1[gy] = DM[pl.ds(pl.multiple_of(gy * 32, 32), 32), :]

    all_of(R1.at[0 : gy_count - 1], y_recv.at[0])

    @pl.when(touches & (sec == 1))
    def _():
        @pl.loop(0, gy_count)
        def _(source):
            fringe_copy(gy, source).wait_recv()

        for g in range(8):
            R1[g] = R1[g] + RG[g]

    loads[0].wait()
    spanwise_forward(R1, WY, XS)

    def chunk_copy(peer, source):
        return remote(XS.at[peer], R2.at[pl.ds(source * 8, 8), :], x_send.at[0], x_recv.at[0], "gx", peer)

    to_all(lambda peer: chunk_copy(peer, gx).start(), gx, gx_count)

    R2[pl.ds(pl.multiple_of(gx * 8, 8), 8), :] = XS[gx]
    send_velocity(1)

    all_of(XS.at[0 : gx_count - 1], x_recv.at[0])

    YS[...] = table_by_columns(WY[0, 4], WY[1, 4], R2[...])

    def wave_copy(peer, source):
        return remote(YS.at[pl.ds(peer * 32, 32), :], R3.at[source], y_send.at[1], y_recv.at[1], "gy", peer)

    to_all(lambda peer: wave_copy(peer, gy).start(), gy, gy_count)

    R3[gy] = YS[pl.ds(pl.multiple_of(gy * 32, 32), 32), :]
    send_velocity(2)

    all_of(R3.at[0 : gy_count - 1], y_recv.at[1])

    solve_levels(R3, INV, SQ)

    def level_copy(f, peer, source):
        return remote(SQ.at[f, peer], R4.at[f, source], x_send.at[1 + f], x_recv.at[1 + f], "gx", peer)

    for f in range(2):
        to_all(lambda peer: level_copy(f, peer, gx).start(), gx, gx_count)
        R4[f, gx] = SQ[f, gx]

    def wait_levels(f):
        all_of(R4.at[f, 0 : gx_count - 1], x_recv.at[1 + f])


    def wait_velocity(c):
        all_of(RA.at[c, 0 : gx_count - 1], a_recv.at[c])

    def quarter_copy(c):
        return pltpu.make_async_remote_copy(
            src_ref=RA.at[c, 24:32],
            dst_ref=BL.at[c],
            send_sem=b_send.at[c],
            recv_sem=b_recv.at[c],
            device_id={"sec": 1},
            device_id_type=MESH,
        )

    def offer(c):
        wait_velocity(c)

        @pl.when(sec == 0)
        def _():
            quarter_copy(c).start()

    def blend(c):
        @pl.when(sec == 1)
        def _():
            quarter_copy(c).wait_recv()
            row = lax.broadcasted_iota(jnp.int32, (64, 128), 0) + 192
            weight = jnp.where((row >= fringe[0]) & (row < fringe[1]), FRINGE_BLEND, 0.0).astype(F32)
            mine = RA[c, 24:32].reshape(64, 128)
            theirs = BL[c].reshape(64, 128)
            RA[c, 24:32] = (mine + weight * (theirs - mine)).reshape(8, 8, 128)

    offer(0)
    offer(1)
    offer(2)
    wait_levels(0)
    x = spanwise_back(R4, 0, WY)
    lane32 = lanes(32)
    ahead = [turned(v, -1) for v in x]
    behind = [turned(v, 1) for v in x]
    for g in range(8):
        F[g, 0] = x[g]
        plus_y = jnp.where(lane32 == 127, ahead[(g + 1) % 8], ahead[g])
        minus_y = jnp.where(lane32 == 0, behind[(g + 7) % 8], behind[g])
        F[g, 1] = 0.5 * (plus_y - minus_y)

    def plane_copy(peer, source):
        return remote(F.at[peer, 0:2], R5.at[source, 0:2], y_send.at[2], y_recv.at[2], "gy", peer)

    def slope_copy(peer, source):
        return remote(F.at[peer, 2], R5.at[source, 2], y_send.at[3], y_recv.at[3], "gy", peer)

    to_all(lambda peer: plane_copy(peer, gy).start(), gy, gy_count)

    wait_levels(1)
    x = spanwise_back(R4, 1, WY)
    for g in range(8):
        F[g, 2] = x[g]

    to_all(lambda peer: slope_copy(peer, gy).start(), gy, gy_count)

    R5[gy] = F[gy]

    blend(0)
    blend(1)

    for c in range(3):
        all_of(RA.at[c, 0 : gx_count - 1], a_send.at[c])
    for k in range(3):
        all_of(XS.at[0 : gx_count - 1], x_send.at[k])
    for k in range(2):
        all_of(R1.at[0 : gy_count - 1], y_send.at[k])

    @pl.when(touches & (sec == 0))
    def _():
        @pl.loop(0, gy_count)
        def _(peer):
            fringe_copy(peer, gy).wait_send()


    all_of(R5.at[0 : gy_count - 1, 0:2], y_recv.at[2])

    def streamwise_back(f):
        return table_by_columns(WY[0, 4], WY[1, 4], jnp.concatenate([R5[g, f] for g in range(8)], axis=0))

    planes = [streamwise_back(0), streamwise_back(1)]
    pressure = planes[0]
    out_p[...] = pressure
    results = [pltpu.make_async_copy(out_v.at[c], velocity_hbm.at[c], written.at[c]) for c in range(3)]
    results.append(pltpu.make_async_copy(out_p, pressure_hbm, written.at[3]))
    results[3].start()
    PP[8:264, :] = pressure
    PP[7:8, :] = pressure[255:256]
    PP[264:265, :] = pressure[0:1]
    out_v[0] = RA[0].reshape(256, 128) - 0.5 * (PP[9:265, :] - PP[7:263, :])
    results[0].start()
    out_v[1] = RA[1].reshape(256, 128) - planes[1]
    results[1].start()
    blend(2)

    all_of(R5.at[0 : gy_count - 1, 2], y_recv.at[3])

    out_v[2] = RA[2].reshape(256, 128) - streamwise_back(2)
    results[2].start()

    all_of(R5.at[0 : gy_count - 1, 0:2], y_send.at[2])
    all_of(R1.at[0 : gy_count - 1], y_send.at[3])

    @pl.when(sec == 0)
    def _():
        for c in range(3):
            quarter_copy(c).wait_send()

    for result in results:
        result.wait()


def hand_over(velocity_in, pressure_in, velocity_out, pressure_out, held, arrived, left):
    parts = [(velocity_in.at[c], velocity_out.at[c]) for c in range(3)] + [(pressure_in, pressure_out)]
    loads = [pltpu.make_async_copy(src, held.at[i], arrived.at[i]) for i, (src, _) in enumerate(parts)]
    stores = [pltpu.make_async_copy(held.at[i], dst, left.at[i]) for i, (_, dst) in enumerate(parts)]
    for load in loads:
        load.start()
    for load, store in zip(loads, stores):
        load.wait()
        store.start()
    for store in stores:
        store.wait()


def on_device(velocity, turbine_cells, fringe_bounds):
    gx_count, gy_count = lax.axis_size("gx"), lax.axis_size("gy")
    vmem = pltpu.VMEM
    dma = pltpu.SemaphoreType.DMA
    scratch = [
        vmem((4, 3, 12, 48, 128), F32),
        vmem((10, 48, 128), F32),
        vmem((4, 4, 32, 128), F32),
        vmem((3, 3, 32, 128), F32),
        vmem((3, 48, 128), F32),
        vmem((32, 128), F32),
        vmem((256, 128), F32),
        vmem((32, 8, 128), F32),
        vmem((2, 5, 256, 256), jnp.bfloat16),
        vmem((256, 128), F32),
        vmem((256, 128), F32),
        vmem((8, 32, 128), F32),
        vmem((8, 32, 128), F32),
        vmem((32, 8, 128), F32),
        vmem((256, 128), F32),
        vmem((256, 128), F32),
        vmem((8, 32, 128), F32),
        vmem((2, 32, 8, 128), F32),
        vmem((2, 32, 8, 128), F32),
        vmem((8, 3, 32, 128), F32),
        vmem((8, 3, 32, 128), F32),
        vmem((3, 32, 8, 128), F32),
        vmem((3, 32, 8, 128), F32),
        vmem((3, 8, 8, 128), F32),
        vmem((272, 128), F32),
        dma((4, 6)),
        dma((4, 6)),
        dma((4,)),
        dma((3,)),
        dma((3,)),
        dma((3,)),
        dma((3,)),
        dma((4,)),
        dma((4,)),
        dma((gy_count,)),
        dma((gy_count,)),
        dma((3,)),
        dma((3,)),
        pltpu.SemaphoreType.REGULAR((5,)),
        vmem((768, 128), F32),
        vmem((3, 64), jnp.int32),
        pltpu.SMEM((2,), jnp.int32),
        vmem((3, 256, 128), F32),
        vmem((256, 128), F32),
        dma((4,)),
    ]
    anywhere = pl.BlockSpec(memory_space=pltpu.HBM)
    next_velocity, pressure = pl.pallas_call(
        step_kernel,
        out_shape=(jax.ShapeDtypeStruct((3, 256, 128), F32), jax.ShapeDtypeStruct((256, 128), F32)),
        in_specs=[anywhere, anywhere, anywhere, anywhere],
        out_specs=(anywhere, anywhere),
        scratch_shapes=scratch,
        compiler_params=pltpu.CompilerParams(collective_id=0, has_side_effects=True, vmem_limit_bytes=67043328),
    )(velocity.reshape(768, 128), turbine_cells.T, fringe_bounds, jnp.asarray(dht_tables()))
    next_velocity, pressure = pl.pallas_call(
        hand_over,
        out_shape=(jax.ShapeDtypeStruct((3, 256, 128), F32), jax.ShapeDtypeStruct((256, 128), F32)),
        in_specs=[anywhere, anywhere],
        out_specs=(pl.BlockSpec(memory_space=pltpu.HBM), pl.BlockSpec(memory_space=pltpu.HBM)),
        scratch_shapes=[vmem((4, 256, 128), F32), dma((4,)), dma((4,))],
    )(next_velocity, pressure)
    return (next_velocity.reshape(1, 3, 1, 256, 128), pressure.reshape(1, 1, 256, 128))


def solution(mesh):
    return jax.shard_map(
        on_device,
        mesh=mesh,
        in_specs=(PartitionSpec("sec", None, None, "gx", "gy"), PartitionSpec(), PartitionSpec()),
        out_specs=(PartitionSpec("sec", None, "gx", None, "gy"), PartitionSpec("sec", "gx", None, "gy")),
        check_vma=False,
    )
```
